32 devices in a mesh: dp: 8 (over z, x), tensor: 4 (over y, core).
Axes of the slice: x: 2, y: 2, z: 4, core: 2. Of those that a mesh axis runs over, the one named last changes fastest.
Arguments:
- features: bfloat16 [32768, 768], P(('dp', 'tensor')), may hold values from -6 to 6
- first_gain: bfloat16 [768], replicated, may hold values from 0.5 to 1.5
- first_shift: bfloat16 [768], replicated, may hold values from -2 to 2
- qkv_weight: bfloat16 [768, 3, 768], P('dp', None, 'tensor'), may hold values from -0.21875 to 0.21875
- qv_bias: bfloat16 [2, 768], P(None, 'tensor'), may hold values from -1.1953125 to 1.1953125
- rel_height: bfloat16 [27, 64], replicated, may hold values from -0.59765625 to 0.59765625
- rel_width: bfloat16 [27, 64], replicated, may hold values from -0.59765625 to 0.59765625
- output_weight: bfloat16 [768, 768], P('dp', 'tensor'), may hold values from -1.25 to 1.25
- output_bias: bfloat16 [768], replicated, may hold values from -2 to 2
- second_gain: bfloat16 [768], replicated, may hold values from 0.5 to 1.5
- second_shift: bfloat16 [768], replicated, may hold values from -2 to 2
- up_weight: bfloat16 [768, 3072], P('dp', 'tensor'), may hold values from -0.21875 to 0.21875
- up_bias: bfloat16 [3072], P('tensor'), may hold values from -2 to 2
- down_weight: bfloat16 [768, 3072], P('dp', 'tensor'), may hold values from -0.109375 to 0.109375
- down_bias: bfloat16 [768], replicated, may hold values from -2 to 2
- cotangent: bfloat16 [32768, 768], P(('dp', 'tensor')), may hold values from -6 to 6
Outputs:
- output: bfloat16 [32768, 768], P(('dp', 'tensor'))
- grad_features: bfloat16 [32768, 768], P(('dp', 'tensor'))
- grad_first_gain: float32 [768], replicated
- grad_first_shift: float32 [768], replicated
- grad_qkv_weight: float32 [768, 3, 768], P('dp', None, 'tensor')
- grad_qv_bias: float32 [2, 768], P(None, 'tensor')
- grad_rel_height: float32 [27, 64], replicated
- grad_rel_width: float32 [27, 64], replicated
- grad_output_weight: float32 [768, 768], P('dp', 'tensor')
- grad_output_bias: float32 [768], replicated
- grad_second_gain: float32 [768], replicated
- grad_second_shift: float32 [768], replicated
- grad_up_weight: float32 [768, 3072], P('dp', 'tensor')
- grad_up_bias: float32 [3072], P('tensor')
- grad_down_weight: float32 [768, 3072], P('dp', 'tensor')
- grad_down_bias: float32 [768], replicated
The draws below stay inside these ranges and needn't reach their ends.
All inputs are finite; a program needn't handle non-finite values.
Results may differ from the reference program's by a relative error of at most 0.015.
Values may be sent and summed in bfloat16 or wider, within the bound.
No kernel may reach another device: no remote copies, remote signals or barrier semaphores. Data moves between devices by JAX's collectives and lax.ppermute only.
A program may use at most 192 MiB of HBM per device.

```python
import jax
import jax.numpy as jnp
from jax import lax

D = 768
HEADS = 12
HD = 64
FF = 3072
GRID = 64
WIN = 14
SIDE = 5
IMAGES = 8
TOKENS = 32768


def with_spikes(drawn, key, source, target, blocks, factor):
    owner, partner = [(jnp.arange(drawn.shape[dim]) // (drawn.shape[dim] // blocks)).reshape([-1 if axis == dim else 1 for axis in range(drawn.ndim)]) for dim in (source, target)]
    chosen = jax.random.permutation(key, blocks)[partner]
    strong = (owner == chosen) | (owner == (partner + blocks // 2) % blocks)
    return jnp.where(strong, factor * drawn, drawn)


def levels(stream_key, dims, split, least, high):
    def one(dim, parts):
        draws = jax.random.uniform(jax.random.fold_in(jax.random.fold_in(stream_key, 6), dim), (parts,), jnp.float32, least / len(split), high / len(split))
        return jnp.repeat(jnp.exp(draws), dims[dim] // parts).reshape((-1,) + (1,) * (len(dims) - dim - 1))

    factor_of = one(*split[0])
    for cut in split[1:]:
        factor_of = factor_of * one(*cut)
    return factor_of


def normal_values(rng, shape, scale, limit, pieces=(), held_as=jnp.bfloat16):
    entries = jax.random.normal(rng, shape, jnp.float32) * scale
    if len(pieces) > 0:
        entries = levels(rng, shape, pieces, -0.22, 0.18) * entries
    return jnp.clip(entries, min=-limit, max=limit).astype(held_as)


def gaussian_with(rng, shape, spread, bound, split, heavy, kind=jnp.bfloat16):
    entries = spread * jax.random.normal(rng, shape, jnp.float32)
    if split:
        entries = entries * levels(rng, shape, split, -0.22, 0.18)
    return jnp.clip(with_spikes(entries, jax.random.fold_in(rng, 3), *heavy), -bound, bound).astype(kind)


def setup_inputs(seed: int = 0) -> dict:
    splits = jax.random.split(jax.random.key(seed), 17)
    return {
        "features": normal_values(splits[0], (TOKENS, D), 1.0, 6.0, ((0, 32),)),
        "first_gain": jnp.clip(1.0 + 0.1 * jax.random.normal(splits[1], (D,), jnp.float32), 0.5, 1.5).astype(jnp.bfloat16),
        "first_shift": normal_values(splits[2], (D,), 0.3, 2.0),
        "qkv_weight": normal_values(splits[3], (D, 3, D), D ** -0.5, 0.21875, ((0, 8), (2, 4))),
        "qv_bias": normal_values(splits[4], (2, D), 0.2, 1.1953125, ((1, 4),)),
        "rel_height": normal_values(splits[5], (2 * WIN - 1, HD), 0.1, 0.59765625),
        "rel_width": normal_values(splits[6], (2 * WIN - 1, HD), 0.1, 0.59765625),
        "output_weight": normal_values(splits[7], (D, D), (D // 32) ** -0.5, 1.25, ((0, 8), (1, 4))),
        "output_bias": normal_values(splits[8], (D,), 0.3, 2.0),
        "second_gain": jnp.clip(1.0 + 0.1 * jax.random.normal(splits[9], (D,), jnp.float32), 0.5, 1.5).astype(jnp.bfloat16),
        "second_shift": normal_values(splits[10], (D,), 0.3, 2.0),
        "up_weight": normal_values(splits[11], (D, FF), D ** -0.5, 0.21875, ((0, 8), (1, 4))),
        "up_bias": normal_values(splits[12], (FF,), 0.3, 2.0, ((0, 4),)),
        "down_weight": normal_values(splits[13], (D, FF), FF ** -0.5, 0.109375, ((0, 8), (1, 4))),
        "down_bias": normal_values(splits[14], (D,), 0.3, 2.0),
        "cotangent": gaussian_with(splits[15], (TOKENS, D), 1.0, 6.0, ((0, 32),), (0, 1, 32, 2.75)),
    }


@jax.custom_vjp
def low(v):
    return lax.optimization_barrier(v.astype(jnp.bfloat16)).astype(jnp.float32)

@jax.custom_vjp
def low_back(v):
    return v

def low_keep(v):
    return (low(v), None)

def low_pass(kept, grad):
    return (grad,)

def back_keep(v):
    return (v, None)

def back_low(kept, grad):
    return (low(grad),)
low.defvjp(low_keep, low_pass)
low_back.defvjp(back_keep, back_low)

def matmul(left, right):
    return jnp.dot(left, right, precision=lax.Precision.HIGHEST, preferred_element_type=jnp.float32)

def layer_norm(value, gain_factor, shift):
    mean_value = lax.optimization_barrier(jnp.mean(value, -1, keepdims=True))
    centered = value - mean_value
    variance = lax.optimization_barrier(jnp.mean(centered * centered, -1, keepdims=True))
    return centered * lax.rsqrt(variance + 1e-06) * gain_factor + shift

def to_windows(grid):
    width = grid.shape[-1]
    extra = SIDE * WIN - GRID
    padded = jnp.pad(grid, ((0, extra), (0, extra), (0, 0)))
    padded = padded.reshape(SIDE, WIN, SIDE, WIN, width).transpose(0, 2, 1, 3, 4)
    return padded.reshape(SIDE * SIDE, WIN * WIN, width)

def from_windows(windows):
    width = windows.shape[-1]
    grid = windows.reshape(SIDE, SIDE, WIN, WIN, width).transpose(0, 2, 1, 3, 4)
    grid = grid.reshape(SIDE * WIN, SIDE * WIN, width)
    return grid[:GRID, :GRID].reshape(GRID * GRID, width)

def image_layer(image, params):
    first_gain, first_shift, qkv_weight, qv_bias, rel_height, rel_width, output_weight, output_bias, second_gain, second_shift, up_weight, up_bias, down_weight, down_bias = params
    count = SIDE * SIDE
    normed = low(layer_norm(image, first_gain, first_shift))
    windows = to_windows(normed.reshape(GRID, GRID, D))
    bias_all = jnp.stack([qv_bias[0], jnp.zeros((D,), jnp.float32), qv_bias[1]]).reshape(3 * D)
    qkv = matmul(windows.reshape(count * WIN * WIN, D), qkv_weight.reshape(D, 3 * D)) + bias_all
    qkv = low(low_back(qkv)).reshape(count, WIN * WIN, 3, HEADS, HD)
    query, keys, values = (qkv[:, :, 0], qkv[:, :, 1], qkv[:, :, 2])
    offsets = jnp.arange(WIN)[:, None] - jnp.arange(WIN)[None, :] + WIN - 1
    table_rows = rel_height[offsets]
    table_cols = rel_width[offsets]
    high = lax.Precision.HIGHEST
    scores = jnp.einsum('nqhc,nkhc->nhqk', query, keys, precision=high) * HD ** (-0.5)
    query_grid = query.reshape(count, WIN, WIN, HEADS, HD)
    along_rows = jnp.einsum('nabhc,akc->nhabk', query_grid, table_rows, precision=high)
    along_cols = jnp.einsum('nabhc,bkc->nhabk', query_grid, table_cols, precision=high)
    scores = scores.reshape(count, HEADS, WIN, WIN, WIN, WIN)
    scores = scores + along_rows[..., :, None] + along_cols[..., None, :]
    scores = low_back(scores.reshape(count, HEADS, WIN * WIN, WIN * WIN))
    probs = jax.nn.softmax(scores, axis=-1)
    attended = jnp.einsum('nhqk,nkhc->nqhc', low(probs), values, precision=high)
    attended = low(low_back(attended)).reshape(count, WIN * WIN, D)
    on_grid = from_windows(attended)
    branch = low_back(matmul(on_grid, output_weight.T) + output_bias)
    hidden_one = image + branch
    normed_two = low(layer_norm(hidden_one, second_gain, second_shift))
    upper = low_back(matmul(normed_two, up_weight) + up_bias)
    active = low(jax.nn.gelu(upper, approximate=False))
    feed = low_back(matmul(active, down_weight.T) + down_bias)
    return hidden_one + feed

def reference(features, first_gain, first_shift, qkv_weight, qv_bias, rel_height, rel_width, output_weight, output_bias, second_gain, second_shift, up_weight, up_bias, down_weight, down_bias, cotangent):
    params = tuple((p.astype(jnp.float32) for p in (first_gain, first_shift, qkv_weight, qv_bias, rel_height, rel_width, output_weight, output_bias, second_gain, second_shift, up_weight, up_bias, down_weight, down_bias)))
    images = features.astype(jnp.float32).reshape(IMAGES, GRID * GRID, D)

    def forward(image_stack, weights):
        return lax.map(lambda image: jax.checkpoint(image_layer)(image, weights), image_stack)
    result, pullback = jax.vjp(forward, images, params)
    grad_images, grads = pullback(cotangent.astype(jnp.float32).reshape(IMAGES, GRID * GRID, D))
    return (result.reshape(TOKENS, D).astype(jnp.bfloat16), grad_images.reshape(TOKENS, D).astype(jnp.bfloat16), grads[0], grads[1], grads[2], grads[3], grads[4], grads[5], grads[6], grads[7], grads[8], grads[9], grads[10], grads[11], grads[12], grads[13])
```

```python
from functools import partial
import math

import jax
import jax.numpy as jnp
from jax import lax
from jax.experimental import pallas as pl
from jax.experimental.pallas import tpu as pltpu
from jax.sharding import PartitionSpec as P
import numpy as np

D = 768
HD = 64
GRID = 64
WIN = 14
SIDE = 5
PITCH = 16
KEYS = WIN * PITCH
EXT = 2 * WIN
PAIRS = D // (2 * HD)
OFFS = 2 * WIN - 1
EPSILON = 1e-06
FAR = -1e30
BF = jnp.bfloat16
F32 = jnp.float32
HIGH = lax.Precision.HIGHEST


def mm(left, right):
    return jnp.dot(left, right, preferred_element_type=F32)


def mm_t(left, right):
    return lax.dot_general(left, right, (((1,), (1,)), ((), ())), preferred_element_type=F32)


def t_mm(left, right):
    return lax.dot_general(left, right, (((0,), (0,)), ((), ())), preferred_element_type=F32)


def norm_parts(value):
    centered = value - jnp.mean(value, -1, keepdims=True)
    inverse = lax.rsqrt(jnp.mean(centered * centered, -1, keepdims=True) + EPSILON)
    return centered * inverse, inverse


def norm_back(upstream, hat, inverse, gain):
    scaled = upstream * gain
    return inverse * (
        scaled
        - jnp.mean(scaled, -1, keepdims=True)
        - hat * jnp.mean(scaled * hat, -1, keepdims=True)
    )


def score_tables():
    ahead = np.zeros((2, KEYS, 128), np.float32)
    back = np.zeros((2, KEYS, 128), np.float32)
    for head in range(2):
        base = 64 - 64 * head
        for c in range(WIN):
            for e in range(PITCH):
                k = c * PITCH + e
                if e >= WIN:
                    ahead[head, k, base] = FAR
                    continue
                ahead[head, k, base + 15 + c] = 1
                ahead[head, k, base + 1 + c] = 1
                ahead[head, k, base + 46 + e] = 1
                ahead[head, k, base + 32 + e] = 1
                back[head, k, base + WIN - 1 - c] = 1
                back[head, k, base + 32 + WIN - 1 - e] = 1
    return ahead, back


def offset_tables(rel_height, rel_width):
    def place(first, second, at_rows, at_cols):
        slab = jnp.zeros((64, HD), BF)
        slab = slab.at[at_rows : at_rows + OFFS].set(first)
        slab = slab.at[at_cols : at_cols + OFFS].set(second)
        low = jnp.concatenate([slab, jnp.zeros_like(slab)], 1)
        high = jnp.concatenate([jnp.zeros_like(slab), slab], 1)
        return jnp.concatenate([jnp.zeros_like(low), low, high, jnp.zeros_like(high)], 0)

    return (
        place(rel_height[::-1], rel_width[::-1], 2, 33),
        place(rel_height, rel_width, 0, 32),
    )


def project_body(place_ref, x_ref, vec_ref, w_ref, nw_ref, q_ref, k_ref, v_ref, nat_ref, *, rows):
    band = pl.program_id(0)
    slot = place_ref[0]

    @pl.when(band == 0)
    def _():
        def one(i, carry):
            hat, _ = norm_parts(x_ref[i].astype(F32))
            normed = hat * vec_ref[0:1] + vec_ref[1:2]
            inside = WIN * slot + i < GRID
            nat_ref[i, 0:GRID, :] = jnp.where(inside, normed, 0.0)
            nat_ref[i, GRID : GRID + PITCH, :] = jnp.zeros((PITCH, D), F32)
            return carry

        lax.fori_loop(0, EXT, one, 0)

    for b in range(SIDE):
        @pl.when(band == b)
        def _(b=b):
            def one(i, carry):
                piece = nat_ref[i, WIN * b : WIN * b + PITCH, :]
                keep = lax.broadcasted_iota(jnp.int32, (PITCH, D), 0) < WIN
                start = pl.multiple_of(i * PITCH, PITCH)
                nw_ref[pl.ds(start, PITCH), :] = jnp.where(keep, piece, 0.0).astype(BF)
                return carry

            lax.fori_loop(0, EXT, one, 0)

    normed = nw_ref[...]
    k_ref[...] = mm(normed, w_ref[:, D : 2 * D]).astype(BF)
    v_ref[...] = (mm(normed, w_ref[:, 2 * D : 3 * D]) + vec_ref[3:4]).astype(BF)
    own = nw_ref[pl.ds(pl.multiple_of(slot * 2 * PITCH, 2 * PITCH), rows * PITCH), :]
    q_ref[...] = (mm(own, w_ref[:, 0:D]) + vec_ref[2:3]).astype(BF)


def project(slot, x_ext, vectors, weight, rows):
    keys, queries = SIDE * EXT * PITCH, SIDE * rows * PITCH
    whole = lambda shape: pl.BlockSpec(shape, lambda b, s: (0,) * len(shape), pipeline_mode=pl.Buffered(1))
    return pl.pallas_call(
        partial(project_body, rows=rows),
        grid_spec=pltpu.PrefetchScalarGridSpec(
            num_scalar_prefetch=1,
            grid=(SIDE,),
            in_specs=[whole((EXT, GRID, D)), whole((8, D)), whole((D, 3 * D))],
            out_specs=[
                pl.BlockSpec((EXT * PITCH, D), lambda b, s: (b, 0)),
                pl.BlockSpec((rows * PITCH, D), lambda b, s: (b, 0)),
                pl.BlockSpec((EXT * PITCH, D), lambda b, s: (b, 0)),
                pl.BlockSpec((EXT * PITCH, D), lambda b, s: (b, 0)),
            ],
            scratch_shapes=[pltpu.VMEM((EXT, GRID + PITCH, D), F32)],
        ),
        out_shape=[
            jax.ShapeDtypeStruct((keys, D), BF),
            jax.ShapeDtypeStruct((queries, D), BF),
            jax.ShapeDtypeStruct((keys, D), BF),
            jax.ShapeDtypeStruct((keys, D), BF),
        ],
        compiler_params=pltpu.CompilerParams(vmem_limit_bytes=60 << 20),
        name="project",
    )(slot, x_ext, vectors, weight)


def head_lanes(shape, head):
    lane = lax.broadcasted_iota(jnp.int32, shape, 1)
    return lane < HD if head == 0 else lane >= HD


def window_split(slot, rows):
    first = WIN - 2 * slot
    return ((0, first * PITCH, 0), (first * PITCH, rows * PITCH, KEYS))


def attend_body(place_ref, q_ref, k_ref, v_ref, rel_ref, tab_ref, o_ref, p_ref, *, rows, slots):
    def variant(slot):
        queries = q_ref[...]
        count = rows * PITCH
        lane = lax.broadcasted_iota(jnp.int32, (PITCH, 128), 1)
        raw = mm(queries, rel_ref[...])
        outs = [None, None]
        for head in range(2):
            base = 64 - 64 * head
            parts = []
            for r in range(rows):
                here = raw[r * PITCH : (r + 1) * PITCH, 128 * head : 128 * head + 128]
                along_row = pltpu.roll(here, (2 * slot + r) % WIN, 1)
                along_col = pltpu.roll(here, 0, 1, stride=1, stride_axis=0)
                both = jnp.where(lane < base + 32, along_row, along_col)
                wanted = ((lane >= base + 15) & (lane < base + 29)) | ((lane >= base + 46) & (lane < base + 60))
                parts.append(jnp.where(wanted, both, 0.0))
            along = jnp.concatenate(parts, 0)
            high = along.astype(BF).astype(F32)
            extra = high + pltpu.roll(along - high, 114, 1)
            wide = lax.broadcasted_iota(jnp.int32, (count, 128), 1)
            extra = jnp.where(wide == base, 1.0, extra)
            mine = head_lanes((count, 128), head)
            left = jnp.where(mine, queries.astype(F32) * HD ** (-0.5), extra).astype(BF)
            out_parts = []
            for start, stop, key in window_split(slot, rows):
                keys = k_ref[key : key + KEYS]
                right = jnp.where(head_lanes((KEYS, 128), head), keys, tab_ref[head])
                scores = mm_t(left[start:stop], right)
                grown = jnp.exp(scores - jnp.max(scores, -1, keepdims=True))
                probs = (grown * (1.0 / jnp.sum(grown, -1, keepdims=True))).astype(BF)
                p_ref[0, head, start:stop, :] = probs
                out_parts.append(mm(probs, v_ref[key : key + KEYS]))
            outs[head] = jnp.concatenate(out_parts, 0)
        o_ref[...] = jnp.where(head_lanes((count, 128), 0), outs[0], outs[1]).astype(BF)

    for slot in range(slots):
        pl.when(place_ref[0] == slot)(partial(variant, slot))


def attend(slot, q, k, v, rel, table, rows, slots):
    queries = rows * PITCH
    steps = SIDE * PAIRS
    return pl.pallas_call(
        partial(attend_body, rows=rows, slots=slots),
        grid_spec=pltpu.PrefetchScalarGridSpec(
            num_scalar_prefetch=1,
            grid=(SIDE, PAIRS),
            in_specs=[
                pl.BlockSpec((queries, 128), lambda b, p, s: (b, p)),
                pl.BlockSpec((EXT * PITCH, 128), lambda b, p, s: (b, p)),
                pl.BlockSpec((EXT * PITCH, 128), lambda b, p, s: (b, p)),
                pl.BlockSpec((128, 256), lambda b, p, s: (0, 0)),
                pl.BlockSpec((2, KEYS, 128), lambda b, p, s: (0, 0, 0)),
            ],
            out_specs=[
                pl.BlockSpec((queries, 128), lambda b, p, s: (b, p)),
                pl.BlockSpec((1, 2, queries, KEYS), lambda b, p, s: (b * PAIRS + p, 0, 0, 0)),
            ],
        ),
        out_shape=[
            jax.ShapeDtypeStruct((SIDE * queries, D), BF),
            jax.ShapeDtypeStruct((steps, 2, queries, KEYS), BF),
        ],
        compiler_params=pltpu.CompilerParams(vmem_limit_bytes=60 << 20),
        name="attend",
    )(slot, q, k, v, rel, table)


def attend_back_body(
    place_ref, q_ref, k_ref, v_ref, p_ref, do_ref, rel_ref, tab_ref,
    dq_ref, dk_ref, dv_ref, drel_ref, *, rows, slots,
):
    count = rows * PITCH

    @pl.when((pl.program_id(0) == 0) & (pl.program_id(1) == 0))
    def _():
        drel_ref[...] = jnp.zeros_like(drel_ref)

    def variant(slot):
        queries = q_ref[...]
        scaled = (queries.astype(F32) * HD ** (-0.5)).astype(BF)
        lane = lax.broadcasted_iota(jnp.int32, (PITCH, 128), 1)
        upstream = do_ref[...]
        split = window_split(slot, rows)
        grad_keys = [[None, None], [None, None]]
        grad_values = [[None, None], [None, None]]
        grad_left, grad_raw = [], []
        for head in range(2):
            base = 64 - 64 * head
            grad_out = jnp.where(head_lanes((count, 128), head), upstream, jnp.zeros_like(upstream))
            lefts = []
            for w, (start, stop, key) in enumerate(split):
                keys, values = k_ref[key : key + KEYS], v_ref[key : key + KEYS]
                probs = p_ref[0, head, start:stop, :]
                grad_probs = mm_t(grad_out[start:stop], values)
                exact = probs.astype(F32)
                inner = jnp.sum(exact * grad_probs, -1, keepdims=True)
                grad_scores = (exact * (grad_probs - inner)).astype(BF)
                grad_values[head][w] = t_mm(probs, grad_out[start:stop])
                right = jnp.where(head_lanes((KEYS, 128), head), keys, tab_ref[head])
                lefts.append(mm(grad_scores, right))
                grad_keys[head][w] = t_mm(grad_scores, scaled[start:stop])
            left = jnp.concatenate(lefts, 0)
            grad_left.append(left)
            parts = []
            for r in range(rows):
                here = left[r * PITCH : (r + 1) * PITCH]
                on_row = jnp.where((lane >= base) & (lane < base + WIN), here, 0.0)
                on_col = jnp.where((lane >= base + 32) & (lane < base + 32 + WIN), here, 0.0)
                on_row = pltpu.roll(on_row, (2 * slot + r) % WIN, 1)
                on_col = pltpu.roll(on_col, 0, 1, stride=1, stride_axis=0)
                parts.append(on_row + on_col)
            grad_raw.append(jnp.concatenate(parts, 0))
        raw = jnp.concatenate(grad_raw, 1).astype(BF)
        first = head_lanes((count, 128), 0)
        direct = jnp.where(first, grad_left[0], grad_left[1]) * HD ** (-0.5)
        dq_ref[...] = (direct + mm(raw, rel_ref[...])).astype(BF)
        drel_ref[...] += t_mm(raw, queries)
        first = head_lanes((KEYS, 128), 0)
        for w, (_, _, key) in enumerate(split):
            dk_ref[key : key + KEYS] = jnp.where(first, grad_keys[0][w], grad_keys[1][w]).astype(BF)
            dv_ref[key : key + KEYS] = (grad_values[0][w] + grad_values[1][w]).astype(BF)

    for slot in range(slots):
        pl.when(place_ref[0] == slot)(partial(variant, slot))


def attend_back(slot, q, k, v, probs, grad_out, rel, table, rows, slots):
    queries = rows * PITCH
    of_q = pl.BlockSpec((queries, 128), lambda b, p, s: (b, p))
    of_k = pl.BlockSpec((EXT * PITCH, 128), lambda b, p, s: (b, p))
    return pl.pallas_call(
        partial(attend_back_body, rows=rows, slots=slots),
        grid_spec=pltpu.PrefetchScalarGridSpec(
            num_scalar_prefetch=1,
            grid=(SIDE, PAIRS),
            in_specs=[
                of_q, of_k, of_k,
                pl.BlockSpec((1, 2, queries, KEYS), lambda b, p, s: (b * PAIRS + p, 0, 0, 0)),
                of_q,
                pl.BlockSpec((256, 128), lambda b, p, s: (0, 0)),
                pl.BlockSpec((2, KEYS, 128), lambda b, p, s: (0, 0, 0)),
            ],
            out_specs=[of_q, of_k, of_k, pl.BlockSpec((256, 128), lambda b, p, s: (0, 0))],
        ),
        out_shape=[
            jax.ShapeDtypeStruct(q.shape, BF),
            jax.ShapeDtypeStruct(k.shape, BF),
            jax.ShapeDtypeStruct(k.shape, BF),
            jax.ShapeDtypeStruct((256, 128), F32),
        ],
        compiler_params=pltpu.CompilerParams(vmem_limit_bytes=60 << 20),
        name="attend_back",
    )(slot, q, k, v, probs, grad_out, rel, table)


def feed_body(
    o_ref, x_ref, g_ref, wo_ref, up_ref, down_ref, vec_ref, bias_ref,
    out_ref, dh_ref, do_ref, gwo_ref, gup_ref, gdown_ref, gvec_ref, gbias_ref,
    nat_ref, onat_ref, n2_ref, h_ref, y_ref, dn_ref, a_ref, du_ref, *, rows, chunks,
):
    step = pl.program_id(0)
    steps = rows * GRID // 256
    lines = 256 // GRID
    blocks = up_ref.shape[0]

    @pl.when(step == 0)
    def _():
        def one(i, carry):
            at = pl.ds(pl.multiple_of(i * 256, 256), 256)
            for b in range(SIDE):
                piece = o_ref[b, pl.ds(i * lines, lines)]
                nat_ref[:, WIN * b : WIN * b + PITCH, :] = piece.astype(F32)
            natural = nat_ref[:, 0:GRID, :].reshape(256, D).astype(BF)
            onat_ref[at, :] = natural
            hidden = x_ref[at, :].astype(F32) + mm_t(natural, wo_ref[...]) + vec_ref[0:1]
            h_ref[at, :] = hidden
            hat, _ = norm_parts(hidden)
            n2_ref[at, :] = (hat * vec_ref[1:2] + vec_ref[2:3]).astype(BF)
            y_ref[at, :] = jnp.zeros((256, D), F32)
            dn_ref[at, :] = jnp.zeros((256, D), F32)
            return carry

        lax.fori_loop(0, steps, one, 0)

    up = up_ref[...].reshape(D, D)
    down = down_ref[...].reshape(D, D)

    def two(i, total):
        at = pl.ds(pl.multiple_of(i * 256, 256), 256)
        upper = mm(n2_ref[at, :], up) + bias_ref[...].reshape(1, D)
        cdf = 0.5 * (1.0 + lax.erf(upper * (1.0 / math.sqrt(2.0))))
        active = (upper * cdf).astype(BF)
        a_ref[at, :] = active
        y_ref[at, :] += mm_t(active, down)
        slope = cdf + upper * jnp.exp(-0.5 * upper * upper) * (1.0 / math.sqrt(2.0 * math.pi))
        delta = (mm(g_ref[at, :], down) * slope).astype(BF)
        du_ref[at, :] = delta
        dn_ref[at, :] += mm_t(delta, up)
        return total + jnp.sum(delta.astype(F32), 0, keepdims=True)

    total = lax.fori_loop(0, steps, two, jnp.zeros((1, D), F32))
    gbias_ref[...] = total.reshape(gbias_ref.shape)
    gup_ref[...] = t_mm(n2_ref[...], du_ref[...]).astype(BF).reshape(gup_ref.shape)
    gdown_ref[...] = t_mm(g_ref[...], a_ref[...]).astype(BF).reshape(gdown_ref.shape)

    @pl.when(step == chunks - 1)
    def _():
        nat_ref[...] = jnp.zeros_like(nat_ref)
        gvec_ref[...] = jnp.zeros_like(gvec_ref)

        def three(i, carry):
            at = pl.ds(pl.multiple_of(i * 256, 256), 256)
            hidden = h_ref[at, :]
            grad = g_ref[at, :].astype(F32)
            hat, inverse = norm_parts(hidden)
            grad_normed = dn_ref[at, :]
            out_ref[at, :] = (hidden + y_ref[at, :] + vec_ref[3:4]).astype(BF)
            grad_hidden = grad + norm_back(grad_normed, hat, inverse, vec_ref[1:2])
            dh_ref[at, :] = grad_hidden
            branch = grad_hidden.astype(BF)
            n2_ref[at, :] = branch
            gvec_ref[0:1] += jnp.sum(grad_normed * hat, 0, keepdims=True)
            gvec_ref[1:2] += jnp.sum(grad_normed, 0, keepdims=True)
            gvec_ref[2:3] += jnp.sum(branch.astype(F32), 0, keepdims=True)
            gvec_ref[3:4] += jnp.sum(grad, 0, keepdims=True)
            grad_out = mm(branch, wo_ref[...])
            nat_ref[:, 0:GRID, :] = grad_out.reshape(lines, GRID, D)
            keep = lax.broadcasted_iota(jnp.int32, (lines, PITCH, D), 1) < WIN
            for b in range(SIDE):
                piece = nat_ref[:, WIN * b : WIN * b + PITCH, :]
                do_ref[b, pl.ds(i * lines, lines)] = jnp.where(keep, piece, 0.0).astype(BF)
            return carry

        lax.fori_loop(0, steps, three, 0)
        gwo_ref[...] = t_mm(n2_ref[...], onat_ref[...]).astype(BF)


def feed(o, x, g, wo, up, down, vectors, up_bias, rows):
    tokens = rows * GRID
    blocks, chunks, depth = up.shape[:3]
    whole = lambda shape: pl.BlockSpec(shape, lambda c: (0,) * len(shape), pipeline_mode=pl.Buffered(1))
    slab = pl.BlockSpec((blocks, None, depth, D), lambda c: (0, c, 0, 0))
    line = pl.BlockSpec((None, 1, D), lambda c: (c, 0, 0))
    grid = (SIDE, rows, PITCH, D)
    return pl.pallas_call(
        partial(feed_body, rows=rows, chunks=chunks),
        grid=(chunks,),
        in_specs=[
            whole(grid), whole((tokens, D)), whole((tokens, D)), whole((D, D)), slab, slab, whole((8, D)), line,
        ],
        out_specs=[
            whole((tokens, D)), whole((tokens, D)), whole(grid), whole((D, D)), slab, slab, whole((8, D)), line,
        ],
        out_shape=[
            jax.ShapeDtypeStruct((tokens, D), BF),
            jax.ShapeDtypeStruct((tokens, D), F32),
            jax.ShapeDtypeStruct(grid, BF),
            jax.ShapeDtypeStruct((D, D), BF),
            jax.ShapeDtypeStruct(up.shape, BF),
            jax.ShapeDtypeStruct(down.shape, BF),
            jax.ShapeDtypeStruct((8, D), F32),
            jax.ShapeDtypeStruct((chunks, 1, D), F32),
        ],
        scratch_shapes=[
            pltpu.VMEM((256 // GRID, GRID + PITCH, D), F32),
            pltpu.VMEM((tokens, D), BF),
            pltpu.VMEM((tokens, D), BF),
            pltpu.VMEM((tokens, D), F32),
            pltpu.VMEM((tokens, D), F32),
            pltpu.VMEM((tokens, D), F32),
            pltpu.VMEM((tokens, D), BF),
            pltpu.VMEM((tokens, D), BF),
        ],
        compiler_params=pltpu.CompilerParams(vmem_limit_bytes=63 << 20),
        name="feed",
    )(o, x, g, wo, up, down, vectors, up_bias)


def body(
    features, first_gain, first_shift, qkv_weight, qv_bias, rel_height, rel_width, output_weight,
    output_bias, second_gain, second_shift, up_weight, up_bias, down_weight, down_bias, cotangent,
    *, groups, slots,
):
    both = ("dp", "tensor")
    depth, _, width = qkv_weight.shape
    hidden = up_weight.shape[1]
    tokens = features.shape[0]
    rows = tokens // GRID
    above, below = 2 * (slots - 1), WIN - 2
    slot = lax.axis_index("tensor")
    place = slot.astype(jnp.int32).reshape(1)

    qkv_all = lax.all_gather(qkv_weight.reshape(depth, 3 * width), both, axis=0)
    rest = jnp.concatenate([output_weight, up_weight, down_weight], 1)
    rest_all = lax.all_gather(rest, both, axis=0).reshape(groups, slots, depth, width + 2 * hidden)
    qkv_full = qkv_all.reshape(groups, slots, depth, 3, width).transpose(0, 2, 3, 1, 4).reshape(D, 3 * D)
    out_full = rest_all[..., :width].transpose(0, 2, 1, 3).reshape(D, D)
    up_all = rest_all[..., width : width + hidden]
    down_all = rest_all[..., width + hidden :]
    biases = lax.all_gather(jnp.concatenate([qv_bias.reshape(-1), up_bias]), "tensor", axis=0)
    qv_all = biases[:, : 2 * width].reshape(slots, 2, width).transpose(1, 0, 2).reshape(2, D)
    up_bias_all = biases[:, 2 * width :].astype(F32).reshape(slots, 1, hidden)

    grid_x = features.reshape(rows, GRID, D)
    up_pairs = [(s, s + 1) for s in range(slots - 1)]
    down_pairs = [(s + 1, s) for s in range(slots - 1)]
    from_above = lax.ppermute(grid_x[rows - above :], "tensor", up_pairs)
    from_below = lax.ppermute(grid_x[:below], "tensor", down_pairs)
    x_ext = lax.dynamic_slice_in_dim(
        jnp.concatenate([from_above, grid_x, from_below], 0), above - 2 * slot, EXT, 0
    )

    vec_one = jnp.concatenate(
        [first_gain[None], first_shift[None], qv_all, jnp.zeros((4, D), BF)], 0
    ).astype(F32)
    normed, q, k, v = project(place, x_ext, vec_one, qkv_full, rows)
    ahead, back = score_tables()
    rel_ahead, rel_back = offset_tables(rel_height, rel_width)
    attended, probs = attend(
        place, q, k, v, rel_ahead.T, jnp.asarray(ahead, BF), rows, slots
    )

    vec_two = jnp.concatenate(
        [output_bias[None], second_gain[None], second_shift[None], down_bias[None], jnp.zeros((4, D), BF)], 0
    ).astype(F32)
    output, grad_hidden, grad_out, grad_wo, grad_up, grad_down, grad_vec, grad_up_bias = feed(
        attended.reshape(SIDE, rows, PITCH, D), features, cotangent, out_full, up_all, down_all,
        vec_two, up_bias_all, rows,
    )
    dq, dk, dv, drel = attend_back(
        place, q, k, v, probs, grad_out.reshape(-1, D), rel_back, jnp.asarray(back, BF), rows, slots
    )

    banded = normed.reshape(SIDE, EXT, PITCH, D)
    own = lax.dynamic_slice_in_dim(banded, 2 * slot, rows, 1).reshape(-1, D)
    grad_wq, grad_wk, grad_wv = t_mm(own, dq), t_mm(normed, dk), t_mm(normed, dv)
    grad_normed = mm_t(dk, qkv_full[:, D : 2 * D]) + mm_t(dv, qkv_full[:, 2 * D :])
    grad_own = mm_t(dq, qkv_full[:, :D])

    def natural(windows, lines):
        grid = windows.reshape(SIDE, lines, PITCH, D)[:, :, :WIN]
        return grid.transpose(1, 0, 2, 3).reshape(lines, SIDE * WIN, D)[:, :GRID]

    wide = jnp.zeros((above + rows + below, GRID, D), F32)
    wide = lax.dynamic_update_slice_in_dim(wide, natural(grad_normed, EXT), above - 2 * slot, 0)
    to_above = wide[:above].astype(BF)
    to_below = wide[above + rows :].astype(BF)
    from_below = lax.ppermute(to_above, "tensor", down_pairs).astype(F32)
    from_above = lax.ppermute(to_below, "tensor", up_pairs).astype(F32)
    total = wide[above : above + rows] + natural(grad_own, rows)
    total = total + jnp.pad(from_above, ((0, rows - below), (0, 0), (0, 0)))
    total = total + jnp.pad(from_below, ((rows - above, 0), (0, 0), (0, 0)))
    total = total.reshape(tokens, D)
    hat, inverse = norm_parts(features.astype(F32))
    grad_features = (grad_hidden + norm_back(total, hat, inverse, vec_one[0:1])).astype(BF)
    grad_gain_one = jnp.sum(total * hat, 0)
    grad_shift_one = jnp.sum(total, 0)
    grad_qv = jnp.stack([jnp.sum(dq.astype(F32), 0), jnp.sum(dv.astype(F32), 0)])

    grad_rest = jnp.concatenate(
        [grad_wo.reshape(groups, depth, slots, width).transpose(0, 2, 1, 3), grad_up, grad_down], -1
    )
    grad_rest = lax.psum_scatter(
        grad_rest.reshape(groups * slots, depth, width + 2 * hidden), both, scatter_dimension=0
    ).astype(F32)
    grad_qkv = jnp.stack([grad_wq, grad_wk, grad_wv], 1).astype(BF)
    grad_qkv = grad_qkv.reshape(groups, depth, 3, slots, width).transpose(0, 3, 1, 2, 4)
    grad_qkv = lax.psum_scatter(
        grad_qkv.reshape(groups * slots, depth, 3 * width), both, scatter_dimension=0
    ).astype(F32)
    small = lax.psum(
        jnp.concatenate(
            [
                grad_vec[:4].reshape(-1), grad_gain_one, grad_shift_one, grad_qv.reshape(-1),
                grad_up_bias.reshape(-1), drel.reshape(-1),
            ]
        ),
        both,
    )
    vec = small[: 6 * D].reshape(6, D)
    qv = small[6 * D : 8 * D].reshape(2, slots, width)
    qv = lax.dynamic_index_in_dim(qv, slot, 1, keepdims=False)
    bias = small[8 * D : 8 * D + slots * hidden].reshape(slots, hidden)
    bias = lax.dynamic_index_in_dim(bias, slot, 0, keepdims=False)
    drel = small[8 * D + slots * hidden :].reshape(4, 64, 128)
    drel = drel[1, :, :HD] + drel[2, :, HD:]
    return (
        output,
        grad_features,
        vec[4],
        vec[5],
        grad_qkv.reshape(depth, 3, width),
        qv,
        drel[0:OFFS],
        drel[32 : 32 + OFFS],
        grad_rest[:, :width],
        vec[2],
        vec[0],
        vec[1],
        grad_rest[:, width : width + hidden],
        bias,
        grad_rest[:, width + hidden :],
        vec[3],
    )


def solution(mesh):
    token = P(("dp", "tensor"), None)
    square = P("dp", "tensor")
    cube = P("dp", None, "tensor")
    return jax.shard_map(
        partial(body, groups=mesh.shape["dp"], slots=mesh.shape["tensor"]),
        mesh=mesh,
        in_specs=(
            token, P(), P(), cube, P(None, "tensor"), P(), P(), square, P(), P(), P(), square,
            P("tensor"), square, P(), token,
        ),
        out_specs=(
            token, token, P(), P(), cube, P(None, "tensor"), P(), P(), square, P(), P(), P(), square,
            P("tensor"), square, P(),
        ),
        check_vma=False,
    )
```

```python
from functools import partial
import math

import jax
import jax.numpy as jnp
from jax import lax
from jax.experimental import pallas as pl
from jax.experimental.pallas import tpu as pltpu
from jax.sharding import PartitionSpec as P
import numpy as np

D = 768
HD = 64
GRID = 64
WIN = 14
SIDE = 5
PITCH = 16
KEYS = WIN * PITCH
EXT = 2 * WIN
PAIRS = D // (2 * HD)
OFFS = 2 * WIN - 1
EPSILON = 1e-06
FAR = -1e30
BF = jnp.bfloat16
F32 = jnp.float32
HIGH = lax.Precision.HIGHEST


def mm(left, right):
    return jnp.dot(left, right, preferred_element_type=F32)


def mm_t(left, right):
    return lax.dot_general(left, right, (((1,), (1,)), ((), ())), preferred_element_type=F32)


def t_mm(left, right):
    return lax.dot_general(left, right, (((0,), (0,)), ((), ())), preferred_element_type=F32)


def norm_parts(value):
    centered = value - jnp.mean(value, -1, keepdims=True)
    inverse = lax.rsqrt(jnp.mean(centered * centered, -1, keepdims=True) + EPSILON)
    return centered * inverse, inverse


def norm_back(upstream, hat, inverse, gain):
    scaled = upstream * gain
    return inverse * (
        scaled
        - jnp.mean(scaled, -1, keepdims=True)
        - hat * jnp.mean(scaled * hat, -1, keepdims=True)
    )


def score_tables():
    ahead = np.zeros((2, KEYS, 128), np.float32)
    back = np.zeros((2, KEYS, 128), np.float32)
    for head in range(2):
        base = 64 - 64 * head
        for c in range(WIN):
            for e in range(PITCH):
                k = c * PITCH + e
                if e >= WIN:
                    ahead[head, k, base] = FAR
                    continue
                ahead[head, k, base + 15 + c] = 1
                ahead[head, k, base + 1 + c] = 1
                ahead[head, k, base + 46 + e] = 1
                ahead[head, k, base + 32 + e] = 1
                back[head, k, base + WIN - 1 - c] = 1
                back[head, k, base + 32 + WIN - 1 - e] = 1
    return ahead, back


def offset_tables(rel_height, rel_width):
    def place(first, second, at_rows, at_cols):
        slab = jnp.zeros((64, HD), BF)
        slab = slab.at[at_rows : at_rows + OFFS].set(first)
        slab = slab.at[at_cols : at_cols + OFFS].set(second)
        low = jnp.concatenate([slab, jnp.zeros_like(slab)], 1)
        high = jnp.concatenate([jnp.zeros_like(slab), slab], 1)
        return jnp.concatenate([jnp.zeros_like(low), low, high, jnp.zeros_like(high)], 0)

    return (
        place(rel_height[::-1], rel_width[::-1], 2, 33),
        place(rel_height, rel_width, 0, 32),
    )


def whole(shape):
    return pl.BlockSpec(shape, lambda *_: (0,) * len(shape), pipeline_mode=pl.Buffered(1))


def windows_body(place_ref, above_ref, x_ref, below_ref, vec_ref, nw_ref, nat_ref, *, rows):
    band = pl.program_id(0)
    slot = place_ref[0]
    above, below = above_ref.shape[0], below_ref.shape[0]

    @pl.when(band == 0)
    def _():
        def normed(piece):
            hat, _ = norm_parts(piece.astype(F32))
            return hat * vec_ref[0:1] + vec_ref[1:2]

        def clear(i, carry):
            nat_ref[i, GRID : GRID + PITCH, :] = jnp.zeros((PITCH, D), F32)
            return carry

        def own(i, carry):
            nat_ref[2 * slot + i, 0:GRID, :] = normed(x_ref[i])
            return carry

        def before(i, carry):
            nat_ref[i, 0:GRID, :] = normed(above_ref[above - 2 * slot + i])
            return carry

        def after(i, carry):
            at = 2 * slot + rows + i
            inside = WIN * slot + at < GRID
            nat_ref[at, 0:GRID, :] = jnp.where(inside, normed(below_ref[i]), 0.0)
            return carry

        lax.fori_loop(0, EXT, clear, 0)
        lax.fori_loop(0, rows, own, 0)
        lax.fori_loop(0, 2 * slot, before, 0)
        lax.fori_loop(0, EXT - rows - 2 * slot, after, 0)

    keep = lax.broadcasted_iota(jnp.int32, (PITCH, D), 0) < WIN
    for b in range(SIDE):
        @pl.when(band == b)
        def _(b=b):
            def one(i, carry):
                piece = nat_ref[i, WIN * b : WIN * b + PITCH, :]
                start = pl.multiple_of(i * PITCH, PITCH)
                nw_ref[pl.ds(start, PITCH), :] = jnp.where(keep, piece, 0.0).astype(BF)
                return carry

            lax.fori_loop(0, EXT, one, 0)


def windows(place, above, x, below, vectors):
    rows = x.shape[0]
    return pl.pallas_call(
        partial(windows_body, rows=rows),
        grid_spec=pltpu.PrefetchScalarGridSpec(
            num_scalar_prefetch=1,
            grid=(SIDE,),
            in_specs=[whole(above.shape), whole(x.shape), whole(below.shape), whole((8, D))],
            out_specs=pl.BlockSpec((EXT * PITCH, D), lambda b, s: (b, 0)),
            scratch_shapes=[pltpu.VMEM((EXT, GRID + PITCH, D), F32)],
        ),
        out_shape=jax.ShapeDtypeStruct((SIDE * EXT * PITCH, D), BF),
        compiler_params=pltpu.CompilerParams(vmem_limit_bytes=63 << 20),
        cost_estimate=guess(8),
        name="windows",
    )(place, above, x, below, vectors)


def project_body(place_ref, nw_ref, *refs, rows, depth):
    *pieces, bias_ref, q_ref, k_ref, v_ref, w_ref, stage_ref = refs
    slot, z, x, y, c = (place_ref[i] for i in range(5))
    width = D // 4

    @pl.when(pl.program_id(0) == 0)
    def _():
        if len(pieces) == 1:
            w_ref[...] = pieces[0][...]
            return
        half = depth // 2
        for sibling in range(2):
            for part in range(2):
                ref = pieces[2 * sibling + part]
                count = ref.shape[2]
                for first in range(2):
                    for second in range(2):
                        dy, dx = (first, second) if part == 0 else (second, first)
                        from_slot = (y ^ dy) * 2 + (c ^ sibling)
                        for dz in range(count):
                            group = lax.rem(z - dz + count, count) * 2 + (x ^ dx)
                            at = pl.multiple_of(group * depth + part * half, half)
                            stage_ref[from_slot, pl.ds(at, half), :] = ref[first, second, dz]

        def join(i, carry):
            at = pl.ds(pl.multiple_of(i * 64, 64), 64)
            for kind in range(3):
                w_ref[at, kind * D : (kind + 1) * D] = jnp.concatenate(
                    [stage_ref[t, at, kind * width : (kind + 1) * width] for t in range(4)], 1
                )
            return carry

        lax.fori_loop(0, D // 64, join, 0)

    normed = nw_ref[...]
    own = nw_ref[pl.ds(pl.multiple_of(slot * 2 * PITCH, 2 * PITCH), rows * PITCH), :]
    q_ref[...] = (mm(own, w_ref[:, 0:D]) + bias_ref[0:1]).astype(BF)
    k_ref[...] = mm(normed, w_ref[:, D : 2 * D]).astype(BF)
    v_ref[...] = (mm(normed, w_ref[:, 2 * D :]) + bias_ref[1:2]).astype(BF)


def guess(us):
    return pl.CostEstimate(flops=int(us * 1.1e9), bytes_accessed=int(us * 3e6), transcendentals=0)


def project(place, normed, pieces, bias, rows, depth):
    of_k = pl.BlockSpec((EXT * PITCH, D), lambda b, s: (b, 0))
    of_q = pl.BlockSpec((rows * PITCH, D), lambda b, s: (b, 0))
    keys = jax.ShapeDtypeStruct((SIDE * EXT * PITCH, D), BF)
    return pl.pallas_call(
        partial(project_body, rows=rows, depth=depth),
        grid_spec=pltpu.PrefetchScalarGridSpec(
            num_scalar_prefetch=1,
            grid=(SIDE,),
            in_specs=[of_k] + [whole(p.shape) for p in pieces] + [whole((2, D))],
            out_specs=[of_q, of_k, of_k, whole((D, 3 * D))],
            scratch_shapes=[pltpu.VMEM((4, D, 3 * D // 4), BF)],
        ),
        out_shape=[
            jax.ShapeDtypeStruct((SIDE * rows * PITCH, D), BF), keys, keys,
            jax.ShapeDtypeStruct((D, 3 * D), BF),
        ],
        compiler_params=pltpu.CompilerParams(vmem_limit_bytes=63 << 20),
        cost_estimate=guess(18),
        name="project",
    )(place, normed, *pieces, bias)


def store_shards(place_ref, refs, value, first=0, lane=0):
    z, x = place_ref[1], place_ref[2]
    count, _, depth = refs.shape[:3]
    lanes = slice(lane, lane + value.shape[1])
    if depth % 32:
        refs[:, :, :, lanes] = value.reshape(count, 2, depth, value.shape[1])
        return
    for zd in range(value.shape[0] // (2 * depth)):
        for xd in range(2):
            start = (zd * 2 + xd) * depth
            refs[lax.rem(first + zd - z + count, count), x ^ xd, :, lanes] = value[start : start + depth]


def project_grad_body(place_ref, nw_ref, dq_ref, dk_ref, dv_ref, send_ref, keep_ref, bias_ref, *, rows, parts):
    step = pl.program_id(0)
    slot, c = place_ref[0], place_ref[4]
    width = D // 4
    lines = rows * PITCH

    @pl.when(step == 0)
    def _():
        bias_ref[0:1] = jnp.sum(dq_ref[...].astype(F32), 0, keepdims=True)
        bias_ref[1:2] = jnp.sum(dv_ref[...].astype(F32), 0, keepdims=True)

    grad_q = None
    for b in range(SIDE):
        start = pl.multiple_of(b * EXT * PITCH + slot * 2 * PITCH, 2 * PITCH)
        term = t_mm(nw_ref[pl.ds(start, lines), :], dq_ref[b * lines : (b + 1) * lines])
        grad_q = term if grad_q is None else grad_q + term
    grads = [grad_q.astype(BF)] + [t_mm(nw_ref[...], ref[...]).astype(BF) for ref in (dk_ref, dv_ref)]
    first = step * (keep_ref.shape[0] // parts)
    for core in range(2):
        value = jnp.concatenate([g[:, core * width : (core + 1) * width] for g in grads], 1)
        for sibling, ref in ((1, send_ref), (0, keep_ref)):
            @pl.when(c ^ core == sibling)
            def _(ref=ref, value=value):
                store_shards(place_ref, ref, value, first)


def project_grad(place, normed, dq, dk, dv, rows, shards):
    count, depth = shards[1], shards[3]
    parts = 2 if depth % 32 == 0 else 1
    out = jax.ShapeDtypeStruct((count, 2, depth, 3 * D // 4), BF)
    return pl.pallas_call(
        partial(project_grad_body, rows=rows, parts=parts),
        grid_spec=pltpu.PrefetchScalarGridSpec(
            num_scalar_prefetch=1,
            grid=(parts,),
            in_specs=[
                pl.BlockSpec((normed.shape[0], D // parts), lambda i, s: (0, i)),
                whole(dq.shape), whole(dk.shape), whole(dv.shape),
            ],
            out_specs=[whole(out.shape), whole(out.shape), whole((2, D // 2))],
        ),
        out_shape=[out, out, jax.ShapeDtypeStruct((2, D // 2), F32)],
        compiler_params=pltpu.CompilerParams(vmem_limit_bytes=63 << 20),
        cost_estimate=guess(6),
        name="project_grad",
    )(place, normed, dq, dk, dv)


def project_back_body(place_ref, *refs, rows):
    dqs, dks, dvs = refs[0:2], refs[2:4], refs[4:6]
    w_ref, above_ref, own_ref, below_ref, nat_ref, dq_ref, dk_ref, dv_ref = refs[6:]
    band = pl.program_id(0)
    slot, y = place_ref[0], place_ref[5]
    above, below = above_ref.shape[0], below_ref.shape[0]

    @pl.when(band == 0)
    def _():
        nat_ref[...] = jnp.zeros_like(nat_ref)

    for halves, ref in ((dqs, dq_ref), (dks, dk_ref), (dvs, dv_ref)):
        for i in range(2):
            at = pl.multiple_of((y ^ (1 - i)) * (D // 2), D // 2)
            ref[:, pl.ds(at, D // 2)] = halves[i][...]
    grad = mm_t(dk_ref[...], w_ref[:, D : 2 * D]) + mm_t(dv_ref[...], w_ref[:, 2 * D :])
    grad = grad.reshape(EXT, PITCH, D)
    direct = mm_t(dq_ref[...], w_ref[:, 0:D]).reshape(rows, PITCH, D)
    base = above - 2 * slot
    for b in range(SIDE):
        @pl.when(band == b)
        def _(b=b):
            at = slice(WIN * b, WIN * b + PITCH)
            nat_ref[pl.ds(base, EXT), at, :] = grad
            nat_ref[above : above + rows, at, :] += direct

    @pl.when(band == SIDE - 1)
    def _():
        above_ref[...] = nat_ref[0:above, 0:GRID, :].astype(BF)
        own_ref[...] = nat_ref[above : above + rows, 0:GRID, :]
        below_ref[...] = nat_ref[above + rows :, 0:GRID, :].astype(BF)


def project_back(place, dqs, dks, dvs, weight, rows, slots):
    above, below = 2 * (slots - 1), WIN - 2
    of_k = pl.BlockSpec((EXT * PITCH, D // 2), lambda b, s: (b, 0))
    of_q = pl.BlockSpec((rows * PITCH, D // 2), lambda b, s: (b, 0))
    shapes = [
        jax.ShapeDtypeStruct((above, GRID, D), BF),
        jax.ShapeDtypeStruct((rows, GRID, D), F32),
        jax.ShapeDtypeStruct((below, GRID, D), BF),
    ]
    return pl.pallas_call(
        partial(project_back_body, rows=rows),
        grid_spec=pltpu.PrefetchScalarGridSpec(
            num_scalar_prefetch=1,
            grid=(SIDE,),
            in_specs=[of_q, of_q, of_k, of_k, of_k, of_k, whole((D, 3 * D))],
            out_specs=[whole(s.shape) for s in shapes],
            scratch_shapes=[
                pltpu.VMEM((above + rows + below, GRID + PITCH, D), F32),
                pltpu.VMEM((rows * PITCH, D), BF),
                pltpu.VMEM((EXT * PITCH, D), BF),
                pltpu.VMEM((EXT * PITCH, D), BF),
            ],
        ),
        out_shape=shapes,
        compiler_params=pltpu.CompilerParams(vmem_limit_bytes=63 << 20),
        cost_estimate=guess(14),
        name="project_back",
    )(place, *dqs, *dks, *dvs, weight)


def head_lanes(shape, head):
    lane = lax.broadcasted_iota(jnp.int32, shape, 1)
    return lane < HD if head == 0 else lane >= HD


def window_split(slot, rows):
    first = WIN - 2 * slot
    return ((0, first * PITCH, 0), (first * PITCH, rows * PITCH, KEYS))


def attend_body(place_ref, q_ref, k_ref, v_ref, rel_ref, tab_ref, o_ref, p_ref, *, rows, slots):
    def variant(slot):
        queries = q_ref[...]
        count = rows * PITCH
        lane = lax.broadcasted_iota(jnp.int32, (PITCH, 128), 1)
        raw = mm(queries, rel_ref[...])
        outs = [None, None]
        for head in range(2):
            base = 64 - 64 * head
            parts = []
            for r in range(rows):
                here = raw[r * PITCH : (r + 1) * PITCH, 128 * head : 128 * head + 128]
                along_row = pltpu.roll(here, (2 * slot + r) % WIN, 1)
                along_col = pltpu.roll(here, 0, 1, stride=1, stride_axis=0)
                both = jnp.where(lane < base + 32, along_row, along_col)
                wanted = ((lane >= base + 15) & (lane < base + 29)) | ((lane >= base + 46) & (lane < base + 60))
                parts.append(jnp.where(wanted, both, 0.0))
            along = jnp.concatenate(parts, 0)
            high = along.astype(BF).astype(F32)
            extra = high + pltpu.roll(along - high, 114, 1)
            wide = lax.broadcasted_iota(jnp.int32, (count, 128), 1)
            extra = jnp.where(wide == base, 1.0, extra)
            mine = head_lanes((count, 128), head)
            left = jnp.where(mine, queries.astype(F32) * HD ** (-0.5), extra).astype(BF)
            out_parts = []
            for start, stop, key in window_split(slot, rows):
                keys = k_ref[key : key + KEYS]
                right = jnp.where(head_lanes((KEYS, 128), head), keys, tab_ref[head])
                scores = mm_t(left[start:stop], right)
                grown = jnp.exp(scores - jnp.max(scores, -1, keepdims=True))
                probs = (grown * (1.0 / jnp.sum(grown, -1, keepdims=True))).astype(BF)
                p_ref[0, head, start:stop, :] = probs
                out_parts.append(mm(probs, v_ref[key : key + KEYS]))
            outs[head] = jnp.concatenate(out_parts, 0)
        o_ref[...] = jnp.where(head_lanes((count, 128), 0), outs[0], outs[1]).astype(BF)

    for slot in range(slots):
        pl.when(place_ref[0] == slot)(partial(variant, slot))


def attend(slot, q, k, v, rel, table, rows, slots):
    queries = rows * PITCH
    steps = SIDE * PAIRS
    return pl.pallas_call(
        partial(attend_body, rows=rows, slots=slots),
        grid_spec=pltpu.PrefetchScalarGridSpec(
            num_scalar_prefetch=1,
            grid=(SIDE, PAIRS),
            in_specs=[
                pl.BlockSpec((queries, 128), lambda b, p, s: (b, p)),
                pl.BlockSpec((EXT * PITCH, 128), lambda b, p, s: (b, p)),
                pl.BlockSpec((EXT * PITCH, 128), lambda b, p, s: (b, p)),
                pl.BlockSpec((128, 256), lambda b, p, s: (0, 0)),
                pl.BlockSpec((2, KEYS, 128), lambda b, p, s: (0, 0, 0)),
            ],
            out_specs=[
                pl.BlockSpec((queries, 128), lambda b, p, s: (b, p)),
                pl.BlockSpec((1, 2, queries, KEYS), lambda b, p, s: (b * PAIRS + p, 0, 0, 0)),
            ],
        ),
        out_shape=[
            jax.ShapeDtypeStruct((SIDE * queries, D), BF),
            jax.ShapeDtypeStruct((steps, 2, queries, KEYS), BF),
        ],
        compiler_params=pltpu.CompilerParams(vmem_limit_bytes=63 << 20),
        cost_estimate=guess(43),
        name="attend",
    )(slot, q, k, v, rel, table)


def attend_back_body(
    place_ref, q_ref, k_ref, v_ref, p_ref, do_ref, rel_ref, tab_ref,
    dq_ref, dk_ref, dv_ref, drel_ref, *, rows, slots,
):
    count = rows * PITCH

    @pl.when((pl.program_id(0) == 0) & (pl.program_id(1) == 0))
    def _():
        drel_ref[...] = jnp.zeros_like(drel_ref)

    def variant(slot):
        queries = q_ref[...]
        scaled = (queries.astype(F32) * HD ** (-0.5)).astype(BF)
        lane = lax.broadcasted_iota(jnp.int32, (PITCH, 128), 1)
        upstream = do_ref[...]
        split = window_split(slot, rows)
        grad_keys = [[None, None], [None, None]]
        grad_values = [[None, None], [None, None]]
        grad_left, grad_raw = [], []
        for head in range(2):
            base = 64 - 64 * head
            grad_out = jnp.where(head_lanes((count, 128), head), upstream, jnp.zeros_like(upstream))
            lefts = []
            for w, (start, stop, key) in enumerate(split):
                keys, values = k_ref[key : key + KEYS], v_ref[key : key + KEYS]
                probs = p_ref[0, head, start:stop, :]
                grad_probs = mm_t(grad_out[start:stop], values)
                exact = probs.astype(F32)
                inner = jnp.sum(exact * grad_probs, -1, keepdims=True)
                grad_scores = (exact * (grad_probs - inner)).astype(BF)
                grad_values[head][w] = t_mm(probs, grad_out[start:stop])
                right = jnp.where(head_lanes((KEYS, 128), head), keys, tab_ref[head])
                lefts.append(mm(grad_scores, right))
                grad_keys[head][w] = t_mm(grad_scores, scaled[start:stop])
            left = jnp.concatenate(lefts, 0)
            grad_left.append(left)
            parts = []
            for r in range(rows):
                here = left[r * PITCH : (r + 1) * PITCH]
                on_row = jnp.where((lane >= base) & (lane < base + WIN), here, 0.0)
                on_col = jnp.where((lane >= base + 32) & (lane < base + 32 + WIN), here, 0.0)
                on_row = pltpu.roll(on_row, (2 * slot + r) % WIN, 1)
                on_col = pltpu.roll(on_col, 0, 1, stride=1, stride_axis=0)
                parts.append(on_row + on_col)
            grad_raw.append(jnp.concatenate(parts, 0))
        raw = jnp.concatenate(grad_raw, 1).astype(BF)
        first = head_lanes((count, 128), 0)
        direct = jnp.where(first, grad_left[0], grad_left[1]) * HD ** (-0.5)
        dq_ref[...] = (direct + mm(raw, rel_ref[...])).astype(BF)
        drel_ref[...] += t_mm(raw, queries)
        first = head_lanes((KEYS, 128), 0)
        for w, (_, _, key) in enumerate(split):
            dk_ref[key : key + KEYS] = jnp.where(first, grad_keys[0][w], grad_keys[1][w]).astype(BF)
            dv_ref[key : key + KEYS] = (grad_values[0][w] + grad_values[1][w]).astype(BF)

    for slot in range(slots):
        pl.when(place_ref[0] == slot)(partial(variant, slot))


def attend_back(slot, q, k, v, probs, grad_out, rel, table, rows, slots, group):
    queries = rows * PITCH
    half = PAIRS // 2
    pair = lambda p, s: p + half * (s[5] ^ (1 - group))
    of_q = pl.BlockSpec((queries, 128), lambda b, p, s: (b, pair(p, s)))
    of_k = pl.BlockSpec((EXT * PITCH, 128), lambda b, p, s: (b, pair(p, s)))
    to_q = pl.BlockSpec((queries, 128), lambda b, p, s: (b, p))
    to_k = pl.BlockSpec((EXT * PITCH, 128), lambda b, p, s: (b, p))
    return pl.pallas_call(
        partial(attend_back_body, rows=rows, slots=slots),
        grid_spec=pltpu.PrefetchScalarGridSpec(
            num_scalar_prefetch=1,
            grid=(SIDE, half),
            in_specs=[
                of_q, of_k, of_k,
                pl.BlockSpec((1, 2, queries, KEYS), lambda b, p, s: (b * PAIRS + pair(p, s), 0, 0, 0)),
                of_q,
                pl.BlockSpec((256, 128), lambda b, p, s: (0, 0)),
                pl.BlockSpec((2, KEYS, 128), lambda b, p, s: (0, 0, 0)),
            ],
            out_specs=[to_q, to_k, to_k, pl.BlockSpec((256, 128), lambda b, p, s: (0, 0))],
        ),
        out_shape=[
            jax.ShapeDtypeStruct((q.shape[0], D // 2), BF),
            jax.ShapeDtypeStruct((k.shape[0], D // 2), BF),
            jax.ShapeDtypeStruct((k.shape[0], D // 2), BF),
            jax.ShapeDtypeStruct((256, 128), F32),
        ],
        compiler_params=pltpu.CompilerParams(vmem_limit_bytes=63 << 20),
        cost_estimate=guess(24),
        name="attend_back",
    )(slot, q, k, v, probs, grad_out, rel, table)


def chunk_of(step, place):
    return (place[3] ^ (1 - step % 2)) * 2 + (place[4] ^ (1 - step // 2))


def feed_body(
    place_ref, o_ref, x_ref, g_ref, wo_ref, up_ref, down_ref, vec_ref, bias_ref,
    out_ref, dh_ref, do_ref, gas_ref, gak_ref, gbs_ref, gbk_ref, gvec_ref, gbias_ref,
    nat_ref, onat_ref, n2_ref, h_ref, y_ref, dn_ref, a_ref, du_ref, w_ref, *, rows,
):
    step = pl.program_id(0)
    steps = rows * GRID // 256
    lines = 256 // GRID
    width = D // 4

    @pl.when(step == 0)
    def _():
        for t in range(4):
            w_ref[:, t * width : (t + 1) * width] = wo_ref[:, t, :, 0:width].reshape(D, width)

        def one(i, carry):
            at = pl.ds(pl.multiple_of(i * 256, 256), 256)
            for b in range(SIDE):
                piece = o_ref[b, pl.ds(i * lines, lines)]
                nat_ref[:, WIN * b : WIN * b + PITCH, :] = piece.astype(F32)
            natural = nat_ref[:, 0:GRID, :].reshape(256, D).astype(BF)
            onat_ref[at, :] = natural
            hidden = x_ref[at, :].astype(F32) + mm_t(natural, w_ref[...]) + vec_ref[0:1]
            h_ref[at, :] = hidden
            hat, _ = norm_parts(hidden)
            n2_ref[at, :] = (hat * vec_ref[1:2] + vec_ref[2:3]).astype(BF)
            y_ref[at, :] = jnp.zeros((256, D), F32)
            dn_ref[at, :] = jnp.zeros((256, D), F32)
            return carry

        lax.fori_loop(0, steps, one, 0)

    up = up_ref[...].reshape(D, D)
    down = down_ref[...].reshape(D, D)

    def two(i, total):
        at = pl.ds(pl.multiple_of(i * 256, 256), 256)
        upper = mm(n2_ref[at, :], up) + bias_ref[...].reshape(1, D)
        cdf = 0.5 * (1.0 + lax.erf(upper * (1.0 / math.sqrt(2.0))))
        active = (upper * cdf).astype(BF)
        a_ref[at, :] = active
        y_ref[at, :] += mm_t(active, down)
        slope = cdf + upper * jnp.exp(-0.5 * upper * upper) * (1.0 / math.sqrt(2.0 * math.pi))
        delta = (mm(g_ref[at, :], down) * slope).astype(BF)
        du_ref[at, :] = delta
        dn_ref[at, :] += mm_t(delta, up)
        return total + jnp.sum(delta.astype(F32), 0, keepdims=True)

    total = lax.fori_loop(0, steps, two, jnp.zeros((1, D), F32))
    gbias_ref[...] = total.reshape(gbias_ref.shape)
    grad_up = t_mm(n2_ref[...], du_ref[...]).astype(BF)
    grad_down = t_mm(g_ref[...], a_ref[...]).astype(BF)

    other_chip = 1 - step % 2

    @pl.when(step < 2)
    def _():
        store_shards(place_ref, gas_ref.at[other_chip], grad_up)
        store_shards(place_ref, gbs_ref.at[other_chip], grad_down)

    @pl.when(step >= 2)
    def _():
        store_shards(place_ref, gak_ref.at[other_chip], grad_up)
        store_shards(place_ref, gbk_ref.at[other_chip], grad_down)

    @pl.when(step == pl.num_programs(0) - 1)
    def _():
        nat_ref[...] = jnp.zeros_like(nat_ref)
        gvec_ref[...] = jnp.zeros_like(gvec_ref)

        def three(i, carry):
            at = pl.ds(pl.multiple_of(i * 256, 256), 256)
            hidden = h_ref[at, :]
            grad = g_ref[at, :].astype(F32)
            hat, inverse = norm_parts(hidden)
            grad_normed = dn_ref[at, :]
            out_ref[at, :] = (hidden + y_ref[at, :] + vec_ref[3:4]).astype(BF)
            grad_hidden = grad + norm_back(grad_normed, hat, inverse, vec_ref[1:2])
            dh_ref[at, :] = grad_hidden
            branch = grad_hidden.astype(BF)
            n2_ref[at, :] = branch
            gvec_ref[0:1] += jnp.sum(grad_normed * hat, 0, keepdims=True)
            gvec_ref[1:2] += jnp.sum(grad_normed, 0, keepdims=True)
            gvec_ref[2:3] += jnp.sum(branch.astype(F32), 0, keepdims=True)
            gvec_ref[3:4] += jnp.sum(grad, 0, keepdims=True)
            grad_out = mm(branch, w_ref[...])
            nat_ref[:, 0:GRID, :] = grad_out.reshape(lines, GRID, D)
            keep = lax.broadcasted_iota(jnp.int32, (lines, PITCH, D), 1) < WIN
            for b in range(SIDE):
                piece = nat_ref[:, WIN * b : WIN * b + PITCH, :]
                do_ref[b, pl.ds(i * lines, lines)] = jnp.where(keep, piece, 0.0).astype(BF)
            return carry

        lax.fori_loop(0, steps, three, 0)
        grad_wo = t_mm(n2_ref[...], onat_ref[...]).astype(BF)
        for sibling, ref in ((1, gas_ref), (0, gak_ref)):
            for t in range(4):
                @pl.when(place_ref[4] ^ (t % 2) == sibling)
                def _(t=t, ref=ref):
                    store_shards(
                        place_ref, ref.at[place_ref[3] ^ (t // 2)], grad_wo[:, t * width : (t + 1) * width], lane=D
                    )


def feed(place, o, x, g, rest, vectors, up_bias, rows, shards):
    tokens = rows * GRID
    blocks, chunks, depth = rest.shape[:3]
    width = D // chunks
    slab = lambda column: pl.BlockSpec(
        (blocks, None, depth, D), lambda s, p: (0, chunk_of(s, p), 0, column)
    )
    line = pl.BlockSpec((None, 1, D), lambda s, p: (chunk_of(s, p), 0, 0))
    grid = (SIDE, rows, PITCH, D)
    first = jax.ShapeDtypeStruct((*shards, D + width), BF)
    second = jax.ShapeDtypeStruct((*shards, D), BF)
    shapes = [
        jax.ShapeDtypeStruct((tokens, D), BF),
        jax.ShapeDtypeStruct((tokens, D), F32),
        jax.ShapeDtypeStruct(grid, BF),
        first, first, second, second,
        jax.ShapeDtypeStruct((8, D), F32),
        jax.ShapeDtypeStruct((chunks, 1, D), F32),
    ]
    specs = [whole(s.shape) for s in shapes]
    specs[8] = line
    return pl.pallas_call(
        partial(feed_body, rows=rows),
        grid_spec=pltpu.PrefetchScalarGridSpec(
            num_scalar_prefetch=1,
            grid=(chunks,),
            in_specs=[
                whole(grid), whole((tokens, D)), whole((tokens, D)),
                pl.BlockSpec((blocks, chunks, depth, 256), lambda s, p: (0, 0, 0, 2 * D // 256), pipeline_mode=pl.Buffered(1)),
                slab(0), slab(1), whole((8, D)), line,
            ],
            out_specs=specs,
            scratch_shapes=[
                pltpu.VMEM((256 // GRID, GRID + PITCH, D), F32),
                pltpu.VMEM((tokens, D), BF),
                pltpu.VMEM((tokens, D), BF),
                pltpu.VMEM((tokens, D), F32),
                pltpu.VMEM((tokens, D), F32),
                pltpu.VMEM((tokens, D), F32),
                pltpu.VMEM((tokens, D), BF),
                pltpu.VMEM((tokens, D), BF),
                pltpu.VMEM((D, D), BF),
            ],
        ),
        out_shape=shapes,
        compiler_params=pltpu.CompilerParams(vmem_limit_bytes=63 << 20),
        cost_estimate=guess(55),
        name="feed",
    )(place, o, x, g, rest, rest, rest, vectors, up_bias)


def finish_body(own_ref, head_ref, tail_ref, x_ref, dh_ref, vec_ref, out_ref, sum_ref):
    rows, below, above = own_ref.shape[0], head_ref.shape[0], tail_ref.shape[0]
    sum_ref[...] = jnp.zeros_like(sum_ref)

    def line(i, low, high):
        grad = own_ref[i]
        if low:
            grad = grad + head_ref[i].astype(F32)
        if high:
            grad = grad + tail_ref[i - (rows - above)].astype(F32)
        hat, inverse = norm_parts(x_ref[i].astype(F32))
        out_ref[i] = (dh_ref[i] + norm_back(grad, hat, inverse, vec_ref[0:1])).astype(BF)
        sum_ref[0:1] += jnp.sum(grad * hat, 0, keepdims=True)
        sum_ref[1:2] += jnp.sum(grad, 0, keepdims=True)

    def over(start, stop, low, high):
        lax.fori_loop(start, stop, lambda i, carry: (line(i, low, high), carry)[1], 0)

    over(0, rows - above, True, False)
    over(rows - above, below, True, True)
    over(below, rows, False, True)


def finish(own, head, tail, x, dh, vectors):
    shapes = [jax.ShapeDtypeStruct(own.shape, BF), jax.ShapeDtypeStruct((8, D), F32)]
    return pl.pallas_call(
        finish_body,
        grid=(1,),
        in_specs=[whole(v.shape) for v in (own, head, tail, x, dh, vectors)],
        out_specs=[whole(v.shape) for v in shapes],
        out_shape=shapes,
        compiler_params=pltpu.CompilerParams(vmem_limit_bytes=63 << 20),
        cost_estimate=guess(5),
        name="finish",
    )(own, head, tail, x, dh, vectors)


def fold_body(*refs, plan):
    terms = sum(count for count, *_ in plan)
    ins, outs = refs[:terms], refs[terms:]
    for (count, axis, index), out in zip(plan, outs):
        here, ins = ins[:count], ins[count:]
        lead = out.shape[:-2]
        for at in np.ndindex(*lead):
            spot = at if axis is None else at[:axis] + (index,) + at[axis:]
            total = here[0][spot].astype(F32)
            for ref in here[1:]:
                total = total + ref[spot].astype(F32)
            out[at] = total.astype(out.dtype)


def fold(*results):
    count = None
    args, in_specs, out_specs, shapes, plan = [], [], [], [], []
    for terms, z_axis, axis, index in results:
        shape = terms[0].shape
        count = shape[z_axis]
        block = tuple(None if i == z_axis else n for i, n in enumerate(shape))
        spec = pl.BlockSpec(block, lambda i, z_axis=z_axis, n=len(shape): tuple(i if k == z_axis else 0 for k in range(n)))
        args += terms
        in_specs += [spec] * len(terms)
        left = [n for i, n in enumerate(shape) if i != axis]
        z_left = z_axis if axis is None or axis > z_axis else z_axis - 1
        block = tuple(None if i == z_left else n for i, n in enumerate(left))
        out_specs.append(
            pl.BlockSpec(block, lambda i, z_left=z_left, n=len(left): tuple(i if k == z_left else 0 for k in range(n)))
        )
        shapes.append(jax.ShapeDtypeStruct(tuple(left), BF))
        inner = None if axis is None else (axis if axis < z_axis else axis - 1)
        plan.append((len(terms), inner, index))
    size = sum(2 * int(np.prod(a.shape)) for a in args)
    return pl.pallas_call(
        partial(fold_body, plan=plan),
        grid=(count,),
        in_specs=in_specs,
        out_specs=out_specs,
        out_shape=shapes,
        compiler_params=pltpu.CompilerParams(vmem_limit_bytes=63 << 20),
        cost_estimate=guess(1 + size / 2e6),
        name="fold",
    )(*args)


AXES = ("z", "x", "y", "c")
SWAP = [(0, 1), (1, 0)]


def swap(value, axis):
    return lax.ppermute(value, axis, SWAP)


def shift(value, count, by):
    return lax.ppermute(value, "z", [(i, (i + by) % count) for i in range(count)])


def gather_lines(shard, count):
    half = shard.shape[0] // 2
    lines = [shard] + [shift(shard, count, k) for k in range(1, count)]
    first = jnp.stack([line[:half] for line in lines])
    second = jnp.stack([line[half:] for line in lines])
    return jnp.stack([first, swap(first, "x")]), jnp.stack([second, swap(second, "y")])


def gather_planes(first, second):
    first = jnp.stack([first, swap(first, "y")])
    second = jnp.stack([second, swap(second, "x")])
    return first, second, swap(first, "c"), swap(second, "c")


def along_z(pieces):
    count = pieces.shape[0]
    total = pieces[0].astype(F32)
    for k in range(1, count):
        total = total + shift(pieces[k], count, k).astype(F32)
    return total


def sum_all(value, count, fast):
    for axis in ("c", "y", "x"):
        value = value + swap(value, axis)
    if not fast:
        return lax.psum(value, "z")
    step = 1
    while step < count:
        value = value + lax.ppermute(value, "z", [(i, i ^ step) for i in range(count)])
        step *= 2
    return value


def body(
    features, first_gain, first_shift, qkv_weight, qv_bias, rel_height, rel_width, output_weight,
    output_bias, second_gain, second_shift, up_weight, up_bias, down_weight, down_bias, cotangent,
    *, count,
):
    depth, _, width = qkv_weight.shape
    hidden = up_weight.shape[1]
    tokens = features.shape[0]
    rows = tokens // GRID
    slots = 4
    fast = count <= 4 and depth % 32 == 0
    z, x, y, c = (lax.axis_index(a).astype(jnp.int32) for a in AXES)
    slot = 2 * y + c
    nought = jnp.zeros((), jnp.int32)
    place = jnp.stack([slot, z, x, y, c, y] if fast else [slot] + [nought] * 4 + [y])
    shards = (2, count, 2, depth)
    above, below = 2 * (slots - 1), WIN - 2

    grid_x = features.reshape(rows, GRID, D)
    pair = ("y", "c")
    up_pairs = [(s, s + 1) for s in range(slots - 1)]
    down_pairs = [(s + 1, s) for s in range(slots - 1)]
    from_above = lax.ppermute(grid_x[rows - above :], pair, up_pairs)
    from_below = lax.ppermute(grid_x[:below], pair, down_pairs)

    rest = jnp.concatenate([up_weight, down_weight, output_weight, jnp.zeros((depth, 256 - width), BF)], 1)
    rest_all = lax.all_gather(rest, AXES, axis=0).reshape(2 * count, slots, depth, 2 * hidden + 256)
    biases = jnp.concatenate([qv_bias.reshape(-1), up_bias])
    biases = jnp.where(jnp.arange(slots)[:, None] == slot, biases[None], jnp.zeros((), BF))
    biases = biases + swap(biases, "c")
    biases = (biases + swap(biases, "y")).astype(F32)
    qv_all = biases[:, : 2 * width].reshape(slots, 2, width).transpose(1, 0, 2).reshape(2, D)
    up_bias_all = biases[:, 2 * width :].reshape(slots, 1, hidden)

    vec_one = jnp.concatenate([first_gain[None], first_shift[None], jnp.zeros((6, D), BF)], 0).astype(F32)
    normed = windows(place, from_above, grid_x, from_below, vec_one)
    if fast:
        lines = gather_lines(qkv_weight.reshape(depth, 3 * width), count)
        normed, *lines = lax.optimization_barrier((normed, *lines))
        pieces = gather_planes(*lines)
    else:
        full = lax.all_gather(qkv_weight, AXES, axis=0).reshape(2 * count, slots, depth, 3, width)
        pieces = [full.transpose(0, 2, 3, 1, 4).reshape(D, 3 * D)]
    q, k, v, weight = project(place, normed, pieces, qv_all, rows, depth)
    ahead, back = score_tables()
    rel_ahead, rel_back = offset_tables(rel_height, rel_width)
    attended, probs = attend(place, q, k, v, rel_ahead.T, jnp.asarray(ahead, BF), rows, slots)

    vec_two = jnp.concatenate(
        [output_bias[None], second_gain[None], second_shift[None], down_bias[None], jnp.zeros((4, D), BF)], 0
    ).astype(F32)
    (
        output, grad_hidden, grad_out, a_send, a_keep, b_send, b_keep, grad_vec, grad_up_bias,
    ) = feed(
        place, attended.reshape(SIDE, rows, PITCH, D), features, cotangent, rest_all, vec_two, up_bias_all,
        rows, shards,
    )
    grad_windows = grad_out.reshape(-1, D)
    table = jnp.asarray(back, BF)
    if fast:
        a_got, b_got = swap(a_send, "c"), swap(b_send, "c")
    *half0, drel0 = attend_back(place, q, k, v, probs, grad_windows, rel_back, table, rows, slots, 0)
    if fast:
        a, b = [a_keep, a_got], [b_keep, b_got]
        a_away, a_here, b_away, b_here = fold((a, 1, 0, 1), (a, 1, 0, 0), (b, 1, 2, 1), (b, 1, 2, 0))
        place, a_away, b_away = lax.optimization_barrier((place, a_away, b_away))
        a_got, b_got = swap(a_away, "y"), swap(b_away, "x")
    first_send, first_keep, first_bias = project_grad(place, normed, *half0, rows, shards)
    if fast:
        first_got = swap(first_send, "c")
    *half1, drel1 = attend_back(place, q, k, v, probs, grad_windows, rel_back, table, rows, slots, 1)
    if fast:
        a, b = [a_here, a_got], [b_here, b_got]
        a_away, a_here, b_away, b_here, crossing = fold(
            (a, 0, 1, 1), (a, 0, 1, 0), (b, 1, 0, 1), (b, 1, 0, 0), ([first_keep, first_got], 0, None, None)
        )
        place, a_away, b_away, crossing = lax.optimization_barrier((place, a_away, b_away, crossing))
        a_got, b_got, crossing = swap(a_away, "x"), swap(b_away, "y"), swap(crossing, "y")
    dqs, dks, dvs = zip(half0, half1)
    to_above, total, to_below = project_back(place, dqs, dks, dvs, weight, rows, slots)
    from_below = lax.ppermute(to_above, pair, down_pairs)
    from_above = lax.ppermute(to_below, pair, up_pairs)
    place, to_above = lax.optimization_barrier((place, to_above))
    last_send, last_keep, last_bias = project_grad(place, normed, *half1, rows, shards)
    if fast:
        last_got = swap(last_send, "c")
        a, b = fold(([a_here, a_got], 0, None, None), ([b_here, b_got], 0, None, None))
        a, b = along_z(a), along_z(b)
        grad_up, grad_wo, grad_down = a[:, :hidden], a[:, hidden:], b
    grad_features, sums_one = finish(
        total, from_above, from_below, grid_x, grad_hidden.reshape(rows, GRID, D), vec_one
    )
    if fast:
        last = [last_keep, last_got, crossing]
        away, here = fold((last, 0, 1, 1), (last, 0, 1, 0))
        (last,) = fold(([here, swap(away, "x")], 0, None, None))
        grad_qkv = along_z(last)
    else:
        pairs = [
            (a_send, a_keep), (b_send, b_keep),
            [
                jnp.where(y == 0, jnp.stack([last, first]), jnp.stack([first, last]))
                for first, last in ((first_send, last_send), (first_keep, last_keep))
            ],
        ]
        a, grad_down, grad_qkv = [
            lax.psum_scatter(
                jnp.stack([keep, send], 3).transpose(1, 2, 0, 3, 4, 5).reshape(8 * count, depth, -1),
                AXES, scatter_dimension=0,
            ).astype(F32)
            for send, keep in pairs
        ]
        grad_up, grad_wo = a[:, :hidden], a[:, hidden:]
    drel = (drel0 + drel1).reshape(4, 64, 128)
    drel = drel[1, :, :HD] + drel[2, :, HD:]
    grad_qv = jnp.where(y == 0, jnp.concatenate([last_bias, first_bias], 1), jnp.concatenate([first_bias, last_bias], 1))
    small = jnp.concatenate(
        [grad_vec[:4], grad_up_bias.reshape(slots, hidden), sums_one[:2], grad_qv], 0
    )
    small = sum_all(jnp.concatenate([small.reshape(-1), drel.reshape(-1)]).reshape(-1, 512), count, fast).reshape(-1)
    vec = small[: 12 * D].reshape(12, D)
    drel = small[12 * D :].reshape(64, HD)
    qv = lax.dynamic_index_in_dim(vec[10:12].reshape(2, slots, width), slot, 1, keepdims=False)
    bias = lax.dynamic_index_in_dim(vec[4:8], slot, 0, keepdims=False)
    return (
        output,
        grad_features.reshape(tokens, D),
        vec[8],
        vec[9],
        grad_qkv.reshape(depth, 3, width),
        qv,
        drel[0:OFFS],
        drel[32 : 32 + OFFS],
        grad_wo,
        vec[2],
        vec[0],
        vec[1],
        grad_up,
        bias,
        grad_down,
        vec[3],
    )


def solution(mesh):
    token = P(AXES, None)
    square = P(("z", "x"), ("y", "c"))
    cube = P(("z", "x"), None, ("y", "c"))
    lane = P(("y", "c"))
    count = mesh.shape["dp"] // 2
    assert mesh.shape["tensor"] == 4
    return jax.shard_map(
        partial(body, count=count),
        mesh=jax.sharding.Mesh(mesh.devices.reshape(count, 2, 2, 2), AXES),
        in_specs=(
            token, P(), P(), cube, P(None, ("y", "c")), P(), P(), square, P(), P(), P(), square,
            lane, square, P(), token,
        ),
        out_specs=(
            token, token, P(), P(), cube, P(None, ("y", "c")), P(), P(), square, P(), P(), P(), square,
            lane, square, P(),
        ),
        check_vma=False,
    )
```

```python
from functools import partial
import math

import jax
import jax.numpy as jnp
from jax import lax
from jax.experimental import pallas as pl
from jax.experimental.pallas import tpu as pltpu
from jax.sharding import PartitionSpec as P
import numpy as np

D = 768
HD = 64
GRID = 64
WIN = 14
SIDE = 5
PITCH = 16
KEYS = WIN * PITCH
EXT = 2 * WIN
PAIRS = D // (2 * HD)
OFFS = 2 * WIN - 1
EPSILON = 1e-06
FAR = -1e30
BF = jnp.bfloat16
F32 = jnp.float32
HIGH = lax.Precision.HIGHEST


def mm(left, right):
    return jnp.dot(left, right, preferred_element_type=F32)


def mm_t(left, right):
    return lax.dot_general(left, right, (((1,), (1,)), ((), ())), preferred_element_type=F32)


def t_mm(left, right):
    return lax.dot_general(left, right, (((0,), (0,)), ((), ())), preferred_element_type=F32)


def norm_parts(value):
    centered = value - jnp.mean(value, -1, keepdims=True)
    inverse = lax.rsqrt(jnp.mean(centered * centered, -1, keepdims=True) + EPSILON)
    return centered * inverse, inverse


def norm_back(upstream, hat, inverse, gain):
    scaled = upstream * gain
    return inverse * (
        scaled
        - jnp.mean(scaled, -1, keepdims=True)
        - hat * jnp.mean(scaled * hat, -1, keepdims=True)
    )


def score_tables():
    ahead = np.zeros((2, KEYS, 128), np.float32)
    back = np.zeros((2, KEYS, 128), np.float32)
    for head in range(2):
        base = 64 - 64 * head
        for c in range(WIN):
            for e in range(PITCH):
                k = c * PITCH + e
                if e >= WIN:
                    ahead[head, k, base] = FAR
                    continue
                ahead[head, k, base + 15 + c] = 1
                ahead[head, k, base + 1 + c] = 1
                ahead[head, k, base + 46 + e] = 1
                ahead[head, k, base + 32 + e] = 1
                back[head, k, base + WIN - 1 - c] = 1
                back[head, k, base + 32 + WIN - 1 - e] = 1
    return ahead, back


def offset_tables(rel_height, rel_width):
    def place(first, second, at_rows, at_cols):
        slab = jnp.zeros((64, HD), BF)
        slab = slab.at[at_rows : at_rows + OFFS].set(first)
        slab = slab.at[at_cols : at_cols + OFFS].set(second)
        low = jnp.concatenate([slab, jnp.zeros_like(slab)], 1)
        high = jnp.concatenate([jnp.zeros_like(slab), slab], 1)
        return jnp.concatenate([jnp.zeros_like(low), low, high, jnp.zeros_like(high)], 0)

    through = jnp.eye(HD, dtype=BF) * BF(HD ** (-0.5))
    nothing = jnp.zeros_like(through)
    through = jnp.concatenate(
        [jnp.concatenate([through, nothing], 1), jnp.zeros((128, 128), BF), jnp.concatenate([nothing, through], 1)], 0
    )
    return (
        place(rel_height[::-1], rel_width[::-1], 2, 33) + through,
        place(rel_height, rel_width, 0, 32),
    )


def whole(shape):
    return pl.BlockSpec(shape, lambda *_: (0,) * len(shape), pipeline_mode=pl.Buffered(1))


def windows_body(place_ref, above_ref, x_ref, below_ref, vec_ref, nw_ref, nat_ref, *, rows):
    band = pl.program_id(0)
    slot = place_ref[0]
    above, below = above_ref.shape[0], below_ref.shape[0]

    @pl.when(band == 0)
    def _():
        def normed(piece):
            hat, _ = norm_parts(piece.astype(F32))
            return hat * vec_ref[0:1] + vec_ref[1:2]

        def clear(i, carry):
            nat_ref[i, GRID : GRID + PITCH, :] = jnp.zeros((PITCH, D), F32)
            return carry

        def own(i, carry):
            nat_ref[2 * slot + i, 0:GRID, :] = normed(x_ref[i])
            return carry

        def before(i, carry):
            nat_ref[i, 0:GRID, :] = normed(above_ref[above - 2 * slot + i])
            return carry

        def after(i, carry):
            at = 2 * slot + rows + i
            inside = WIN * slot + at < GRID
            nat_ref[at, 0:GRID, :] = jnp.where(inside, normed(below_ref[i]), 0.0)
            return carry

        lax.fori_loop(0, EXT, clear, 0)
        lax.fori_loop(0, rows, own, 0)
        lax.fori_loop(0, 2 * slot, before, 0)
        lax.fori_loop(0, EXT - rows - 2 * slot, after, 0)

    keep = lax.broadcasted_iota(jnp.int32, (PITCH, D), 0) < WIN
    for b in range(SIDE):
        @pl.when(band == b)
        def _(b=b):
            def one(i, carry):
                piece = nat_ref[i, WIN * b : WIN * b + PITCH, :]
                start = pl.multiple_of(i * PITCH, PITCH)
                nw_ref[pl.ds(start, PITCH), :] = jnp.where(keep, piece, 0.0).astype(BF)
                return carry

            lax.fori_loop(0, EXT, one, 0)


def windows(place, above, x, below, vectors):
    rows = x.shape[0]
    return pl.pallas_call(
        partial(windows_body, rows=rows),
        grid_spec=pltpu.PrefetchScalarGridSpec(
            num_scalar_prefetch=1,
            grid=(SIDE,),
            in_specs=[whole(above.shape), whole(x.shape), whole(below.shape), whole((8, D))],
            out_specs=pl.BlockSpec((EXT * PITCH, D), lambda b, s: (b, 0)),
            scratch_shapes=[pltpu.VMEM((EXT, GRID + PITCH, D), F32)],
        ),
        out_shape=jax.ShapeDtypeStruct((SIDE * EXT * PITCH, D), BF),
        compiler_params=pltpu.CompilerParams(vmem_limit_bytes=63 << 20),
        cost_estimate=guess(8),
        name="windows",
    )(place, above, x, below, vectors)


def project_body(place_ref, nw_ref, *refs, rows, depth):
    *pieces, bias_ref, q_ref, k_ref, v_ref, w_ref, stage_ref = refs
    slot, z, x, y, c = (place_ref[i] for i in range(5))
    width = D // 4

    @pl.when(pl.program_id(0) == 0)
    def _():
        if len(pieces) == 1:
            w_ref[...] = pieces[0][...]
            return
        half = depth // 2
        for sibling in range(2):
            for part in range(2):
                ref = pieces[2 * sibling + part]
                count = ref.shape[2]
                for first in range(2):
                    for second in range(2):
                        dy, dx = (first, second) if part == 0 else (second, first)
                        from_slot = (y ^ dy) * 2 + (c ^ sibling)
                        for dz in range(count):
                            group = lax.rem(z - dz + count, count) * 2 + (x ^ dx)
                            at = pl.multiple_of(group * depth + part * half, half)
                            stage_ref[from_slot, pl.ds(at, half), :] = ref[first, second, dz]

        def join(i, carry):
            at = pl.ds(pl.multiple_of(i * 64, 64), 64)
            for kind in range(3):
                w_ref[at, kind * D : (kind + 1) * D] = jnp.concatenate(
                    [stage_ref[t, at, kind * width : (kind + 1) * width] for t in range(4)], 1
                )
            return carry

        lax.fori_loop(0, D // 64, join, 0)

    normed = nw_ref[...]
    own = nw_ref[pl.ds(pl.multiple_of(slot * 2 * PITCH, 2 * PITCH), rows * PITCH), :]
    q_ref[...] = (mm(own, w_ref[:, 0:D]) + bias_ref[0:1]).astype(BF)
    k_ref[...] = mm(normed, w_ref[:, D : 2 * D]).astype(BF)
    v_ref[...] = (mm(normed, w_ref[:, 2 * D :]) + bias_ref[1:2]).astype(BF)


def guess(us):
    return pl.CostEstimate(flops=int(us * 1.1e9), bytes_accessed=int(us * 3e6), transcendentals=0)


def project(place, normed, pieces, bias, rows, depth):
    of_k = pl.BlockSpec((EXT * PITCH, D), lambda b, s: (b, 0))
    of_q = pl.BlockSpec((rows * PITCH, D), lambda b, s: (b, 0))
    keys = jax.ShapeDtypeStruct((SIDE * EXT * PITCH, D), BF)
    return pl.pallas_call(
        partial(project_body, rows=rows, depth=depth),
        grid_spec=pltpu.PrefetchScalarGridSpec(
            num_scalar_prefetch=1,
            grid=(SIDE,),
            in_specs=[of_k] + [whole(p.shape) for p in pieces] + [whole((2, D))],
            out_specs=[of_q, of_k, of_k, whole((D, 3 * D))],
            scratch_shapes=[pltpu.VMEM((4, D, 3 * D // 4), BF)],
        ),
        out_shape=[
            jax.ShapeDtypeStruct((SIDE * rows * PITCH, D), BF), keys, keys,
            jax.ShapeDtypeStruct((D, 3 * D), BF),
        ],
        compiler_params=pltpu.CompilerParams(vmem_limit_bytes=63 << 20),
        cost_estimate=guess(18),
        name="project",
    )(place, normed, *pieces, bias)


def store_shards(place_ref, refs, value, first=0, lane=0):
    z, x = place_ref[1], place_ref[2]
    count, _, depth = refs.shape[:3]
    lanes = slice(lane, lane + value.shape[1])
    if depth % 32:
        refs[:, :, :, lanes] = value.reshape(count, 2, depth, value.shape[1])
        return
    for zd in range(value.shape[0] // (2 * depth)):
        for xd in range(2):
            start = (zd * 2 + xd) * depth
            refs[lax.rem(first + zd - z + count, count), x ^ xd, :, lanes] = value[start : start + depth]


def project_grad_body(place_ref, nw_ref, dq_ref, dk_ref, dv_ref, send_ref, keep_ref, bias_ref, *, rows, parts):
    step = pl.program_id(0)
    slot, c = place_ref[0], place_ref[4]
    width = D // 4
    lines = rows * PITCH

    @pl.when(step == 0)
    def _():
        bias_ref[0:1] = jnp.sum(dq_ref[...].astype(F32), 0, keepdims=True)
        bias_ref[1:2] = jnp.sum(dv_ref[...].astype(F32), 0, keepdims=True)

    grad_q = None
    for b in range(SIDE):
        start = pl.multiple_of(b * EXT * PITCH + slot * 2 * PITCH, 2 * PITCH)
        term = t_mm(nw_ref[pl.ds(start, lines), :], dq_ref[b * lines : (b + 1) * lines])
        grad_q = term if grad_q is None else grad_q + term
    grads = [grad_q.astype(BF)] + [t_mm(nw_ref[...], ref[...]).astype(BF) for ref in (dk_ref, dv_ref)]
    first = step * (keep_ref.shape[0] // parts)
    for core in range(2):
        value = jnp.concatenate([g[:, core * width : (core + 1) * width] for g in grads], 1)
        for sibling, ref in ((1, send_ref), (0, keep_ref)):
            @pl.when(c ^ core == sibling)
            def _(ref=ref, value=value):
                store_shards(place_ref, ref, value, first)


def project_grad(place, normed, dq, dk, dv, rows, shards):
    count, depth = shards[1], shards[3]
    parts = 2 if depth % 32 == 0 else 1
    out = jax.ShapeDtypeStruct((count, 2, depth, 3 * D // 4), BF)
    return pl.pallas_call(
        partial(project_grad_body, rows=rows, parts=parts),
        grid_spec=pltpu.PrefetchScalarGridSpec(
            num_scalar_prefetch=1,
            grid=(parts,),
            in_specs=[
                pl.BlockSpec((normed.shape[0], D // parts), lambda i, s: (0, i)),
                whole(dq.shape), whole(dk.shape), whole(dv.shape),
            ],
            out_specs=[whole(out.shape), whole(out.shape), whole((2, D // 2))],
        ),
        out_shape=[out, out, jax.ShapeDtypeStruct((2, D // 2), F32)],
        compiler_params=pltpu.CompilerParams(vmem_limit_bytes=63 << 20),
        cost_estimate=guess(6),
        name="project_grad",
    )(place, normed, dq, dk, dv)


def project_back_body(place_ref, *refs, rows):
    dqs, dks, dvs = refs[0:2], refs[2:4], refs[4:6]
    w_ref, above_ref, own_ref, below_ref, nat_ref, dq_ref, dk_ref, dv_ref = refs[6:]
    band = pl.program_id(0)
    slot, y = place_ref[0], place_ref[5]
    above, below = above_ref.shape[0], below_ref.shape[0]

    @pl.when(band == 0)
    def _():
        nat_ref[...] = jnp.zeros_like(nat_ref)

    for halves, ref in ((dqs, dq_ref), (dks, dk_ref), (dvs, dv_ref)):
        for i in range(2):
            at = pl.multiple_of((y ^ (1 - i)) * (D // 2), D // 2)
            ref[:, pl.ds(at, D // 2)] = halves[i][...]
    grad = mm_t(dk_ref[...], w_ref[:, D : 2 * D]) + mm_t(dv_ref[...], w_ref[:, 2 * D :])
    grad = grad.reshape(EXT, PITCH, D)
    direct = mm_t(dq_ref[...], w_ref[:, 0:D]).reshape(rows, PITCH, D)
    base = above - 2 * slot
    for b in range(SIDE):
        @pl.when(band == b)
        def _(b=b):
            at = slice(WIN * b, WIN * b + PITCH)
            nat_ref[pl.ds(base, EXT), at, :] = grad
            nat_ref[above : above + rows, at, :] += direct

    @pl.when(band == SIDE - 1)
    def _():
        above_ref[...] = nat_ref[0:above, 0:GRID, :].astype(BF)
        own_ref[...] = nat_ref[above : above + rows, 0:GRID, :]
        below_ref[...] = nat_ref[above + rows :, 0:GRID, :].astype(BF)


def project_back(place, dqs, dks, dvs, weight, rows, slots):
    above, below = 2 * (slots - 1), WIN - 2
    of_k = pl.BlockSpec((EXT * PITCH, D // 2), lambda b, s: (b, 0))
    of_q = pl.BlockSpec((rows * PITCH, D // 2), lambda b, s: (b, 0))
    shapes = [
        jax.ShapeDtypeStruct((above, GRID, D), BF),
        jax.ShapeDtypeStruct((rows, GRID, D), F32),
        jax.ShapeDtypeStruct((below, GRID, D), BF),
    ]
    return pl.pallas_call(
        partial(project_back_body, rows=rows),
        grid_spec=pltpu.PrefetchScalarGridSpec(
            num_scalar_prefetch=1,
            grid=(SIDE,),
            in_specs=[of_q, of_q, of_k, of_k, of_k, of_k, whole((D, 3 * D))],
            out_specs=[whole(s.shape) for s in shapes],
            scratch_shapes=[
                pltpu.VMEM((above + rows + below, GRID + PITCH, D), F32),
                pltpu.VMEM((rows * PITCH, D), BF),
                pltpu.VMEM((EXT * PITCH, D), BF),
                pltpu.VMEM((EXT * PITCH, D), BF),
            ],
        ),
        out_shape=shapes,
        compiler_params=pltpu.CompilerParams(vmem_limit_bytes=63 << 20),
        cost_estimate=guess(14),
        name="project_back",
    )(place, *dqs, *dks, *dvs, weight)


def head_lanes(shape, head):
    lane = lax.broadcasted_iota(jnp.int32, shape, 1)
    return lane < HD if head == 0 else lane >= HD


def early_window(slot, rows):
    return (WIN - 2 * slot) * PITCH - rows * PITCH // 2


def lanes_of(pair):
    return slice(128 * pair, 128 * pair + 128)


def attend_body(place_ref, q_ref, k_ref, v_ref, rel_ref, tab_ref, o_ref, p_ref, *, rows):
    slot = place_ref[0]
    half = rows * PITCH // 2
    lane = lax.broadcasted_iota(jnp.int32, (PITCH, 128), 1)
    first = lax.broadcasted_iota(jnp.int32, (1, half), 1) < early_window(slot, rows)
    turns = [lax.rem(2 * slot + r, WIN) for r in range(rows)]
    heads = [(pair, head) for pair in range(q_ref.shape[1] // 128) for head in range(2)]
    raws = [mm(q_ref[:, lanes_of(pair)], rel_ref[...]) for pair in range(len(heads) // 2)]

    def extended(pair, head):
        base = 64 - 64 * head
        one = jnp.where(lane == base, 1.0, 0.0)
        on_row = (lane >= base + 15) & (lane < base + 29)
        on_col = (lane >= base + 46) & (lane < base + 60)
        mine = head_lanes((PITCH, 128), head)
        parts = []
        for r in range(rows):
            here = raws[pair][r * PITCH : (r + 1) * PITCH, lanes_of(head)]
            along_row = pltpu.roll(here, turns[r], 1)
            along_col = pltpu.roll(here, 0, 1, stride=1, stride_axis=0)
            kept = jnp.where(mine, here, one)
            both = jnp.where(on_row, along_row, jnp.where(on_col, along_col, kept))
            high = both.astype(BF).astype(F32)
            parts.append((high + pltpu.roll(both - high, 114, 1)).astype(BF))
        return jnp.concatenate(parts, 0)

    def scored(pair, head, left):
        mine = head_lanes((KEYS, 128), head)
        keys_a = jnp.where(mine, k_ref[0:KEYS, lanes_of(pair)], tab_ref[head])
        keys_b = jnp.where(mine, k_ref[KEYS:, lanes_of(pair)], tab_ref[head])
        scores = mm_t(keys_a, left)
        return scores[:, :half], jnp.where(first, scores[:, half:], mm_t(keys_b, left[half:]))

    def softmax(pair, head, pieces):
        for i, piece in enumerate(pieces):
            grown = jnp.exp(piece - jnp.max(piece, 0, keepdims=True))
            probs = (grown * (1.0 / jnp.sum(grown, 0, keepdims=True))).astype(BF)
            p_ref[pair, head, :, i * half : (i + 1) * half] = probs

    def weighed(pair, head):
        rows_of = slice(HD * head, HD * head + HD)
        out = mm(v_ref[0:KEYS, lanes_of(pair)].T[rows_of], p_ref[pair, head])
        late = mm(v_ref[KEYS:, lanes_of(pair)].T[rows_of], p_ref[pair, head, :, half:])
        return jnp.concatenate([out[:, :half], jnp.where(first, out[:, half:], late)], 1)

    lefts = [extended(*h) for h in heads]
    scores = [scored(*h, left) for h, left in zip(heads, lefts)]
    for h, pieces in zip(heads, scores):
        softmax(*h, pieces)
    outs = [weighed(*h) for h in heads]
    for pair in range(len(heads) // 2):
        o_ref[:, lanes_of(pair)] = jnp.concatenate(outs[2 * pair : 2 * pair + 2], 0).T.astype(BF)


def attend(slot, q, k, v, rel, table, rows):
    queries = rows * PITCH
    many = PAIRS // 2
    of_k = pl.BlockSpec((EXT * PITCH, 128 * many), lambda b, p, s: (b, p))
    of_q = pl.BlockSpec((queries, 128 * many), lambda b, p, s: (b, p))
    return pl.pallas_call(
        partial(attend_body, rows=rows),
        grid_spec=pltpu.PrefetchScalarGridSpec(
            num_scalar_prefetch=1,
            grid=(SIDE, PAIRS // many),
            in_specs=[of_q, of_k, of_k, whole((128, 256)), whole((2, KEYS, 128))],
            out_specs=[
                of_q,
                pl.BlockSpec((many, 2, KEYS, queries), lambda b, p, s: (b * (PAIRS // many) + p, 0, 0, 0)),
            ],
        ),
        out_shape=[
            jax.ShapeDtypeStruct((SIDE * queries, D), BF),
            jax.ShapeDtypeStruct((SIDE * PAIRS, 2, KEYS, queries), BF),
        ],
        compiler_params=pltpu.CompilerParams(vmem_limit_bytes=63 << 20),
        cost_estimate=guess(24),
        name="attend",
    )(slot, q, k, v, rel, table)


def attend_back_body(
    place_ref, q_ref, k_ref, v_ref, p_ref, do_ref, rel_ref, tab_ref, dq_ref, dk_ref, dv_ref, drel_ref, *, rows,
):
    slot = place_ref[0]
    count = rows * PITCH
    half = count // 2
    early = early_window(slot, rows)

    @pl.when(pl.program_id(0) == 0)
    def _():
        drel_ref[...] = jnp.zeros_like(drel_ref)

    lane = lax.broadcasted_iota(jnp.int32, (PITCH, 128), 1)
    first = lax.broadcasted_iota(jnp.int32, (1, half), 1) < early
    turns = [lax.rem(2 * slot + r, WIN) for r in range(rows)]
    heads = [(pair, head) for pair in range(q_ref.shape[1] // 128) for head in range(2)]

    def split(value, head):
        spot = lax.broadcasted_iota(jnp.int32, (half, 128), 0)
        mine = head_lanes((half, 128), head)
        value = value.astype(F32)
        top = jnp.where(mine, value[:half], 0.0)
        mid = jnp.where(mine & (spot < early), value[half:], 0.0)
        low = jnp.where(mine & (spot >= early), value[half:], 0.0)
        return jnp.concatenate([top, mid], 0).astype(BF), low.astype(BF), (mid + low).astype(BF)

    def upstream(pair, head):
        return split(do_ref[:, lanes_of(pair)], head)

    def probs_grad(pair, head, out_a, late):
        whole_out = jnp.concatenate([out_a[:half], late], 0)
        grad = mm_t(v_ref[0:KEYS, lanes_of(pair)], whole_out)
        more = mm_t(v_ref[KEYS:, lanes_of(pair)], late)
        return grad[:, :half], jnp.where(first, grad[:, half:], more)

    def scores_grad(pair, head, pieces):
        grads = []
        for i, piece in enumerate(pieces):
            exact = p_ref[pair, head, :, i * half : (i + 1) * half].astype(F32)
            inner = jnp.sum(exact * piece, 0, keepdims=True)
            grads.append((exact * (piece - inner)).astype(BF))
        return jnp.concatenate(grads, 1)

    def left_grad(pair, head, grad, turned):
        spot = lax.broadcasted_iota(jnp.int32, (128, KEYS), 0)
        mine = spot < HD if head == 0 else spot >= HD
        left = mm(jnp.where(mine, turned[0], tab_ref[head]), grad)
        late = mm(jnp.where(mine, turned[1], tab_ref[head]), grad[:, half:])
        return jnp.concatenate([left[:, :half], jnp.where(first, left[:, half:], late)], 1).T

    def raw_grad(head, left):
        base = 64 - 64 * head
        on_row = (lane >= base) & (lane < base + WIN)
        on_col = (lane >= base + 32) & (lane < base + 32 + WIN)
        parts = []
        for r in range(rows):
            here = left[r * PITCH : (r + 1) * PITCH]
            along_row = pltpu.roll(jnp.where(on_row, here, 0.0), turns[r], 1)
            along_col = pltpu.roll(jnp.where(on_col, here, 0.0), 0, 1, stride=1, stride_axis=0)
            parts.append((along_row + along_col).astype(BF))
        return jnp.concatenate(parts, 0)

    outs = [upstream(*h) for h in heads]
    pieces = [probs_grad(*h, out[0], out[2]) for h, out in zip(heads, outs)]
    grads = [scores_grad(*h, piece) for h, piece in zip(heads, pieces)]
    lefts = []
    for pair in range(len(heads) // 2):
        turned = [k_ref[w * KEYS : (w + 1) * KEYS, lanes_of(pair)].T for w in range(2)]
        lefts += [left_grad(pair, head, grads[2 * pair + head], turned) for head in range(2)]
    for pair in range(len(heads) // 2):
        scaled = q_ref[:, lanes_of(pair)].astype(F32) * HD ** (-0.5)
        owns = [split(scaled, head) for head in range(2)]
        for w in range(2):
            at = (slice(w * KEYS, (w + 1) * KEYS), lanes_of(pair))
            part = slice(0, count) if w == 0 else slice(half, count)
            dv_ref[at] = sum(mm(p_ref[pair, h, :, part], outs[2 * pair + h][w]) for h in range(2)).astype(BF)
            dk_ref[at] = sum(mm(grads[2 * pair + h][:, part], owns[h][w]) for h in range(2)).astype(BF)
    for pair in range(len(heads) // 2):
        mine = lefts[2 * pair : 2 * pair + 2]
        raw = jnp.concatenate([raw_grad(head, mine[head]) for head in range(2)], 1)
        direct = jnp.where(head_lanes((count, 128), 0), *mine) * HD ** (-0.5)
        dq_ref[:, lanes_of(pair)] = (direct + mm(raw, rel_ref[...])).astype(BF)
        drel_ref[...] += t_mm(q_ref[:, lanes_of(pair)], raw)


def attend_back(slot, q, k, v, probs, grad_out, rel, table, rows, group):
    queries = rows * PITCH
    many = PAIRS // 2
    half = lambda s: s[5] ^ (1 - group)
    of_q = pl.BlockSpec((queries, 128 * many), lambda b, s: (b, half(s)))
    of_k = pl.BlockSpec((EXT * PITCH, 128 * many), lambda b, s: (b, half(s)))
    to_q = pl.BlockSpec((queries, 128 * many), lambda b, s: (b, 0))
    to_k = pl.BlockSpec((EXT * PITCH, 128 * many), lambda b, s: (b, 0))
    return pl.pallas_call(
        partial(attend_back_body, rows=rows),
        grid_spec=pltpu.PrefetchScalarGridSpec(
            num_scalar_prefetch=1,
            grid=(SIDE,),
            in_specs=[
                of_q, of_k, of_k,
                pl.BlockSpec((many, 2, KEYS, queries), lambda b, s: (b * 2 + half(s), 0, 0, 0)),
                of_q, whole((256, 128)), whole((2, 128, KEYS)),
            ],
            out_specs=[to_q, to_k, to_k, whole((128, 256))],
        ),
        out_shape=[
            jax.ShapeDtypeStruct((q.shape[0], D // 2), BF),
            jax.ShapeDtypeStruct((k.shape[0], D // 2), BF),
            jax.ShapeDtypeStruct((k.shape[0], D // 2), BF),
            jax.ShapeDtypeStruct((128, 256), F32),
        ],
        compiler_params=pltpu.CompilerParams(vmem_limit_bytes=63 << 20),
        cost_estimate=guess(16),
        name="attend_back",
    )(slot, q, k, v, probs, grad_out, rel, table)


def chunk_of(step, place):
    return (place[3] ^ (1 - step % 2)) * 2 + (place[4] ^ (1 - step // 2))


def feed_body(
    place_ref, o_ref, x_ref, g_ref, wo_ref, up_ref, down_ref, vec_ref, bias_ref,
    out_ref, dh_ref, do_ref, gas_ref, gak_ref, gbs_ref, gbk_ref, gvec_ref, gbias_ref,
    nat_ref, onat_ref, n2_ref, h_ref, y_ref, dn_ref, a_ref, du_ref, w_ref, *, rows,
):
    step = pl.program_id(0)
    steps = rows * GRID // 256
    lines = 256 // GRID
    width = D // 4

    @pl.when(step == 0)
    def _():
        for t in range(4):
            w_ref[:, t * width : (t + 1) * width] = wo_ref[:, t, :, 0:width].reshape(D, width)

        def one(i, carry):
            at = pl.ds(pl.multiple_of(i * 256, 256), 256)
            for b in range(SIDE):
                piece = o_ref[b, pl.ds(i * lines, lines)]
                nat_ref[:, WIN * b : WIN * b + PITCH, :] = piece.astype(F32)
            natural = nat_ref[:, 0:GRID, :].reshape(256, D).astype(BF)
            onat_ref[at, :] = natural
            hidden = x_ref[at, :].astype(F32) + mm_t(natural, w_ref[...]) + vec_ref[0:1]
            h_ref[at, :] = hidden
            hat, _ = norm_parts(hidden)
            n2_ref[at, :] = (hat * vec_ref[1:2] + vec_ref[2:3]).astype(BF)
            y_ref[at, :] = jnp.zeros((256, D), F32)
            dn_ref[at, :] = jnp.zeros((256, D), F32)
            return carry

        lax.fori_loop(0, steps, one, 0)

    up = up_ref[...].reshape(D, D)
    down = down_ref[...].reshape(D, D)

    def two(i, total):
        at = pl.ds(pl.multiple_of(i * 256, 256), 256)
        upper = mm(n2_ref[at, :], up) + bias_ref[...].reshape(1, D)
        cdf = 0.5 * (1.0 + lax.erf(upper * (1.0 / math.sqrt(2.0))))
        active = (upper * cdf).astype(BF)
        a_ref[at, :] = active
        y_ref[at, :] += mm_t(active, down)
        slope = cdf + upper * jnp.exp(-0.5 * upper * upper) * (1.0 / math.sqrt(2.0 * math.pi))
        delta = (mm(g_ref[at, :], down) * slope).astype(BF)
        du_ref[at, :] = delta
        dn_ref[at, :] += mm_t(delta, up)
        return total + jnp.sum(delta.astype(F32), 0, keepdims=True)

    total = lax.fori_loop(0, steps, two, jnp.zeros((1, D), F32))
    gbias_ref[...] = total.reshape(gbias_ref.shape)
    grad_up = t_mm(n2_ref[...], du_ref[...]).astype(BF)
    grad_down = t_mm(g_ref[...], a_ref[...]).astype(BF)

    other_chip = 1 - step % 2

    @pl.when(step < 2)
    def _():
        store_shards(place_ref, gas_ref.at[other_chip], grad_up)
        store_shards(place_ref, gbs_ref.at[other_chip], grad_down)

    @pl.when(step >= 2)
    def _():
        store_shards(place_ref, gak_ref.at[other_chip], grad_up)
        store_shards(place_ref, gbk_ref.at[other_chip], grad_down)

    @pl.when(step == pl.num_programs(0) - 1)
    def _():
        nat_ref[...] = jnp.zeros_like(nat_ref)
        gvec_ref[...] = jnp.zeros_like(gvec_ref)

        def three(i, carry):
            at = pl.ds(pl.multiple_of(i * 256, 256), 256)
            hidden = h_ref[at, :]
            grad = g_ref[at, :].astype(F32)
            hat, inverse = norm_parts(hidden)
            grad_normed = dn_ref[at, :]
            out_ref[at, :] = (hidden + y_ref[at, :] + vec_ref[3:4]).astype(BF)
            grad_hidden = grad + norm_back(grad_normed, hat, inverse, vec_ref[1:2])
            dh_ref[at, :] = grad_hidden
            branch = grad_hidden.astype(BF)
            n2_ref[at, :] = branch
            gvec_ref[0:1] += jnp.sum(grad_normed * hat, 0, keepdims=True)
            gvec_ref[1:2] += jnp.sum(grad_normed, 0, keepdims=True)
            gvec_ref[2:3] += jnp.sum(branch.astype(F32), 0, keepdims=True)
            gvec_ref[3:4] += jnp.sum(grad, 0, keepdims=True)
            grad_out = mm(branch, w_ref[...])
            nat_ref[:, 0:GRID, :] = grad_out.reshape(lines, GRID, D)
            keep = lax.broadcasted_iota(jnp.int32, (lines, PITCH, D), 1) < WIN
            for b in range(SIDE):
                piece = nat_ref[:, WIN * b : WIN * b + PITCH, :]
                do_ref[b, pl.ds(i * lines, lines)] = jnp.where(keep, piece, 0.0).astype(BF)
            return carry

        lax.fori_loop(0, steps, three, 0)
        grad_wo = t_mm(n2_ref[...], onat_ref[...]).astype(BF)
        for sibling, ref in ((1, gas_ref), (0, gak_ref)):
            for t in range(4):
                @pl.when(place_ref[4] ^ (t % 2) == sibling)
                def _(t=t, ref=ref):
                    store_shards(
                        place_ref, ref.at[place_ref[3] ^ (t // 2)], grad_wo[:, t * width : (t + 1) * width], lane=D
                    )


def feed(place, o, x, g, rest, vectors, up_bias, rows, shards):
    tokens = rows * GRID
    blocks, chunks, depth = rest.shape[:3]
    width = D // chunks
    slab = lambda column: pl.BlockSpec(
        (blocks, None, depth, D), lambda s, p: (0, chunk_of(s, p), 0, column)
    )
    line = pl.BlockSpec((None, 1, D), lambda s, p: (chunk_of(s, p), 0, 0))
    grid = (SIDE, rows, PITCH, D)
    first = jax.ShapeDtypeStruct((*shards, D + width), BF)
    second = jax.ShapeDtypeStruct((*shards, D), BF)
    shapes = [
        jax.ShapeDtypeStruct((tokens, D), BF),
        jax.ShapeDtypeStruct((tokens, D), F32),
        jax.ShapeDtypeStruct(grid, BF),
        first, first, second, second,
        jax.ShapeDtypeStruct((8, D), F32),
        jax.ShapeDtypeStruct((chunks, 1, D), F32),
    ]
    specs = [whole(s.shape) for s in shapes]
    specs[8] = line
    return pl.pallas_call(
        partial(feed_body, rows=rows),
        grid_spec=pltpu.PrefetchScalarGridSpec(
            num_scalar_prefetch=1,
            grid=(chunks,),
            in_specs=[
                whole(grid), whole((tokens, D)), whole((tokens, D)),
                pl.BlockSpec((blocks, chunks, depth, 256), lambda s, p: (0, 0, 0, 2 * D // 256), pipeline_mode=pl.Buffered(1)),
                slab(0), slab(1), whole((8, D)), line,
            ],
            out_specs=specs,
            scratch_shapes=[
                pltpu.VMEM((256 // GRID, GRID + PITCH, D), F32),
                pltpu.VMEM((tokens, D), BF),
                pltpu.VMEM((tokens, D), BF),
                pltpu.VMEM((tokens, D), F32),
                pltpu.VMEM((tokens, D), F32),
                pltpu.VMEM((tokens, D), F32),
                pltpu.VMEM((tokens, D), BF),
                pltpu.VMEM((tokens, D), BF),
                pltpu.VMEM((D, D), BF),
            ],
        ),
        out_shape=shapes,
        compiler_params=pltpu.CompilerParams(vmem_limit_bytes=63 << 20),
        cost_estimate=guess(55),
        name="feed",
    )(place, o, x, g, rest, rest, rest, vectors, up_bias)


def finish_body(own_ref, head_ref, tail_ref, x_ref, dh_ref, vec_ref, out_ref, sum_ref):
    rows, below, above = own_ref.shape[0], head_ref.shape[0], tail_ref.shape[0]
    sum_ref[...] = jnp.zeros_like(sum_ref)

    def line(i, low, high):
        grad = own_ref[i]
        if low:
            grad = grad + head_ref[i].astype(F32)
        if high:
            grad = grad + tail_ref[i - (rows - above)].astype(F32)
        hat, inverse = norm_parts(x_ref[i].astype(F32))
        out_ref[i] = (dh_ref[i] + norm_back(grad, hat, inverse, vec_ref[0:1])).astype(BF)
        sum_ref[0:1] += jnp.sum(grad * hat, 0, keepdims=True)
        sum_ref[1:2] += jnp.sum(grad, 0, keepdims=True)

    def over(start, stop, low, high):
        lax.fori_loop(start, stop, lambda i, carry: (line(i, low, high), carry)[1], 0)

    over(0, rows - above, True, False)
    over(rows - above, below, True, True)
    over(below, rows, False, True)


def finish(own, head, tail, x, dh, vectors):
    shapes = [jax.ShapeDtypeStruct(own.shape, BF), jax.ShapeDtypeStruct((8, D), F32)]
    return pl.pallas_call(
        finish_body,
        grid=(1,),
        in_specs=[whole(v.shape) for v in (own, head, tail, x, dh, vectors)],
        out_specs=[whole(v.shape) for v in shapes],
        out_shape=shapes,
        compiler_params=pltpu.CompilerParams(vmem_limit_bytes=63 << 20),
        cost_estimate=guess(5),
        name="finish",
    )(own, head, tail, x, dh, vectors)


def fold_body(*refs, plan):
    terms = sum(count for count, *_ in plan)
    ins, outs = refs[:terms], refs[terms:]
    for (count, axis, index), out in zip(plan, outs):
        here, ins = ins[:count], ins[count:]
        lead = out.shape[:-2]
        for at in np.ndindex(*lead):
            spot = at if axis is None else at[:axis] + (index,) + at[axis:]
            total = here[0][spot].astype(F32)
            for ref in here[1:]:
                total = total + ref[spot].astype(F32)
            out[at] = total.astype(out.dtype)


def fold(*results):
    count = None
    args, in_specs, out_specs, shapes, plan = [], [], [], [], []
    for terms, z_axis, axis, index in results:
        shape = terms[0].shape
        count = shape[z_axis]
        block = tuple(None if i == z_axis else n for i, n in enumerate(shape))
        spec = pl.BlockSpec(block, lambda i, z_axis=z_axis, n=len(shape): tuple(i if k == z_axis else 0 for k in range(n)))
        args += terms
        in_specs += [spec] * len(terms)
        left = [n for i, n in enumerate(shape) if i != axis]
        z_left = z_axis if axis is None or axis > z_axis else z_axis - 1
        block = tuple(None if i == z_left else n for i, n in enumerate(left))
        out_specs.append(
            pl.BlockSpec(block, lambda i, z_left=z_left, n=len(left): tuple(i if k == z_left else 0 for k in range(n)))
        )
        shapes.append(jax.ShapeDtypeStruct(tuple(left), BF))
        inner = None if axis is None else (axis if axis < z_axis else axis - 1)
        plan.append((len(terms), inner, index))
    size = sum(2 * int(np.prod(a.shape)) for a in args)
    return pl.pallas_call(
        partial(fold_body, plan=plan),
        grid=(count,),
        in_specs=in_specs,
        out_specs=out_specs,
        out_shape=shapes,
        compiler_params=pltpu.CompilerParams(vmem_limit_bytes=63 << 20),
        cost_estimate=guess(1 + size / 2e6),
        name="fold",
    )(*args)


AXES = ("z", "x", "y", "c")
SWAP = [(0, 1), (1, 0)]


def swap(value, axis):
    return lax.ppermute(value, axis, SWAP)


def shift(value, count, by):
    return lax.ppermute(value, "z", [(i, (i + by) % count) for i in range(count)])


def gather_lines(shard, count):
    half = shard.shape[0] // 2
    lines = [shard] + [shift(shard, count, k) for k in range(1, count)]
    first = jnp.stack([line[:half] for line in lines])
    second = jnp.stack([line[half:] for line in lines])
    return jnp.stack([first, swap(first, "x")]), jnp.stack([second, swap(second, "y")])


def gather_planes(first, second):
    first = jnp.stack([first, swap(first, "y")])
    second = jnp.stack([second, swap(second, "x")])
    return first, second, swap(first, "c"), swap(second, "c")


def along_z(pieces):
    count = pieces.shape[0]
    total = pieces[0].astype(F32)
    for k in range(1, count):
        total = total + shift(pieces[k], count, k).astype(F32)
    return total


def sum_all(value, count, fast):
    for axis in ("c", "y", "x"):
        value = value + swap(value, axis)
    if not fast:
        return lax.psum(value, "z")
    step = 1
    while step < count:
        value = value + lax.ppermute(value, "z", [(i, i ^ step) for i in range(count)])
        step *= 2
    return value


def body(
    features, first_gain, first_shift, qkv_weight, qv_bias, rel_height, rel_width, output_weight,
    output_bias, second_gain, second_shift, up_weight, up_bias, down_weight, down_bias, cotangent,
    *, count,
):
    depth, _, width = qkv_weight.shape
    hidden = up_weight.shape[1]
    tokens = features.shape[0]
    rows = tokens // GRID
    slots = 4
    fast = count <= 4 and depth % 32 == 0
    z, x, y, c = (lax.axis_index(a).astype(jnp.int32) for a in AXES)
    slot = 2 * y + c
    nought = jnp.zeros((), jnp.int32)
    place = jnp.stack([slot, z, x, y, c, y] if fast else [slot] + [nought] * 4 + [y])
    shards = (2, count, 2, depth)
    above, below = 2 * (slots - 1), WIN - 2

    grid_x = features.reshape(rows, GRID, D)
    pair = ("y", "c")
    up_pairs = [(s, s + 1) for s in range(slots - 1)]
    down_pairs = [(s + 1, s) for s in range(slots - 1)]
    from_above = lax.ppermute(grid_x[rows - above :], pair, up_pairs)
    from_below = lax.ppermute(grid_x[:below], pair, down_pairs)

    rest = jnp.concatenate([up_weight, down_weight, output_weight, jnp.zeros((depth, 256 - width), BF)], 1)
    rest_all = lax.all_gather(rest, AXES, axis=0).reshape(2 * count, slots, depth, 2 * hidden + 256)
    biases = jnp.concatenate([qv_bias.reshape(-1), up_bias])
    biases = jnp.where(jnp.arange(slots)[:, None] == slot, biases[None], jnp.zeros((), BF))
    biases = biases + swap(biases, "c")
    biases = (biases + swap(biases, "y")).astype(F32)
    qv_all = biases[:, : 2 * width].reshape(slots, 2, width).transpose(1, 0, 2).reshape(2, D)
    up_bias_all = biases[:, 2 * width :].reshape(slots, 1, hidden)

    vec_one = jnp.concatenate([first_gain[None], first_shift[None], jnp.zeros((6, D), BF)], 0).astype(F32)
    normed = windows(place, from_above, grid_x, from_below, vec_one)
    if fast:
        lines = gather_lines(qkv_weight.reshape(depth, 3 * width), count)
        normed, *lines = lax.optimization_barrier((normed, *lines))
        pieces = gather_planes(*lines)
    else:
        full = lax.all_gather(qkv_weight, AXES, axis=0).reshape(2 * count, slots, depth, 3, width)
        pieces = [full.transpose(0, 2, 3, 1, 4).reshape(D, 3 * D)]
    q, k, v, weight = project(place, normed, pieces, qv_all, rows, depth)
    ahead, back = score_tables()
    rel_ahead, rel_back = offset_tables(rel_height, rel_width)
    attended, probs = attend(place, q, k, v, rel_ahead.T, jnp.asarray(ahead, BF), rows)

    vec_two = jnp.concatenate(
        [output_bias[None], second_gain[None], second_shift[None], down_bias[None], jnp.zeros((4, D), BF)], 0
    ).astype(F32)
    (
        output, grad_hidden, grad_out, a_send, a_keep, b_send, b_keep, grad_vec, grad_up_bias,
    ) = feed(
        place, attended.reshape(SIDE, rows, PITCH, D), features, cotangent, rest_all, vec_two, up_bias_all,
        rows, shards,
    )
    grad_windows = grad_out.reshape(-1, D)
    table = jnp.asarray(back.transpose(0, 2, 1), BF)
    if fast:
        a_got, b_got = swap(a_send, "c"), swap(b_send, "c")
    *half0, drel0 = attend_back(place, q, k, v, probs, grad_windows, rel_back, table, rows, 0)
    if fast:
        a, b = [a_keep, a_got], [b_keep, b_got]
        a_away, a_here, b_away, b_here = fold((a, 1, 0, 1), (a, 1, 0, 0), (b, 1, 2, 1), (b, 1, 2, 0))
        place, a_away, b_away = lax.optimization_barrier((place, a_away, b_away))
        a_got, b_got = swap(a_away, "y"), swap(b_away, "x")
    first_send, first_keep, first_bias = project_grad(place, normed, *half0, rows, shards)
    if fast:
        first_got = swap(first_send, "c")
    *half1, drel1 = attend_back(place, q, k, v, probs, grad_windows, rel_back, table, rows, 1)
    if fast:
        a, b = [a_here, a_got], [b_here, b_got]
        a_away, a_here, b_away, b_here, crossing = fold(
            (a, 0, 1, 1), (a, 0, 1, 0), (b, 1, 0, 1), (b, 1, 0, 0), ([first_keep, first_got], 0, None, None)
        )
        place, a_away, b_away, crossing = lax.optimization_barrier((place, a_away, b_away, crossing))
        a_got, b_got, crossing = swap(a_away, "x"), swap(b_away, "y"), swap(crossing, "y")
    dqs, dks, dvs = zip(half0, half1)
    to_above, total, to_below = project_back(place, dqs, dks, dvs, weight, rows, slots)
    from_below = lax.ppermute(to_above, pair, down_pairs)
    from_above = lax.ppermute(to_below, pair, up_pairs)
    place, to_above = lax.optimization_barrier((place, to_above))
    last_send, last_keep, last_bias = project_grad(place, normed, *half1, rows, shards)
    if fast:
        last_got = swap(last_send, "c")
        a, b = fold(([a_here, a_got], 0, None, None), ([b_here, b_got], 0, None, None))
        a, b = along_z(a), along_z(b)
        grad_up, grad_wo, grad_down = a[:, :hidden], a[:, hidden:], b
    grad_features, sums_one = finish(
        total, from_above, from_below, grid_x, grad_hidden.reshape(rows, GRID, D), vec_one
    )
    if fast:
        last = [last_keep, last_got, crossing]
        away, here = fold((last, 0, 1, 1), (last, 0, 1, 0))
        (last,) = fold(([here, swap(away, "x")], 0, None, None))
        grad_qkv = along_z(last)
    else:
        pairs = [
            (a_send, a_keep), (b_send, b_keep),
            [
                jnp.where(y == 0, jnp.stack([last, first]), jnp.stack([first, last]))
                for first, last in ((first_send, last_send), (first_keep, last_keep))
            ],
        ]
        a, grad_down, grad_qkv = [
            lax.psum_scatter(
                jnp.stack([keep, send], 3).transpose(1, 2, 0, 3, 4, 5).reshape(8 * count, depth, -1),
                AXES, scatter_dimension=0,
            ).astype(F32)
            for send, keep in pairs
        ]
        grad_up, grad_wo = a[:, :hidden], a[:, hidden:]
    drel = (drel0 + drel1).T.reshape(4, 64, 128)
    drel = drel[1, :, :HD] + drel[2, :, HD:]
    grad_qv = jnp.where(y == 0, jnp.concatenate([last_bias, first_bias], 1), jnp.concatenate([first_bias, last_bias], 1))
    small = jnp.concatenate(
        [grad_vec[:4], grad_up_bias.reshape(slots, hidden), sums_one[:2], grad_qv], 0
    )
    small = sum_all(jnp.concatenate([small.reshape(-1), drel.reshape(-1)]).reshape(-1, 512), count, fast).reshape(-1)
    vec = small[: 12 * D].reshape(12, D)
    drel = small[12 * D :].reshape(64, HD)
    qv = lax.dynamic_index_in_dim(vec[10:12].reshape(2, slots, width), slot, 1, keepdims=False)
    bias = lax.dynamic_index_in_dim(vec[4:8], slot, 0, keepdims=False)
    return (
        output,
        grad_features.reshape(tokens, D),
        vec[8],
        vec[9],
        grad_qkv.reshape(depth, 3, width),
        qv,
        drel[0:OFFS],
        drel[32 : 32 + OFFS],
        grad_wo,
        vec[2],
        vec[0],
        vec[1],
        grad_up,
        bias,
        grad_down,
        vec[3],
    )


def solution(mesh):
    token = P(AXES, None)
    square = P(("z", "x"), ("y", "c"))
    cube = P(("z", "x"), None, ("y", "c"))
    lane = P(("y", "c"))
    count = mesh.shape["dp"] // 2
    assert mesh.shape["tensor"] == 4
    return jax.shard_map(
        partial(body, count=count),
        mesh=jax.sharding.Mesh(mesh.devices.reshape(count, 2, 2, 2), AXES),
        in_specs=(
            token, P(), P(), cube, P(None, ("y", "c")), P(), P(), square, P(), P(), P(), square,
            lane, square, P(), token,
        ),
        out_specs=(
            token, token, P(), P(), cube, P(None, ("y", "c")), P(), P(), square, P(), P(), P(), square,
            lane, square, P(),
        ),
        check_vma=False,
    )
```

```python
from functools import partial
import math

import jax
import jax.numpy as jnp
from jax import lax
from jax.experimental import pallas as pl
from jax.experimental.pallas import tpu as pltpu
from jax.sharding import PartitionSpec as P
import numpy as np

D = 768
HD = 64
GRID = 64
WIN = 14
SIDE = 5
PITCH = 16
KEYS = WIN * PITCH
EXT = 2 * WIN
PAIRS = D // (2 * HD)
OFFS = 2 * WIN - 1
EPSILON = 1e-06
FAR = -1e30
BF = jnp.bfloat16
F32 = jnp.float32
HIGH = lax.Precision.HIGHEST


def mm(left, right):
    return jnp.dot(left, right, preferred_element_type=F32)


def mm_t(left, right):
    return lax.dot_general(left, right, (((1,), (1,)), ((), ())), preferred_element_type=F32)


def t_mm(left, right):
    return lax.dot_general(left, right, (((0,), (0,)), ((), ())), preferred_element_type=F32)


def norm_parts(value):
    centered = value - jnp.mean(value, -1, keepdims=True)
    inverse = lax.rsqrt(jnp.mean(centered * centered, -1, keepdims=True) + EPSILON)
    return centered * inverse, inverse


def norm_back(upstream, hat, inverse, gain):
    scaled = upstream * gain
    return inverse * (
        scaled
        - jnp.mean(scaled, -1, keepdims=True)
        - hat * jnp.mean(scaled * hat, -1, keepdims=True)
    )


def score_tables():
    ahead = np.zeros((2, KEYS, 128), np.float32)
    back = np.zeros((2, KEYS, 128), np.float32)
    for head in range(2):
        base = 64 - 64 * head
        for c in range(WIN):
            for e in range(PITCH):
                k = c * PITCH + e
                if e >= WIN:
                    ahead[head, k, base] = FAR
                    continue
                ahead[head, k, base + 15 + c] = 1
                ahead[head, k, base + 1 + c] = 1
                ahead[head, k, base + 46 + e] = 1
                ahead[head, k, base + 32 + e] = 1
                back[head, k, base + WIN - 1 - c] = 1
                back[head, k, base + 32 + WIN - 1 - e] = 1
    return ahead, back


def offset_tables(rel_height, rel_width):
    def place(first, second, at_rows, at_cols):
        slab = jnp.zeros((64, HD), BF)
        slab = slab.at[at_rows : at_rows + OFFS].set(first)
        slab = slab.at[at_cols : at_cols + OFFS].set(second)
        low = jnp.concatenate([slab, jnp.zeros_like(slab)], 1)
        high = jnp.concatenate([jnp.zeros_like(slab), slab], 1)
        return jnp.concatenate([jnp.zeros_like(low), low, high, jnp.zeros_like(high)], 0)

    through = jnp.eye(HD, dtype=BF) * BF(HD ** (-0.5))
    nothing = jnp.zeros_like(through)
    through = jnp.concatenate(
        [jnp.concatenate([through, nothing], 1), jnp.zeros((128, 128), BF), jnp.concatenate([nothing, through], 1)], 0
    )
    return (
        place(rel_height[::-1], rel_width[::-1], 2, 33) + through,
        place(rel_height, rel_width, 0, 32),
    )


def whole(shape):
    return pl.BlockSpec(shape, lambda *_: (0,) * len(shape), pipeline_mode=pl.Buffered(1))


def windows_body(place_ref, above_ref, x_ref, below_ref, vec_ref, nw_ref, nat_ref, *, rows):
    band = pl.program_id(0)
    slot = place_ref[0]
    above, below = above_ref.shape[0], below_ref.shape[0]

    @pl.when(band == 0)
    def _():
        def normed(piece):
            hat, _ = norm_parts(piece.astype(F32))
            return hat * vec_ref[0:1] + vec_ref[1:2]

        def clear(i, carry):
            nat_ref[i, GRID : GRID + PITCH, :] = jnp.zeros((PITCH, D), F32)
            return carry

        def own(i, carry):
            nat_ref[2 * slot + i, 0:GRID, :] = normed(x_ref[i])
            return carry

        def before(i, carry):
            nat_ref[i, 0:GRID, :] = normed(above_ref[above - 2 * slot + i])
            return carry

        def after(i, carry):
            at = 2 * slot + rows + i
            inside = WIN * slot + at < GRID
            nat_ref[at, 0:GRID, :] = jnp.where(inside, normed(below_ref[i]), 0.0)
            return carry

        lax.fori_loop(0, EXT, clear, 0)
        lax.fori_loop(0, rows, own, 0)
        lax.fori_loop(0, 2 * slot, before, 0)
        lax.fori_loop(0, EXT - rows - 2 * slot, after, 0)

    keep = lax.broadcasted_iota(jnp.int32, (PITCH, D), 0) < WIN
    for b in range(SIDE):
        @pl.when(band == b)
        def _(b=b):
            def one(i, carry):
                piece = nat_ref[i, WIN * b : WIN * b + PITCH, :]
                start = pl.multiple_of(i * PITCH, PITCH)
                nw_ref[pl.ds(start, PITCH), :] = jnp.where(keep, piece, 0.0).astype(BF)
                return carry

            lax.fori_loop(0, EXT, one, 0)


def windows(place, above, x, below, vectors):
    rows = x.shape[0]
    return pl.pallas_call(
        partial(windows_body, rows=rows),
        grid_spec=pltpu.PrefetchScalarGridSpec(
            num_scalar_prefetch=1,
            grid=(SIDE,),
            in_specs=[whole(above.shape), whole(x.shape), whole(below.shape), whole((8, D))],
            out_specs=pl.BlockSpec((EXT * PITCH, D), lambda b, s: (b, 0)),
            scratch_shapes=[pltpu.VMEM((EXT, GRID + PITCH, D), F32)],
        ),
        out_shape=jax.ShapeDtypeStruct((SIDE * EXT * PITCH, D), BF),
        compiler_params=pltpu.CompilerParams(vmem_limit_bytes=63 << 20),
        cost_estimate=guess(8),
        name="windows",
    )(place, above, x, below, vectors)


def project_body(place_ref, nw_ref, *refs, rows, depth):
    *pieces, bias_ref, q_ref, k_ref, v_ref, w_ref, stage_ref = refs
    slot, z, x, y, c = (place_ref[i] for i in range(5))
    width = D // 4

    @pl.when(pl.program_id(0) == 0)
    def _():
        if len(pieces) == 1:
            w_ref[...] = pieces[0][...]
            return
        half = depth // 2
        for sibling in range(2):
            for part in range(2):
                ref = pieces[2 * sibling + part]
                count = ref.shape[2]
                for first in range(2):
                    for second in range(2):
                        dy, dx = (first, second) if part == 0 else (second, first)
                        from_slot = (y ^ dy) * 2 + (c ^ sibling)
                        for dz in range(count):
                            group = lax.rem(z - dz + count, count) * 2 + (x ^ dx)
                            at = pl.multiple_of(group * depth + part * half, half)
                            stage_ref[from_slot, pl.ds(at, half), :] = ref[first, second, dz]

        def join(i, carry):
            at = pl.ds(pl.multiple_of(i * 64, 64), 64)
            for kind in range(3):
                w_ref[at, kind * D : (kind + 1) * D] = jnp.concatenate(
                    [stage_ref[t, at, kind * width : (kind + 1) * width] for t in range(4)], 1
                )
            return carry

        lax.fori_loop(0, D // 64, join, 0)

    normed = nw_ref[...]
    own = nw_ref[pl.ds(pl.multiple_of(slot * 2 * PITCH, 2 * PITCH), rows * PITCH), :]
    q_ref[...] = (mm(own, w_ref[:, 0:D]) + bias_ref[0:1]).astype(BF)
    k_ref[...] = mm(normed, w_ref[:, D : 2 * D]).astype(BF)
    v_ref[...] = (mm(normed, w_ref[:, 2 * D :]) + bias_ref[1:2]).astype(BF)


def guess(us):
    return pl.CostEstimate(flops=int(us * 1.1e9), bytes_accessed=int(us * 3e6), transcendentals=0)


def project(place, normed, pieces, bias, rows, depth):
    of_k = pl.BlockSpec((EXT * PITCH, D), lambda b, s: (b, 0))
    of_q = pl.BlockSpec((rows * PITCH, D), lambda b, s: (b, 0))
    keys = jax.ShapeDtypeStruct((SIDE * EXT * PITCH, D), BF)
    return pl.pallas_call(
        partial(project_body, rows=rows, depth=depth),
        grid_spec=pltpu.PrefetchScalarGridSpec(
            num_scalar_prefetch=1,
            grid=(SIDE,),
            in_specs=[of_k] + [whole(p.shape) for p in pieces] + [whole((2, D))],
            out_specs=[of_q, of_k, of_k, whole((D, 3 * D))],
            scratch_shapes=[pltpu.VMEM((4, D, 3 * D // 4), BF)],
        ),
        out_shape=[
            jax.ShapeDtypeStruct((SIDE * rows * PITCH, D), BF), keys, keys,
            jax.ShapeDtypeStruct((D, 3 * D), BF),
        ],
        compiler_params=pltpu.CompilerParams(vmem_limit_bytes=63 << 20),
        cost_estimate=guess(18),
        name="project",
    )(place, normed, *pieces, bias)


def store_shards(place_ref, refs, value, first=0):
    z, x = place_ref[1], place_ref[2]
    count, _, depth = refs.shape[:3]
    if depth % 32:
        refs[...] = value.reshape(refs.shape)
        return
    for zd in range(value.shape[0] // (2 * depth)):
        for xd in range(2):
            start = (zd * 2 + xd) * depth
            refs[lax.rem(first + zd - z + count, count), x ^ xd] = value[start : start + depth]


def project_grad_body(place_ref, nw_ref, dq_ref, dk_ref, dv_ref, send_ref, keep_ref, bias_ref, *, rows, parts):
    step = pl.program_id(0)
    slot, c = place_ref[0], place_ref[4]
    width = D // 4
    lines = rows * PITCH

    @pl.when(step == 0)
    def _():
        bias_ref[0:1] = jnp.sum(dq_ref[...].astype(F32), 0, keepdims=True)
        bias_ref[1:2] = jnp.sum(dv_ref[...].astype(F32), 0, keepdims=True)

    grad_q = None
    for b in range(SIDE):
        start = pl.multiple_of(b * EXT * PITCH + slot * 2 * PITCH, 2 * PITCH)
        term = t_mm(nw_ref[pl.ds(start, lines), :], dq_ref[b * lines : (b + 1) * lines])
        grad_q = term if grad_q is None else grad_q + term
    grads = [grad_q.astype(BF)] + [t_mm(nw_ref[...], ref[...]).astype(BF) for ref in (dk_ref, dv_ref)]
    first = step * (keep_ref.shape[0] // parts)
    for core in range(2):
        value = jnp.concatenate([g[:, core * width : (core + 1) * width] for g in grads], 1)
        for sibling, ref in ((1, send_ref), (0, keep_ref)):
            @pl.when(c ^ core == sibling)
            def _(ref=ref, value=value):
                store_shards(place_ref, ref, value, first)


def project_grad(place, normed, dq, dk, dv, rows, shards):
    count, depth = shards[1], shards[3]
    parts = 2 if depth % 32 == 0 else 1
    out = jax.ShapeDtypeStruct((count, 2, depth, 3 * D // 4), BF)
    return pl.pallas_call(
        partial(project_grad_body, rows=rows, parts=parts),
        grid_spec=pltpu.PrefetchScalarGridSpec(
            num_scalar_prefetch=1,
            grid=(parts,),
            in_specs=[
                pl.BlockSpec((normed.shape[0], D // parts), lambda i, s: (0, i)),
                whole(dq.shape), whole(dk.shape), whole(dv.shape),
            ],
            out_specs=[whole(out.shape), whole(out.shape), whole((2, D // 2))],
        ),
        out_shape=[out, out, jax.ShapeDtypeStruct((2, D // 2), F32)],
        compiler_params=pltpu.CompilerParams(vmem_limit_bytes=63 << 20),
        cost_estimate=guess(6),
        name="project_grad",
    )(place, normed, dq, dk, dv)


def project_back_body(place_ref, *refs, rows):
    dqs, dks, dvs = refs[0:2], refs[2:4], refs[4:6]
    w_ref, above_ref, own_ref, below_ref, nat_ref, dq_ref, dk_ref, dv_ref = refs[6:]
    band = pl.program_id(0)
    slot, y = place_ref[0], place_ref[5]
    above, below = above_ref.shape[0], below_ref.shape[0]

    @pl.when(band == 0)
    def _():
        nat_ref[...] = jnp.zeros_like(nat_ref)

    for halves, ref in ((dqs, dq_ref), (dks, dk_ref), (dvs, dv_ref)):
        for i in range(2):
            at = pl.multiple_of((y ^ (1 - i)) * (D // 2), D // 2)
            ref[:, pl.ds(at, D // 2)] = halves[i][...]
    grad = mm_t(dk_ref[...], w_ref[:, D : 2 * D]) + mm_t(dv_ref[...], w_ref[:, 2 * D :])
    grad = grad.reshape(EXT, PITCH, D)
    direct = mm_t(dq_ref[...], w_ref[:, 0:D]).reshape(rows, PITCH, D)
    base = above - 2 * slot
    for b in range(SIDE):
        @pl.when(band == b)
        def _(b=b):
            at = slice(WIN * b, WIN * b + PITCH)
            nat_ref[pl.ds(base, EXT), at, :] = grad
            nat_ref[above : above + rows, at, :] += direct

    @pl.when(band == SIDE - 1)
    def _():
        above_ref[...] = nat_ref[0:above, 0:GRID, :].astype(BF)
        own_ref[...] = nat_ref[above : above + rows, 0:GRID, :]
        below_ref[...] = nat_ref[above + rows :, 0:GRID, :].astype(BF)


def project_back(place, dqs, dks, dvs, weight, rows, slots):
    above, below = 2 * (slots - 1), WIN - 2
    of_k = pl.BlockSpec((EXT * PITCH, D // 2), lambda b, s: (b, 0))
    of_q = pl.BlockSpec((rows * PITCH, D // 2), lambda b, s: (b, 0))
    shapes = [
        jax.ShapeDtypeStruct((above, GRID, D), BF),
        jax.ShapeDtypeStruct((rows, GRID, D), F32),
        jax.ShapeDtypeStruct((below, GRID, D), BF),
    ]
    return pl.pallas_call(
        partial(project_back_body, rows=rows),
        grid_spec=pltpu.PrefetchScalarGridSpec(
            num_scalar_prefetch=1,
            grid=(SIDE,),
            in_specs=[of_q, of_q, of_k, of_k, of_k, of_k, whole((D, 3 * D))],
            out_specs=[whole(s.shape) for s in shapes],
            scratch_shapes=[
                pltpu.VMEM((above + rows + below, GRID + PITCH, D), F32),
                pltpu.VMEM((rows * PITCH, D), BF),
                pltpu.VMEM((EXT * PITCH, D), BF),
                pltpu.VMEM((EXT * PITCH, D), BF),
            ],
        ),
        out_shape=shapes,
        compiler_params=pltpu.CompilerParams(vmem_limit_bytes=63 << 20),
        cost_estimate=guess(14),
        name="project_back",
    )(place, *dqs, *dks, *dvs, weight)


def head_lanes(shape, head):
    lane = lax.broadcasted_iota(jnp.int32, shape, 1)
    return lane < HD if head == 0 else lane >= HD


def early_window(slot, rows):
    return (WIN - 2 * slot) * PITCH - rows * PITCH // 2


def lanes_of(pair):
    return slice(128 * pair, 128 * pair + 128)


def attend_body(place_ref, q_ref, k_ref, v_ref, rel_ref, tab_ref, o_ref, p_ref, *, rows):
    slot = place_ref[0]
    half = rows * PITCH // 2
    lane = lax.broadcasted_iota(jnp.int32, (PITCH, 128), 1)
    first = lax.broadcasted_iota(jnp.int32, (1, half), 1) < early_window(slot, rows)
    turns = [lax.rem(2 * slot + r, WIN) for r in range(rows)]
    heads = [(pair, head) for pair in range(q_ref.shape[1] // 128) for head in range(2)]
    raws = [mm(q_ref[:, lanes_of(pair)], rel_ref[...]) for pair in range(len(heads) // 2)]

    def extended(pair, head):
        base = 64 - 64 * head
        one = jnp.where(lane == base, 1.0, 0.0)
        on_row = (lane >= base + 15) & (lane < base + 29)
        on_col = (lane >= base + 46) & (lane < base + 60)
        mine = head_lanes((PITCH, 128), head)
        parts = []
        for r in range(rows):
            here = raws[pair][r * PITCH : (r + 1) * PITCH, lanes_of(head)]
            along_row = pltpu.roll(here, turns[r], 1)
            along_col = pltpu.roll(here, 0, 1, stride=1, stride_axis=0)
            kept = jnp.where(mine, here, one)
            both = jnp.where(on_row, along_row, jnp.where(on_col, along_col, kept))
            high = both.astype(BF).astype(F32)
            parts.append((high + pltpu.roll(both - high, 114, 1)).astype(BF))
        return jnp.concatenate(parts, 0)

    def scored(pair, head, left):
        mine = head_lanes((KEYS, 128), head)
        keys_a = jnp.where(mine, k_ref[0:KEYS, lanes_of(pair)], tab_ref[head])
        keys_b = jnp.where(mine, k_ref[KEYS:, lanes_of(pair)], tab_ref[head])
        scores = mm_t(keys_a, left)
        return scores[:, :half], jnp.where(first, scores[:, half:], mm_t(keys_b, left[half:]))

    def softmax(pair, head, pieces):
        for i, piece in enumerate(pieces):
            grown = jnp.exp(piece - jnp.max(piece, 0, keepdims=True))
            probs = (grown * (1.0 / jnp.sum(grown, 0, keepdims=True))).astype(BF)
            p_ref[pair, head, :, i * half : (i + 1) * half] = probs

    def weighed(pair, head):
        rows_of = slice(HD * head, HD * head + HD)
        out = mm(v_ref[0:KEYS, lanes_of(pair)].T[rows_of], p_ref[pair, head])
        late = mm(v_ref[KEYS:, lanes_of(pair)].T[rows_of], p_ref[pair, head, :, half:])
        return jnp.concatenate([out[:, :half], jnp.where(first, out[:, half:], late)], 1)

    lefts = [extended(*h) for h in heads]
    scores = [scored(*h, left) for h, left in zip(heads, lefts)]
    for h, pieces in zip(heads, scores):
        softmax(*h, pieces)
    outs = [weighed(*h) for h in heads]
    for pair in range(len(heads) // 2):
        o_ref[:, lanes_of(pair)] = jnp.concatenate(outs[2 * pair : 2 * pair + 2], 0).T.astype(BF)


def attend(slot, q, k, v, rel, table, rows):
    queries = rows * PITCH
    many = PAIRS // 2
    of_k = pl.BlockSpec((EXT * PITCH, 128 * many), lambda b, p, s: (b, p))
    of_q = pl.BlockSpec((queries, 128 * many), lambda b, p, s: (b, p))
    return pl.pallas_call(
        partial(attend_body, rows=rows),
        grid_spec=pltpu.PrefetchScalarGridSpec(
            num_scalar_prefetch=1,
            grid=(SIDE, PAIRS // many),
            in_specs=[of_q, of_k, of_k, whole((128, 256)), whole((2, KEYS, 128))],
            out_specs=[
                of_q,
                pl.BlockSpec((many, 2, KEYS, queries), lambda b, p, s: (b * (PAIRS // many) + p, 0, 0, 0)),
            ],
        ),
        out_shape=[
            jax.ShapeDtypeStruct((SIDE * queries, D), BF),
            jax.ShapeDtypeStruct((SIDE * PAIRS, 2, KEYS, queries), BF),
        ],
        compiler_params=pltpu.CompilerParams(vmem_limit_bytes=63 << 20),
        cost_estimate=guess(24),
        name="attend",
    )(slot, q, k, v, rel, table)


def attend_back_body(
    place_ref, q_ref, k_ref, v_ref, p_ref, do_ref, rel_ref, tab_ref, dq_ref, dk_ref, dv_ref, drel_ref, *, rows,
):
    slot = place_ref[0]
    count = rows * PITCH
    half = count // 2
    early = early_window(slot, rows)

    @pl.when(pl.program_id(0) == 0)
    def _():
        drel_ref[...] = jnp.zeros_like(drel_ref)

    lane = lax.broadcasted_iota(jnp.int32, (PITCH, 128), 1)
    first = lax.broadcasted_iota(jnp.int32, (1, half), 1) < early
    turns = [lax.rem(2 * slot + r, WIN) for r in range(rows)]
    heads = [(pair, head) for pair in range(q_ref.shape[1] // 128) for head in range(2)]

    def split(value, head):
        spot = lax.broadcasted_iota(jnp.int32, (half, 128), 0)
        mine = head_lanes((half, 128), head)
        value = value.astype(F32)
        top = jnp.where(mine, value[:half], 0.0)
        mid = jnp.where(mine & (spot < early), value[half:], 0.0)
        low = jnp.where(mine & (spot >= early), value[half:], 0.0)
        return jnp.concatenate([top, mid], 0).astype(BF), low.astype(BF), (mid + low).astype(BF)

    def upstream(pair, head):
        return split(do_ref[:, lanes_of(pair)], head)

    def probs_grad(pair, head, out_a, late):
        whole_out = jnp.concatenate([out_a[:half], late], 0)
        grad = mm_t(v_ref[0:KEYS, lanes_of(pair)], whole_out)
        more = mm_t(v_ref[KEYS:, lanes_of(pair)], late)
        return grad[:, :half], jnp.where(first, grad[:, half:], more)

    def scores_grad(pair, head, pieces):
        grads = []
        for i, piece in enumerate(pieces):
            exact = p_ref[pair, head, :, i * half : (i + 1) * half].astype(F32)
            inner = jnp.sum(exact * piece, 0, keepdims=True)
            grads.append((exact * (piece - inner)).astype(BF))
        return jnp.concatenate(grads, 1)

    def left_grad(pair, head, grad, turned):
        spot = lax.broadcasted_iota(jnp.int32, (128, KEYS), 0)
        mine = spot < HD if head == 0 else spot >= HD
        left = mm(jnp.where(mine, turned[0], tab_ref[head]), grad)
        late = mm(jnp.where(mine, turned[1], tab_ref[head]), grad[:, half:])
        return jnp.concatenate([left[:, :half], jnp.where(first, left[:, half:], late)], 1).T

    def raw_grad(head, left):
        base = 64 - 64 * head
        on_row = (lane >= base) & (lane < base + WIN)
        on_col = (lane >= base + 32) & (lane < base + 32 + WIN)
        parts = []
        for r in range(rows):
            here = left[r * PITCH : (r + 1) * PITCH]
            along_row = pltpu.roll(jnp.where(on_row, here, 0.0), turns[r], 1)
            along_col = pltpu.roll(jnp.where(on_col, here, 0.0), 0, 1, stride=1, stride_axis=0)
            parts.append((along_row + along_col).astype(BF))
        return jnp.concatenate(parts, 0)

    outs = [upstream(*h) for h in heads]
    pieces = [probs_grad(*h, out[0], out[2]) for h, out in zip(heads, outs)]
    grads = [scores_grad(*h, piece) for h, piece in zip(heads, pieces)]
    lefts = []
    for pair in range(len(heads) // 2):
        turned = [k_ref[w * KEYS : (w + 1) * KEYS, lanes_of(pair)].T for w in range(2)]
        lefts += [left_grad(pair, head, grads[2 * pair + head], turned) for head in range(2)]
    for pair in range(len(heads) // 2):
        scaled = q_ref[:, lanes_of(pair)].astype(F32) * HD ** (-0.5)
        owns = [split(scaled, head) for head in range(2)]
        for w in range(2):
            at = (slice(w * KEYS, (w + 1) * KEYS), lanes_of(pair))
            part = slice(0, count) if w == 0 else slice(half, count)
            dv_ref[at] = sum(mm(p_ref[pair, h, :, part], outs[2 * pair + h][w]) for h in range(2)).astype(BF)
            dk_ref[at] = sum(mm(grads[2 * pair + h][:, part], owns[h][w]) for h in range(2)).astype(BF)
    for pair in range(len(heads) // 2):
        mine = lefts[2 * pair : 2 * pair + 2]
        raw = jnp.concatenate([raw_grad(head, mine[head]) for head in range(2)], 1)
        direct = jnp.where(head_lanes((count, 128), 0), *mine) * HD ** (-0.5)
        dq_ref[:, lanes_of(pair)] = (direct + mm(raw, rel_ref[...])).astype(BF)
        drel_ref[...] += t_mm(q_ref[:, lanes_of(pair)], raw)


def attend_back(slot, q, k, v, probs, grad_out, rel, table, rows, group):
    queries = rows * PITCH
    many = PAIRS // 2
    half = lambda s: s[5] ^ (1 - group)
    of_q = pl.BlockSpec((queries, 128 * many), lambda b, s: (b, half(s)))
    of_k = pl.BlockSpec((EXT * PITCH, 128 * many), lambda b, s: (b, half(s)))
    to_q = pl.BlockSpec((queries, 128 * many), lambda b, s: (b, 0))
    to_k = pl.BlockSpec((EXT * PITCH, 128 * many), lambda b, s: (b, 0))
    return pl.pallas_call(
        partial(attend_back_body, rows=rows),
        grid_spec=pltpu.PrefetchScalarGridSpec(
            num_scalar_prefetch=1,
            grid=(SIDE,),
            in_specs=[
                of_q, of_k, of_k,
                pl.BlockSpec((many, 2, KEYS, queries), lambda b, s: (b * 2 + half(s), 0, 0, 0)),
                of_q, whole((256, 128)), whole((2, 128, KEYS)),
            ],
            out_specs=[to_q, to_k, to_k, whole((128, 256))],
        ),
        out_shape=[
            jax.ShapeDtypeStruct((q.shape[0], D // 2), BF),
            jax.ShapeDtypeStruct((k.shape[0], D // 2), BF),
            jax.ShapeDtypeStruct((k.shape[0], D // 2), BF),
            jax.ShapeDtypeStruct((128, 256), F32),
        ],
        compiler_params=pltpu.CompilerParams(vmem_limit_bytes=63 << 20),
        cost_estimate=guess(16),
        name="attend_back",
    )(slot, q, k, v, probs, grad_out, rel, table)


def feed_body(place_ref, o_ref, x_ref, g_ref, vec_ref, bias_ref, rest_ref, *refs, rows):
    (
        out_ref, dh_ref, do_ref, grad_ref, gas_ref, gak_ref, gvec_ref, gbias_ref,
        nat_ref, onat_ref, n2_ref, n2t_ref, gt_ref, h_ref, y_ref, dn_ref, a_ref, du_ref, w_ref,
        up_ref, down_ref, slots_ref, sems,
    ) = refs
    step = pl.program_id(0)
    steps = rows * GRID // 256
    lines = 256 // GRID
    width = D // 4
    y, c = place_ref[3], place_ref[4]
    buffer = lax.rem(step, 2)

    def fetch(chunk, where):
        for i, ref in enumerate((up_ref, down_ref)):
            source = rest_ref.at[:, chunk, :, pl.ds(i * D, D)]
            pltpu.make_async_copy(source, ref.at[where], sems.at[where, i]).start()

    @pl.when(step == 0)
    def _():
        pltpu.make_async_copy(rest_ref.at[:, :, :, pl.ds(2 * D, 256)], slots_ref, sems.at[2, 0]).start()
        fetch(step, buffer)

    @pl.when(step < pl.num_programs(0) - 1)
    def _():
        fetch(step + 1, 1 - buffer)

    @pl.when(step == 0)
    def _():
        pltpu.make_async_copy(slots_ref, slots_ref, sems.at[2, 0]).wait()

        for t in range(4):
            w_ref[:, t * width : (t + 1) * width] = slots_ref[:, t, :, 0:width].reshape(D, width)

        def one(i, carry):
            at = pl.ds(pl.multiple_of(i * 256, 256), 256)
            for b in range(SIDE):
                piece = o_ref[b, pl.ds(i * lines, lines)]
                nat_ref[:, WIN * b : WIN * b + PITCH, :] = piece.astype(F32)
            natural = nat_ref[:, 0:GRID, :].reshape(256, D).astype(BF)
            onat_ref[at, :] = natural
            hidden = x_ref[at, :].astype(F32) + mm_t(natural, w_ref[...]) + vec_ref[0:1]
            h_ref[at, :] = hidden
            hat, _ = norm_parts(hidden)
            normed = (hat * vec_ref[1:2] + vec_ref[2:3]).astype(BF)
            n2_ref[at, :] = normed
            n2t_ref[:, at] = normed.T
            gt_ref[:, at] = g_ref[at, :].T
            y_ref[at, :] = jnp.zeros((256, D), F32)
            dn_ref[at, :] = jnp.zeros((256, D), F32)
            return carry

        lax.fori_loop(0, steps, one, 0)

    pltpu.make_async_copy(up_ref.at[buffer], up_ref.at[buffer], sems.at[buffer, 0]).wait()
    pltpu.make_async_copy(down_ref.at[buffer], down_ref.at[buffer], sems.at[buffer, 1]).wait()
    up, down = up_ref[buffer].reshape(D, D), down_ref[buffer].reshape(D, D)
    total = jnp.zeros((1, D), F32)

    def inward(i):
        at = slice(i * 512, i * 512 + 512)
        upper = mm(n2_ref[at, :], up) + bias_ref[...].reshape(1, D)
        cdf = 0.5 * (1.0 + lax.erf(upper * (1.0 / math.sqrt(2.0))))
        a_ref[at, :] = (upper * cdf).astype(BF)
        slope = cdf + upper * jnp.exp(-0.5 * upper * upper) * (1.0 / math.sqrt(2.0 * math.pi))
        delta = (mm(g_ref[at, :], down) * slope).astype(BF)
        du_ref[at, :] = delta
        return jnp.sum(delta.astype(F32), 0, keepdims=True)

    def outward(i):
        at = slice(i * 512, i * 512 + 512)
        y_ref[at, :] += mm_t(a_ref[at, :], down)
        dn_ref[at, :] += mm_t(du_ref[at, :], up)

    for i in range(rows * GRID // 512):
        total = total + inward(i)
        if i:
            outward(i - 1)
    outward(rows * GRID // 512 - 1)
    gbias_ref[...] = total.reshape(gbias_ref.shape)
    grad_up = mm(n2t_ref[...], du_ref[...]).astype(BF)
    grad_down = mm(gt_ref[...], a_ref[...]).astype(BF)
    shape = (grad_ref.shape[0], grad_ref.shape[1], D)
    grad_ref[:, :, 0:D] = grad_up.reshape(shape)
    grad_ref[:, :, D:] = grad_down.reshape(shape)

    @pl.when(step == pl.num_programs(0) - 1)
    def _():
        nat_ref[...] = jnp.zeros_like(nat_ref)
        gvec_ref[...] = jnp.zeros_like(gvec_ref)

        def three(i, carry):
            at = pl.ds(pl.multiple_of(i * 256, 256), 256)
            hidden = h_ref[at, :]
            grad = g_ref[at, :].astype(F32)
            hat, inverse = norm_parts(hidden)
            grad_normed = dn_ref[at, :]
            out_ref[at, :] = (hidden + y_ref[at, :] + vec_ref[3:4]).astype(BF)
            grad_hidden = grad + norm_back(grad_normed, hat, inverse, vec_ref[1:2])
            dh_ref[at, :] = grad_hidden
            branch = grad_hidden.astype(BF)
            n2_ref[at, :] = branch
            gvec_ref[0:1] += jnp.sum(grad_normed * hat, 0, keepdims=True)
            gvec_ref[1:2] += jnp.sum(grad_normed, 0, keepdims=True)
            gvec_ref[2:3] += jnp.sum(branch.astype(F32), 0, keepdims=True)
            gvec_ref[3:4] += jnp.sum(grad, 0, keepdims=True)
            grad_out = mm(branch, w_ref[...])
            nat_ref[:, 0:GRID, :] = grad_out.reshape(lines, GRID, D)
            keep = lax.broadcasted_iota(jnp.int32, (lines, PITCH, D), 1) < WIN
            for b in range(SIDE):
                piece = nat_ref[:, WIN * b : WIN * b + PITCH, :]
                do_ref[b, pl.ds(i * lines, lines)] = jnp.where(keep, piece, 0.0).astype(BF)
            return carry

        lax.fori_loop(0, steps, three, 0)
        grad_wo = t_mm(n2_ref[...], onat_ref[...]).astype(BF)
        for sibling, ref in ((1, gas_ref), (0, gak_ref)):
            for t in range(4):
                @pl.when(c ^ (t % 2) == sibling)
                def _(t=t, ref=ref):
                    store_shards(
                        place_ref, ref.at[y ^ (t // 2)], grad_wo[:, t * width : (t + 1) * width]
                    )


def feed(place, o, x, g, rest, vectors, up_bias, rows, shards):
    tokens = rows * GRID
    blocks, chunks, depth = rest.shape[:3]
    line = pl.BlockSpec((None, 1, D), lambda s, p: (s, 0, 0))
    grid = (SIDE, rows, PITCH, D)
    out = jax.ShapeDtypeStruct((*shards, D // chunks), BF)
    shapes = [
        jax.ShapeDtypeStruct((tokens, D), BF),
        jax.ShapeDtypeStruct((tokens, D), F32),
        jax.ShapeDtypeStruct(grid, BF),
        jax.ShapeDtypeStruct((blocks, chunks, depth, 2 * D), BF),
        out, out,
        jax.ShapeDtypeStruct((8, D), F32),
        jax.ShapeDtypeStruct((chunks, 1, D), F32),
    ]
    specs = [whole(s.shape) for s in shapes]
    specs[3] = pl.BlockSpec((blocks, None, depth, 2 * D), lambda s, p: (0, s, 0, 0))
    specs[7] = line
    return pl.pallas_call(
        partial(feed_body, rows=rows),
        grid_spec=pltpu.PrefetchScalarGridSpec(
            num_scalar_prefetch=1,
            grid=(chunks,),
            in_specs=[
                whole(grid), whole((tokens, D)), whole((tokens, D)), whole((8, D)), line,
                pl.BlockSpec(memory_space=pl.ANY),
            ],
            out_specs=specs,
            scratch_shapes=[
                pltpu.VMEM((256 // GRID, GRID + PITCH, D), F32),
                pltpu.VMEM((tokens, D), BF),
                pltpu.VMEM((tokens, D), BF),
                pltpu.VMEM((D, tokens), BF),
                pltpu.VMEM((D, tokens), BF),
                pltpu.VMEM((tokens, D), F32),
                pltpu.VMEM((tokens, D), F32),
                pltpu.VMEM((tokens, D), F32),
                pltpu.VMEM((tokens, D), BF),
                pltpu.VMEM((tokens, D), BF),
                pltpu.VMEM((D, D), BF),
                pltpu.VMEM((2, blocks, depth, D), BF),
                pltpu.VMEM((2, blocks, depth, D), BF),
                pltpu.VMEM((blocks, chunks, depth, 256), BF),
                pltpu.SemaphoreType.DMA((3, 2)),
            ],
        ),
        out_shape=shapes,
        compiler_params=pltpu.CompilerParams(vmem_limit_bytes=63 << 20),
        cost_estimate=guess(50),
        name="feed",
    )(place, o, x, g, vectors, up_bias, rest)


def finish_body(own_ref, head_ref, tail_ref, x_ref, dh_ref, vec_ref, out_ref, sum_ref):
    rows, below, above = own_ref.shape[0], head_ref.shape[0], tail_ref.shape[0]
    sum_ref[...] = jnp.zeros_like(sum_ref)

    def line(i, low, high):
        grad = own_ref[i]
        if low:
            grad = grad + head_ref[i].astype(F32)
        if high:
            grad = grad + tail_ref[i - (rows - above)].astype(F32)
        hat, inverse = norm_parts(x_ref[i].astype(F32))
        out_ref[i] = (dh_ref[i] + norm_back(grad, hat, inverse, vec_ref[0:1])).astype(BF)
        sum_ref[0:1] += jnp.sum(grad * hat, 0, keepdims=True)
        sum_ref[1:2] += jnp.sum(grad, 0, keepdims=True)

    def over(start, stop, low, high):
        lax.fori_loop(start, stop, lambda i, carry: (line(i, low, high), carry)[1], 0)

    over(0, rows - above, True, False)
    over(rows - above, below, True, True)
    over(below, rows, False, True)


def finish(own, head, tail, x, dh, vectors):
    shapes = [jax.ShapeDtypeStruct(own.shape, BF), jax.ShapeDtypeStruct((8, D), F32)]
    return pl.pallas_call(
        finish_body,
        grid=(1,),
        in_specs=[whole(v.shape) for v in (own, head, tail, x, dh, vectors)],
        out_specs=[whole(v.shape) for v in shapes],
        out_shape=shapes,
        compiler_params=pltpu.CompilerParams(vmem_limit_bytes=63 << 20),
        cost_estimate=guess(5),
        name="finish",
    )(own, head, tail, x, dh, vectors)


def fold_body(*refs, plan):
    terms = sum(count for count, *_ in plan)
    ins, outs = refs[:terms], refs[terms:]
    for (count, axis, index), out in zip(plan, outs):
        here, ins = ins[:count], ins[count:]
        lead = out.shape[:-2]
        for at in np.ndindex(*lead):
            spot = at if axis is None else at[:axis] + (index,) + at[axis:]
            total = here[0][spot].astype(F32)
            for ref in here[1:]:
                total = total + ref[spot].astype(F32)
            out[at] = total.astype(out.dtype)


def fold(*results):
    count = None
    args, in_specs, out_specs, shapes, plan = [], [], [], [], []
    for terms, z_axis, axis, index in results:
        shape = terms[0].shape
        count = shape[z_axis]
        block = tuple(None if i == z_axis else n for i, n in enumerate(shape))
        spec = pl.BlockSpec(block, lambda i, z_axis=z_axis, n=len(shape): tuple(i if k == z_axis else 0 for k in range(n)))
        args += terms
        in_specs += [spec] * len(terms)
        left = [n for i, n in enumerate(shape) if i != axis]
        z_left = z_axis if axis is None or axis > z_axis else z_axis - 1
        block = tuple(None if i == z_left else n for i, n in enumerate(left))
        out_specs.append(
            pl.BlockSpec(block, lambda i, z_left=z_left, n=len(left): tuple(i if k == z_left else 0 for k in range(n)))
        )
        shapes.append(jax.ShapeDtypeStruct(tuple(left), BF))
        inner = None if axis is None else (axis if axis < z_axis else axis - 1)
        plan.append((len(terms), inner, index))
    size = sum(2 * int(np.prod(a.shape)) for a in args)
    return pl.pallas_call(
        partial(fold_body, plan=plan),
        grid=(count,),
        in_specs=in_specs,
        out_specs=out_specs,
        out_shape=shapes,
        compiler_params=pltpu.CompilerParams(vmem_limit_bytes=63 << 20),
        cost_estimate=guess(1 + size / 2e6),
        name="fold",
    )(*args)


AXES = ("z", "x", "y", "c")
SWAP = [(0, 1), (1, 0)]


def swap(value, axis):
    return lax.ppermute(value, axis, SWAP)


def shift(value, count, by):
    return lax.ppermute(value, "z", [(i, (i + by) % count) for i in range(count)])


def gather_lines(shard, count):
    half = shard.shape[0] // 2
    lines = [shard] + [shift(shard, count, k) for k in range(1, count)]
    first = jnp.stack([line[:half] for line in lines])
    second = jnp.stack([line[half:] for line in lines])
    return jnp.stack([first, swap(first, "x")]), jnp.stack([second, swap(second, "y")])


def gather_planes(first, second):
    first = jnp.stack([first, swap(first, "y")])
    second = jnp.stack([second, swap(second, "x")])
    return first, second, swap(first, "c"), swap(second, "c")


def after(value, *others):
    return lax.optimization_barrier((value, *others))


def along_z(pieces):
    count = pieces.shape[0]
    total = pieces[0].astype(F32)
    for k in range(1, count):
        total = total + shift(pieces[k], count, k).astype(F32)
    return total


def sum_all(value, count, fast):
    for axis in ("c", "y", "x"):
        value = value + swap(value, axis)
    if not fast:
        return lax.psum(value, "z")
    step = 1
    while step < count:
        value = value + lax.ppermute(value, "z", [(i, i ^ step) for i in range(count)])
        step *= 2
    return value


def body(
    features, first_gain, first_shift, qkv_weight, qv_bias, rel_height, rel_width, output_weight,
    output_bias, second_gain, second_shift, up_weight, up_bias, down_weight, down_bias, cotangent,
    *, count,
):
    depth, _, width = qkv_weight.shape
    hidden = up_weight.shape[1]
    tokens = features.shape[0]
    rows = tokens // GRID
    slots = 4
    fast = count <= 4 and depth % 32 == 0
    z, x, y, c = (lax.axis_index(a).astype(jnp.int32) for a in AXES)
    slot = 2 * y + c
    nought = jnp.zeros((), jnp.int32)
    place = jnp.stack([slot, z, x, y, c, y] if fast else [slot] + [nought] * 4 + [y])
    shards = (2, count, 2, depth)
    above, below = 2 * (slots - 1), WIN - 2

    grid_x = features.reshape(rows, GRID, D)
    pair = ("y", "c")
    up_pairs = [(s, s + 1) for s in range(slots - 1)]
    down_pairs = [(s + 1, s) for s in range(slots - 1)]
    from_above = lax.ppermute(grid_x[rows - above :], pair, up_pairs)
    from_below = lax.ppermute(grid_x[:below], pair, down_pairs)

    rest = jnp.concatenate([up_weight, down_weight, output_weight, jnp.zeros((depth, 256 - width), BF)], 1)
    rest_all = lax.all_gather(rest, AXES, axis=0).reshape(2 * count, slots, depth, 2 * hidden + 256)
    biases = jnp.concatenate([qv_bias.reshape(-1), up_bias])
    biases = jnp.where(jnp.arange(slots)[:, None] == slot, biases[None], jnp.zeros((), BF))
    biases = biases + swap(biases, "c")
    biases = (biases + swap(biases, "y")).astype(F32)
    qv_all = biases[:, : 2 * width].reshape(slots, 2, width).transpose(1, 0, 2).reshape(2, D)
    up_bias_all = biases[:, 2 * width :].reshape(slots, 1, hidden)

    vec_one = jnp.concatenate([first_gain[None], first_shift[None], jnp.zeros((6, D), BF)], 0).astype(F32)
    normed = windows(place, from_above, grid_x, from_below, vec_one)
    if fast:
        lines = gather_lines(qkv_weight.reshape(depth, 3 * width), count)
        normed, *lines = lax.optimization_barrier((normed, *lines))
        pieces = gather_planes(*lines)
    else:
        full = lax.all_gather(qkv_weight, AXES, axis=0).reshape(2 * count, slots, depth, 3, width)
        pieces = [full.transpose(0, 2, 3, 1, 4).reshape(D, 3 * D)]
    q, k, v, weight = project(place, normed, pieces, qv_all, rows, depth)
    ahead, back = score_tables()
    rel_ahead, rel_back = offset_tables(rel_height, rel_width)
    attended, probs = attend(place, q, k, v, rel_ahead.T, jnp.asarray(ahead, BF), rows)

    vec_two = jnp.concatenate(
        [output_bias[None], second_gain[None], second_shift[None], down_bias[None], jnp.zeros((4, D), BF)], 0
    ).astype(F32)
    (
        output, grad_hidden, grad_out, grad_feed, out_send, out_keep, grad_vec, grad_up_bias,
    ) = feed(
        place, attended.reshape(SIDE, rows, PITCH, D), features, cotangent, rest_all, vec_two, up_bias_all,
        rows, shards,
    )
    grad_windows = grad_out.reshape(-1, D)
    table = jnp.asarray(back.transpose(0, 2, 1), BF)
    grad_feed = lax.psum_scatter(
        grad_feed.reshape(8 * count, depth, 2 * hidden), AXES, scatter_dimension=0
    ).astype(F32)
    grad_up, grad_down = grad_feed[:, :hidden], grad_feed[:, hidden:]
    if fast:
        out_got = swap(out_send, "c")
    *half0, drel0 = attend_back(place, q, k, v, probs, grad_windows, rel_back, table, rows, 0)
    first_send, first_keep, first_bias = project_grad(place, normed, *half0, rows, shards)
    if fast:
        first_got = swap(first_send, "c")
    *half1, drel1 = attend_back(place, q, k, v, probs, grad_windows, rel_back, table, rows, 1)
    if fast:
        first, out = [first_keep, first_got], [out_keep, out_got]
        first_away, first_here, out_away, out_here = fold(
            (first, 0, 1, 1), (first, 0, 1, 0), (out, 1, 2, 1), (out, 1, 2, 0)
        )
        place, first_away, out_away = after(place, first_away, out_away)
        first_got, out_got = swap(first_away, "x"), swap(out_away, "x")
    dqs, dks, dvs = zip(half0, half1)
    to_above, total, to_below = project_back(place, dqs, dks, dvs, weight, rows, slots)
    place, to_above, to_below = after(place, to_above, to_below)
    from_below = lax.ppermute(to_above, pair, down_pairs)
    from_above = lax.ppermute(to_below, pair, up_pairs)
    last_send, last_keep, last_bias = project_grad(place, normed, *half1, rows, shards)
    if fast:
        last_got = swap(last_send, "c")
        first_got, out_got, last_keep = after(first_got, out_got, last_keep)
        crossing, out_away, out_here = fold(
            ([first_here, first_got], 0, None, None), ([out_here, out_got], 1, 0, 1), ([out_here, out_got], 1, 0, 0)
        )
        crossing, out_got = swap(crossing, "y"), swap(out_away, "y")
    grad_features, sums_one = finish(
        total, from_above, from_below, grid_x, grad_hidden.reshape(rows, GRID, D), vec_one
    )
    if fast:
        last = [last_keep, last_got]
        away, here = fold((last, 0, 1, 1), (last, 0, 1, 0))
        last, out = fold(([here, swap(away, "x"), crossing], 0, None, None), ([out_here, out_got], 0, None, None))
        grad_qkv, grad_wo = along_z(last), along_z(out)
    else:
        pairs = [
            (out_send, out_keep),
            [
                jnp.where(y == 0, jnp.stack([last, first]), jnp.stack([first, last]))
                for first, last in ((first_send, last_send), (first_keep, last_keep))
            ],
        ]
        grad_wo, grad_qkv = [
            lax.psum_scatter(
                jnp.stack([keep, send], 3).transpose(1, 2, 0, 3, 4, 5).reshape(8 * count, depth, -1),
                AXES, scatter_dimension=0,
            ).astype(F32)
            for send, keep in pairs
        ]
    drel = (drel0 + drel1).T.reshape(4, 64, 128)
    drel = drel[1, :, :HD] + drel[2, :, HD:]
    grad_qv = jnp.where(y == 0, jnp.concatenate([last_bias, first_bias], 1), jnp.concatenate([first_bias, last_bias], 1))
    small = jnp.concatenate(
        [grad_vec[:4], grad_up_bias.reshape(slots, hidden), sums_one[:2], grad_qv], 0
    )
    small = sum_all(jnp.concatenate([small.reshape(-1), drel.reshape(-1)]).reshape(-1, 512), count, fast).reshape(-1)
    vec = small[: 12 * D].reshape(12, D)
    drel = small[12 * D :].reshape(64, HD)
    qv = lax.dynamic_index_in_dim(vec[10:12].reshape(2, slots, width), slot, 1, keepdims=False)
    bias = lax.dynamic_index_in_dim(vec[4:8], slot, 0, keepdims=False)
    return (
        output,
        grad_features.reshape(tokens, D),
        vec[8],
        vec[9],
        grad_qkv.reshape(depth, 3, width),
        qv,
        drel[0:OFFS],
        drel[32 : 32 + OFFS],
        grad_wo,
        vec[2],
        vec[0],
        vec[1],
        grad_up,
        bias,
        grad_down,
        vec[3],
    )


def solution(mesh):
    token = P(AXES, None)
    square = P(("z", "x"), ("y", "c"))
    cube = P(("z", "x"), None, ("y", "c"))
    lane = P(("y", "c"))
    count = mesh.shape["dp"] // 2
    assert mesh.shape["tensor"] == 4
    return jax.shard_map(
        partial(body, count=count),
        mesh=jax.sharding.Mesh(mesh.devices.reshape(count, 2, 2, 2), AXES),
        in_specs=(
            token, P(), P(), cube, P(None, ("y", "c")), P(), P(), square, P(), P(), P(), square,
            lane, square, P(), token,
        ),
        out_specs=(
            token, token, P(), P(), cube, P(None, ("y", "c")), P(), P(), square, P(), P(), P(), square,
            lane, square, P(),
        ),
        check_vma=False,
    )
```

```python
from functools import partial
import math

import jax
import jax.numpy as jnp
from jax import lax
from jax.experimental import pallas as pl
from jax.experimental.pallas import tpu as pltpu
from jax.sharding import PartitionSpec as P
import numpy as np

D = 768
HD = 64
GRID = 64
WIN = 14
SIDE = 5
PITCH = 16
KEYS = WIN * PITCH
EXT = 2 * WIN
PAIRS = D // (2 * HD)
OFFS = 2 * WIN - 1
EPSILON = 1e-06
FAR = -1e30
BF = jnp.bfloat16
F32 = jnp.float32
HIGH = lax.Precision.HIGHEST


def mm(left, right):
    return jnp.dot(left, right, preferred_element_type=F32)


def mm_t(left, right):
    return lax.dot_general(left, right, (((1,), (1,)), ((), ())), preferred_element_type=F32)


def t_mm(left, right):
    return lax.dot_general(left, right, (((0,), (0,)), ((), ())), preferred_element_type=F32)


def norm_parts(value):
    centered = value - jnp.mean(value, -1, keepdims=True)
    inverse = lax.rsqrt(jnp.mean(centered * centered, -1, keepdims=True) + EPSILON)
    return centered * inverse, inverse


def norm_back(upstream, hat, inverse, gain):
    scaled = upstream * gain
    return inverse * (
        scaled
        - jnp.mean(scaled, -1, keepdims=True)
        - hat * jnp.mean(scaled * hat, -1, keepdims=True)
    )


def score_tables():
    ahead = np.zeros((2, KEYS, 128), np.float32)
    back = np.zeros((2, KEYS, 128), np.float32)
    for head in range(2):
        base = 64 - 64 * head
        for c in range(WIN):
            for e in range(PITCH):
                k = c * PITCH + e
                if e >= WIN:
                    ahead[head, k, base] = FAR
                    continue
                ahead[head, k, base + 15 + c] = 1
                ahead[head, k, base + 1 + c] = 1
                ahead[head, k, base + 46 + e] = 1
                ahead[head, k, base + 32 + e] = 1
                back[head, k, base + WIN - 1 - c] = 1
                back[head, k, base + 32 + WIN - 1 - e] = 1
    return ahead, back


def offset_tables(rel_height, rel_width):
    def place(first, second, at_rows, at_cols):
        slab = jnp.zeros((64, HD), BF)
        slab = slab.at[at_rows : at_rows + OFFS].set(first)
        slab = slab.at[at_cols : at_cols + OFFS].set(second)
        low = jnp.concatenate([slab, jnp.zeros_like(slab)], 1)
        high = jnp.concatenate([jnp.zeros_like(slab), slab], 1)
        return jnp.concatenate([jnp.zeros_like(low), low, high, jnp.zeros_like(high)], 0)

    through = jnp.eye(HD, dtype=BF) * BF(HD ** (-0.5))
    nothing = jnp.zeros_like(through)
    through = jnp.concatenate(
        [jnp.concatenate([through, nothing], 1), jnp.zeros((128, 128), BF), jnp.concatenate([nothing, through], 1)], 0
    )
    return (
        place(rel_height[::-1], rel_width[::-1], 2, 33) + through,
        place(rel_height, rel_width, 0, 32),
    )


def whole(shape):
    return pl.BlockSpec(shape, lambda *_: (0,) * len(shape), pipeline_mode=pl.Buffered(1))


def windows_body(place_ref, above_ref, x_ref, below_ref, vec_ref, nw_ref, turned_ref, own_ref, nat_ref, *, rows):
    band = pl.program_id(0)
    slot = place_ref[0]
    above, below = above_ref.shape[0], below_ref.shape[0]

    @pl.when(band == 0)
    def _():
        def normed(piece):
            hat, _ = norm_parts(piece.astype(F32))
            return hat * vec_ref[0:1] + vec_ref[1:2]

        def clear(i, carry):
            nat_ref[i, GRID : GRID + PITCH, :] = jnp.zeros((PITCH, D), F32)
            return carry

        def own(i, carry):
            nat_ref[2 * slot + i, 0:GRID, :] = normed(x_ref[i])
            return carry

        def before(i, carry):
            nat_ref[i, 0:GRID, :] = normed(above_ref[above - 2 * slot + i])
            return carry

        def after(i, carry):
            at = 2 * slot + rows + i
            inside = WIN * slot + at < GRID
            nat_ref[at, 0:GRID, :] = jnp.where(inside, normed(below_ref[i]), 0.0)
            return carry

        lax.fori_loop(0, EXT, clear, 0)
        lax.fori_loop(0, rows, own, 0)
        lax.fori_loop(0, 2 * slot, before, 0)
        lax.fori_loop(0, EXT - rows - 2 * slot, after, 0)

    keep = lax.broadcasted_iota(jnp.int32, (PITCH, D), 0) < WIN
    for b in range(SIDE):
        @pl.when(band == b)
        def _(b=b):
            def one(i, carry):
                piece = nat_ref[i, WIN * b : WIN * b + PITCH, :]
                start = pl.multiple_of(i * PITCH, PITCH)
                nw_ref[pl.ds(start, PITCH), :] = jnp.where(keep, piece, 0.0).astype(BF)
                return carry

            lax.fori_loop(0, EXT, one, 0)

    turned_ref[...] = nw_ref[...].T
    own_ref[...] = nw_ref[pl.ds(pl.multiple_of(slot * 2 * PITCH, 2 * PITCH), rows * PITCH), :].T


def windows(place, above, x, below, vectors):
    rows = x.shape[0]
    return pl.pallas_call(
        partial(windows_body, rows=rows),
        grid_spec=pltpu.PrefetchScalarGridSpec(
            num_scalar_prefetch=1,
            grid=(SIDE,),
            in_specs=[whole(above.shape), whole(x.shape), whole(below.shape), whole((8, D))],
            out_specs=[
                pl.BlockSpec((EXT * PITCH, D), lambda b, s: (b, 0)),
                pl.BlockSpec((None, D, EXT * PITCH), lambda b, s: (b, 0, 0)),
                pl.BlockSpec((None, D, rows * PITCH), lambda b, s: (b, 0, 0)),
            ],
            scratch_shapes=[pltpu.VMEM((EXT, GRID + PITCH, D), F32)],
        ),
        out_shape=[
            jax.ShapeDtypeStruct((SIDE * EXT * PITCH, D), BF),
            jax.ShapeDtypeStruct((SIDE, D, EXT * PITCH), BF),
            jax.ShapeDtypeStruct((SIDE, D, rows * PITCH), BF),
        ],
        compiler_params=pltpu.CompilerParams(vmem_limit_bytes=63 << 20),
        cost_estimate=guess(8),
        name="windows",
    )(place, above, x, below, vectors)


def project_body(place_ref, nw_ref, *refs, rows, depth):
    *pieces, bias_ref, q_ref, k_ref, v_ref, w_ref, stage_ref = refs
    slot, z, x, y, c = (place_ref[i] for i in range(5))
    width = D // 4

    @pl.when(pl.program_id(0) == 0)
    def _():
        if len(pieces) == 1:
            w_ref[...] = pieces[0][...]
            return
        half = depth // 2
        for index, ref in enumerate(pieces):
            sibling, part, dx, dy = index // 8, index // 4 % 2, index // 2 % 2, index % 2
            count = ref.shape[0]
            from_slot = (y ^ dy) * 2 + (c ^ sibling)
            for dz in range(count):
                group = lax.rem(z - dz + count, count) * 2 + (x ^ dx)
                at = pl.multiple_of(group * depth + part * half, half)
                stage_ref[from_slot, pl.ds(at, half), :] = ref[dz]

        def join(i, carry):
            at = pl.ds(pl.multiple_of(i * 64, 64), 64)
            for kind in range(3):
                w_ref[at, kind * D : (kind + 1) * D] = jnp.concatenate(
                    [stage_ref[t, at, kind * width : (kind + 1) * width] for t in range(4)], 1
                )
            return carry

        lax.fori_loop(0, D // 64, join, 0)

    normed = nw_ref[...]
    own = nw_ref[pl.ds(pl.multiple_of(slot * 2 * PITCH, 2 * PITCH), rows * PITCH), :]
    q_ref[...] = (mm(own, w_ref[:, 0:D]) + bias_ref[0:1]).astype(BF)
    k_ref[...] = mm(normed, w_ref[:, D : 2 * D]).astype(BF)
    v_ref[...] = (mm(normed, w_ref[:, 2 * D :]) + bias_ref[1:2]).astype(BF)


def guess(us):
    return pl.CostEstimate(flops=int(us * 1.1e9), bytes_accessed=int(us * 3e6), transcendentals=0)


def project(place, normed, pieces, bias, rows, depth):
    of_k = pl.BlockSpec((EXT * PITCH, D), lambda b, s: (b, 0))
    of_q = pl.BlockSpec((rows * PITCH, D), lambda b, s: (b, 0))
    keys = jax.ShapeDtypeStruct((SIDE * EXT * PITCH, D), BF)
    return pl.pallas_call(
        partial(project_body, rows=rows, depth=depth),
        grid_spec=pltpu.PrefetchScalarGridSpec(
            num_scalar_prefetch=1,
            grid=(SIDE,),
            in_specs=[of_k] + [whole(p.shape) for p in pieces] + [whole((2, D))],
            out_specs=[of_q, of_k, of_k, whole((D, 3 * D))],
            scratch_shapes=[pltpu.VMEM((4, D, 3 * D // 4), BF)],
        ),
        out_shape=[
            jax.ShapeDtypeStruct((SIDE * rows * PITCH, D), BF), keys, keys,
            jax.ShapeDtypeStruct((D, 3 * D), BF),
        ],
        compiler_params=pltpu.CompilerParams(vmem_limit_bytes=63 << 20),
        cost_estimate=guess(18),
        name="project",
    )(place, normed, *pieces, bias)


def store_shards(place_ref, refs, value, first=0):
    z, x = place_ref[1], place_ref[2]
    count, _, depth = refs.shape[:3]
    if depth % 32:
        refs[...] = value.reshape(refs.shape)
        return
    for zd in range(value.shape[0] // (2 * depth)):
        for xd in range(2):
            start = (zd * 2 + xd) * depth
            refs[lax.rem(first + zd - z + count, count), x ^ xd] = value[start : start + depth]


def project_grad_body(place_ref, turned_ref, own_ref, dq_ref, dk_ref, dv_ref, send_ref, keep_ref, bias_ref, *, parts):
    step = pl.program_id(0)
    c = place_ref[4]
    width = D // 4

    @pl.when(step == 0)
    def _():
        bias_ref[0:1] = jnp.sum(dq_ref[...].astype(F32), 0, keepdims=True)
        bias_ref[1:2] = jnp.sum(dv_ref[...].astype(F32), 0, keepdims=True)

    def over_bands(left, right):
        lines = left.shape[2]
        return sum(mm(left[b], right(slice(b * lines, (b + 1) * lines))) for b in range(SIDE)).astype(BF)

    both = over_bands(turned_ref, lambda at: jnp.concatenate([dk_ref[at], dv_ref[at]], 1))
    grads = [over_bands(own_ref, lambda at: dq_ref[at]), both[:, : D // 2], both[:, D // 2 :]]
    first = step * (keep_ref.shape[0] // parts)
    for core in range(2):
        value = jnp.concatenate([g[:, core * width : (core + 1) * width] for g in grads], 1)
        for sibling, ref in ((1, send_ref), (0, keep_ref)):
            @pl.when(c ^ core == sibling)
            def _(ref=ref, value=value):
                store_shards(place_ref, ref, value, first)


def project_grad(place, turned, own, dq, dk, dv, shards):
    count, depth = shards[1], shards[3]
    parts = 2 if depth % 32 == 0 else 1
    out = jax.ShapeDtypeStruct((count, 2, depth, 3 * D // 4), BF)
    return pl.pallas_call(
        partial(project_grad_body, parts=parts),
        grid_spec=pltpu.PrefetchScalarGridSpec(
            num_scalar_prefetch=1,
            grid=(parts,),
            in_specs=[
                pl.BlockSpec((SIDE, D // parts, turned.shape[2]), lambda i, s: (0, i, 0)),
                pl.BlockSpec((SIDE, D // parts, own.shape[2]), lambda i, s: (0, i, 0)),
                whole(dq.shape), whole(dk.shape), whole(dv.shape),
            ],
            out_specs=[whole(out.shape), whole(out.shape), whole((2, D // 2))],
        ),
        out_shape=[out, out, jax.ShapeDtypeStruct((2, D // 2), F32)],
        compiler_params=pltpu.CompilerParams(vmem_limit_bytes=63 << 20),
        cost_estimate=guess(6),
        name="project_grad",
    )(place, turned, own, dq, dk, dv)


def project_back_body(place_ref, *refs, rows):
    dqs, dks, dvs = refs[0:2], refs[2:4], refs[4:6]
    w_ref, above_ref, own_ref, below_ref, all_ref, dq_ref, dk_ref, dv_ref = refs[6:]
    slot, y = place_ref[0], place_ref[5]
    above, below = above_ref.shape[0], below_ref.shape[0]
    for halves, ref in ((dqs, dq_ref), (dks, dk_ref), (dvs, dv_ref)):
        for i in range(2):
            at = pl.multiple_of((y ^ (1 - i)) * (D // 2), D // 2)
            ref[:, pl.ds(at, D // 2)] = halves[i][...]
    grad = mm_t(dk_ref[...], w_ref[:, D : 2 * D]) + mm_t(dv_ref[...], w_ref[:, 2 * D :])
    direct = mm_t(dq_ref[...], w_ref[:, 0:D]).reshape(rows, PITCH, D)
    all_ref[0:above] = jnp.zeros((above, PITCH, D), F32)
    all_ref[above + rows :] = jnp.zeros((below, PITCH, D), F32)
    all_ref[pl.ds(above - 2 * slot, EXT)] = grad.reshape(EXT, PITCH, D)
    above_ref[...] = all_ref[0:above].astype(BF)
    own_ref[...] = all_ref[above : above + rows] + direct
    below_ref[...] = all_ref[above + rows :].astype(BF)


def project_back(place, dqs, dks, dvs, weight, rows):
    above, below = 8, WIN - 2
    of_k = pl.BlockSpec((EXT * PITCH, D // 2), lambda b, s: (b, 0))
    of_q = pl.BlockSpec((rows * PITCH, D // 2), lambda b, s: (b, 0))
    part = lambda n: pl.BlockSpec((None, n, PITCH, D), lambda b, s: (b, 0, 0, 0))
    return pl.pallas_call(
        partial(project_back_body, rows=rows),
        grid_spec=pltpu.PrefetchScalarGridSpec(
            num_scalar_prefetch=1,
            grid=(SIDE,),
            in_specs=[of_q, of_q, of_k, of_k, of_k, of_k, whole((D, 3 * D))],
            out_specs=[part(above), part(rows), part(below)],
            scratch_shapes=[
                pltpu.VMEM((above + rows + below, PITCH, D), F32),
                pltpu.VMEM((rows * PITCH, D), BF),
                pltpu.VMEM((EXT * PITCH, D), BF),
                pltpu.VMEM((EXT * PITCH, D), BF),
            ],
        ),
        out_shape=[
            jax.ShapeDtypeStruct((SIDE, above, PITCH, D), BF),
            jax.ShapeDtypeStruct((SIDE, rows, PITCH, D), F32),
            jax.ShapeDtypeStruct((SIDE, below, PITCH, D), BF),
        ],
        compiler_params=pltpu.CompilerParams(vmem_limit_bytes=63 << 20),
        cost_estimate=guess(10),
        name="project_back",
    )(place, *dqs, *dks, *dvs, weight)


def head_lanes(shape, head):
    lane = lax.broadcasted_iota(jnp.int32, shape, 1)
    return lane < HD if head == 0 else lane >= HD


def early_window(slot, rows):
    return (WIN - 2 * slot) * PITCH - rows * PITCH // 2


def lanes_of(pair):
    return slice(128 * pair, 128 * pair + 128)


def attend_body(place_ref, q_ref, k_ref, v_ref, rel_ref, tab_ref, o_ref, p_ref, *, rows):
    slot = place_ref[0]
    half = rows * PITCH // 2
    lane = lax.broadcasted_iota(jnp.int32, (PITCH, 128), 1)
    first = lax.broadcasted_iota(jnp.int32, (1, half), 1) < early_window(slot, rows)
    turns = [lax.rem(2 * slot + r, WIN) for r in range(rows)]
    heads = [(pair, head) for pair in range(q_ref.shape[1] // 128) for head in range(2)]
    raws = [mm(q_ref[:, lanes_of(pair)], rel_ref[...]) for pair in range(len(heads) // 2)]

    def extended(pair, head):
        base = 64 - 64 * head
        one = jnp.where(lane == base, 1.0, 0.0)
        on_row = (lane >= base + 15) & (lane < base + 29)
        on_col = (lane >= base + 46) & (lane < base + 60)
        mine = head_lanes((PITCH, 128), head)
        parts = []
        for r in range(rows):
            here = raws[pair][r * PITCH : (r + 1) * PITCH, lanes_of(head)]
            along_row = pltpu.roll(here, turns[r], 1)
            along_col = pltpu.roll(here, 0, 1, stride=1, stride_axis=0)
            kept = jnp.where(mine, here, one)
            both = jnp.where(on_row, along_row, jnp.where(on_col, along_col, kept))
            high = both.astype(BF).astype(F32)
            parts.append((high + pltpu.roll(both - high, 114, 1)).astype(BF))
        return jnp.concatenate(parts, 0)

    def scored(pair, head, left):
        mine = head_lanes((KEYS, 128), head)
        keys_a = jnp.where(mine, k_ref[0:KEYS, lanes_of(pair)], tab_ref[head])
        keys_b = jnp.where(mine, k_ref[KEYS:, lanes_of(pair)], tab_ref[head])
        scores = mm_t(keys_a, left)
        return scores[:, :half], jnp.where(first, scores[:, half:], mm_t(keys_b, left[half:]))

    def softmax(pair, head, pieces):
        for i, piece in enumerate(pieces):
            grown = jnp.exp(piece - jnp.max(piece, 0, keepdims=True))
            probs = (grown * (1.0 / jnp.sum(grown, 0, keepdims=True))).astype(BF)
            p_ref[pair, head, :, i * half : (i + 1) * half] = probs

    def weighed(pair, head):
        rows_of = slice(HD * head, HD * head + HD)
        out = mm(v_ref[0:KEYS, lanes_of(pair)].T[rows_of], p_ref[pair, head])
        late = mm(v_ref[KEYS:, lanes_of(pair)].T[rows_of], p_ref[pair, head, :, half:])
        return jnp.concatenate([out[:, :half], jnp.where(first, out[:, half:], late)], 1)

    lefts = [extended(*h) for h in heads]
    scores = [scored(*h, left) for h, left in zip(heads, lefts)]
    for h, pieces in zip(heads, scores):
        softmax(*h, pieces)
    outs = [weighed(*h) for h in heads]
    for pair in range(len(heads) // 2):
        o_ref[:, lanes_of(pair)] = jnp.concatenate(outs[2 * pair : 2 * pair + 2], 0).T.astype(BF)


def attend(slot, q, k, v, rel, table, rows):
    queries = rows * PITCH
    many = PAIRS // 2
    of_k = pl.BlockSpec((EXT * PITCH, 128 * many), lambda b, p, s: (b, p))
    of_q = pl.BlockSpec((queries, 128 * many), lambda b, p, s: (b, p))
    return pl.pallas_call(
        partial(attend_body, rows=rows),
        grid_spec=pltpu.PrefetchScalarGridSpec(
            num_scalar_prefetch=1,
            grid=(SIDE, PAIRS // many),
            in_specs=[of_q, of_k, of_k, whole((128, 256)), whole((2, KEYS, 128))],
            out_specs=[
                of_q,
                pl.BlockSpec((many, 2, KEYS, queries), lambda b, p, s: (b * (PAIRS // many) + p, 0, 0, 0)),
            ],
        ),
        out_shape=[
            jax.ShapeDtypeStruct((SIDE * queries, D), BF),
            jax.ShapeDtypeStruct((SIDE * PAIRS, 2, KEYS, queries), BF),
        ],
        compiler_params=pltpu.CompilerParams(vmem_limit_bytes=63 << 20),
        cost_estimate=guess(24),
        name="attend",
    )(slot, q, k, v, rel, table)


def attend_back_body(
    place_ref, q_ref, k_ref, v_ref, p_ref, do_ref, rel_ref, tab_ref, dq_ref, dk_ref, dv_ref, drel_ref, *, rows,
):
    slot = place_ref[0]
    count = rows * PITCH
    half = count // 2
    early = early_window(slot, rows)

    @pl.when(pl.program_id(0) == 0)
    def _():
        drel_ref[...] = jnp.zeros_like(drel_ref)

    lane = lax.broadcasted_iota(jnp.int32, (PITCH, 128), 1)
    first = lax.broadcasted_iota(jnp.int32, (1, half), 1) < early
    turns = [lax.rem(2 * slot + r, WIN) for r in range(rows)]
    heads = [(pair, head) for pair in range(q_ref.shape[1] // 128) for head in range(2)]

    def split(value, head):
        spot = lax.broadcasted_iota(jnp.int32, (half, 128), 0)
        mine = head_lanes((half, 128), head)
        value = value.astype(F32)
        top = jnp.where(mine, value[:half], 0.0)
        mid = jnp.where(mine & (spot < early), value[half:], 0.0)
        low = jnp.where(mine & (spot >= early), value[half:], 0.0)
        return jnp.concatenate([top, mid], 0).astype(BF), low.astype(BF), (mid + low).astype(BF)

    def upstream(pair, head):
        return split(do_ref[:, lanes_of(pair)], head)

    def probs_grad(pair, head, out_a, late):
        whole_out = jnp.concatenate([out_a[:half], late], 0)
        grad = mm_t(v_ref[0:KEYS, lanes_of(pair)], whole_out)
        more = mm_t(v_ref[KEYS:, lanes_of(pair)], late)
        return grad[:, :half], jnp.where(first, grad[:, half:], more)

    def scores_grad(pair, head, pieces):
        grads = []
        for i, piece in enumerate(pieces):
            exact = p_ref[pair, head, :, i * half : (i + 1) * half].astype(F32)
            inner = jnp.sum(exact * piece, 0, keepdims=True)
            grads.append((exact * (piece - inner)).astype(BF))
        return jnp.concatenate(grads, 1)

    def left_grad(pair, head, grad, turned):
        spot = lax.broadcasted_iota(jnp.int32, (128, KEYS), 0)
        mine = spot < HD if head == 0 else spot >= HD
        left = mm(jnp.where(mine, turned[0], tab_ref[head]), grad)
        late = mm(jnp.where(mine, turned[1], tab_ref[head]), grad[:, half:])
        return jnp.concatenate([left[:, :half], jnp.where(first, left[:, half:], late)], 1).T

    def raw_grad(head, left):
        base = 64 - 64 * head
        on_row = (lane >= base) & (lane < base + WIN)
        on_col = (lane >= base + 32) & (lane < base + 32 + WIN)
        parts = []
        for r in range(rows):
            here = left[r * PITCH : (r + 1) * PITCH]
            along_row = pltpu.roll(jnp.where(on_row, here, 0.0), turns[r], 1)
            along_col = pltpu.roll(jnp.where(on_col, here, 0.0), 0, 1, stride=1, stride_axis=0)
            parts.append((along_row + along_col).astype(BF))
        return jnp.concatenate(parts, 0)

    outs = [upstream(*h) for h in heads]
    pieces = [probs_grad(*h, out[0], out[2]) for h, out in zip(heads, outs)]
    grads = [scores_grad(*h, piece) for h, piece in zip(heads, pieces)]
    lefts = []
    for pair in range(len(heads) // 2):
        turned = [k_ref[w * KEYS : (w + 1) * KEYS, lanes_of(pair)].T for w in range(2)]
        lefts += [left_grad(pair, head, grads[2 * pair + head], turned) for head in range(2)]
    for pair in range(len(heads) // 2):
        scaled = q_ref[:, lanes_of(pair)].astype(F32) * HD ** (-0.5)
        owns = [split(scaled, head) for head in range(2)]
        for w in range(2):
            at = (slice(w * KEYS, (w + 1) * KEYS), lanes_of(pair))
            part = slice(0, count) if w == 0 else slice(half, count)
            dv_ref[at] = sum(mm(p_ref[pair, h, :, part], outs[2 * pair + h][w]) for h in range(2)).astype(BF)
            dk_ref[at] = sum(mm(grads[2 * pair + h][:, part], owns[h][w]) for h in range(2)).astype(BF)
    for pair in range(len(heads) // 2):
        mine = lefts[2 * pair : 2 * pair + 2]
        raw = jnp.concatenate([raw_grad(head, mine[head]) for head in range(2)], 1)
        direct = jnp.where(head_lanes((count, 128), 0), *mine) * HD ** (-0.5)
        dq_ref[:, lanes_of(pair)] = (direct + mm(raw, rel_ref[...])).astype(BF)
        drel_ref[...] += t_mm(q_ref[:, lanes_of(pair)], raw)


def attend_back(slot, q, k, v, probs, grad_out, rel, table, rows, group):
    queries = rows * PITCH
    many = PAIRS // 2
    half = lambda s: s[5] ^ (1 - group)
    of_q = pl.BlockSpec((queries, 128 * many), lambda b, s: (b, half(s)))
    of_k = pl.BlockSpec((EXT * PITCH, 128 * many), lambda b, s: (b, half(s)))
    to_q = pl.BlockSpec((queries, 128 * many), lambda b, s: (b, 0))
    to_k = pl.BlockSpec((EXT * PITCH, 128 * many), lambda b, s: (b, 0))
    return pl.pallas_call(
        partial(attend_back_body, rows=rows),
        grid_spec=pltpu.PrefetchScalarGridSpec(
            num_scalar_prefetch=1,
            grid=(SIDE,),
            in_specs=[
                of_q, of_k, of_k,
                pl.BlockSpec((many, 2, KEYS, queries), lambda b, s: (b * 2 + half(s), 0, 0, 0)),
                of_q, whole((256, 128)), whole((2, 128, KEYS)),
            ],
            out_specs=[to_q, to_k, to_k, whole((128, 256))],
        ),
        out_shape=[
            jax.ShapeDtypeStruct((q.shape[0], D // 2), BF),
            jax.ShapeDtypeStruct((k.shape[0], D // 2), BF),
            jax.ShapeDtypeStruct((k.shape[0], D // 2), BF),
            jax.ShapeDtypeStruct((128, 256), F32),
        ],
        compiler_params=pltpu.CompilerParams(vmem_limit_bytes=63 << 20),
        cost_estimate=guess(16),
        name="attend_back",
    )(slot, q, k, v, probs, grad_out, rel, table)


def feed_body(place_ref, o_ref, x_ref, g_ref, vec_ref, bias_ref, rest_ref, *refs, rows):
    (
        out_ref, dh_ref, do_ref, grad_ref, gas_ref, gak_ref, gvec_ref, gbias_ref,
        nat_ref, onat_ref, n2_ref, n2t_ref, gt_ref, h_ref, y_ref, dn_ref, a_ref, du_ref, w_ref,
        up_ref, down_ref, slots_ref, sems,
    ) = refs
    step = pl.program_id(0)
    steps = rows * GRID // 256
    lines = 256 // GRID
    width = D // 4
    y, c = place_ref[3], place_ref[4]
    buffer = lax.rem(step, 2)

    def fetch(chunk, where):
        for i, ref in enumerate((up_ref, down_ref)):
            source = rest_ref.at[:, chunk, :, pl.ds(i * D, D)]
            pltpu.make_async_copy(source, ref.at[where], sems.at[where, i]).start()

    @pl.when(step == 0)
    def _():
        pltpu.make_async_copy(rest_ref.at[:, :, :, pl.ds(2 * D, 256)], slots_ref, sems.at[2, 0]).start()
        fetch(step, buffer)

    @pl.when(step < pl.num_programs(0) - 1)
    def _():
        fetch(step + 1, 1 - buffer)

    @pl.when(step == 0)
    def _():
        pltpu.make_async_copy(slots_ref, slots_ref, sems.at[2, 0]).wait()

        for t in range(4):
            w_ref[:, t * width : (t + 1) * width] = slots_ref[:, t, :, 0:width].reshape(D, width)

        def one(i, carry):
            at = pl.ds(pl.multiple_of(i * 256, 256), 256)
            for b in range(SIDE):
                piece = o_ref[b, pl.ds(i * lines, lines)]
                nat_ref[:, WIN * b : WIN * b + PITCH, :] = piece.astype(F32)
            natural = nat_ref[:, 0:GRID, :].reshape(256, D).astype(BF)
            onat_ref[at, :] = natural
            hidden = x_ref[at, :].astype(F32) + mm_t(natural, w_ref[...]) + vec_ref[0:1]
            h_ref[at, :] = hidden
            hat, _ = norm_parts(hidden)
            normed = (hat * vec_ref[1:2] + vec_ref[2:3]).astype(BF)
            n2_ref[at, :] = normed
            n2t_ref[:, at] = normed.T
            gt_ref[:, at] = g_ref[at, :].T
            y_ref[at, :] = jnp.zeros((256, D), F32)
            dn_ref[at, :] = jnp.zeros((256, D), F32)
            return carry

        lax.fori_loop(0, steps, one, 0, unroll=2)

    pltpu.make_async_copy(up_ref.at[buffer], up_ref.at[buffer], sems.at[buffer, 0]).wait()
    pltpu.make_async_copy(down_ref.at[buffer], down_ref.at[buffer], sems.at[buffer, 1]).wait()
    up, down = up_ref[buffer].reshape(D, D), down_ref[buffer].reshape(D, D)
    total = jnp.zeros((1, D), F32)

    def inward(i):
        at = slice(i * 512, i * 512 + 512)
        upper = mm(n2_ref[at, :], up) + bias_ref[...].reshape(1, D)
        cdf = 0.5 * (1.0 + lax.erf(upper * (1.0 / math.sqrt(2.0))))
        a_ref[at, :] = (upper * cdf).astype(BF)
        slope = cdf + upper * jnp.exp(-0.5 * upper * upper) * (1.0 / math.sqrt(2.0 * math.pi))
        delta = (mm(g_ref[at, :], down) * slope).astype(BF)
        du_ref[at, :] = delta
        return jnp.sum(delta.astype(F32), 0, keepdims=True)

    def outward(i):
        at = slice(i * 512, i * 512 + 512)
        y_ref[at, :] += mm_t(a_ref[at, :], down)
        dn_ref[at, :] += mm_t(du_ref[at, :], up)

    for i in range(rows * GRID // 512):
        total = total + inward(i)
        if i:
            outward(i - 1)
    outward(rows * GRID // 512 - 1)
    gbias_ref[...] = total.reshape(gbias_ref.shape)
    grad_up = mm(n2t_ref[...], du_ref[...]).astype(BF)
    grad_down = mm(gt_ref[...], a_ref[...]).astype(BF)
    shape = (grad_ref.shape[0], grad_ref.shape[1], D)
    grad_ref[:, :, 0:D] = grad_up.reshape(shape)
    grad_ref[:, :, D:] = grad_down.reshape(shape)

    @pl.when(step == pl.num_programs(0) - 1)
    def _():
        nat_ref[...] = jnp.zeros_like(nat_ref)
        gvec_ref[...] = jnp.zeros_like(gvec_ref)

        def three(i, carry):
            at = pl.ds(pl.multiple_of(i * 256, 256), 256)
            hidden = h_ref[at, :]
            grad = g_ref[at, :].astype(F32)
            hat, inverse = norm_parts(hidden)
            grad_normed = dn_ref[at, :]
            out_ref[at, :] = (hidden + y_ref[at, :] + vec_ref[3:4]).astype(BF)
            grad_hidden = grad + norm_back(grad_normed, hat, inverse, vec_ref[1:2])
            dh_ref[at, :] = grad_hidden
            branch = grad_hidden.astype(BF)
            n2_ref[at, :] = branch
            gvec_ref[0:1] += jnp.sum(grad_normed * hat, 0, keepdims=True)
            gvec_ref[1:2] += jnp.sum(grad_normed, 0, keepdims=True)
            gvec_ref[2:3] += jnp.sum(branch.astype(F32), 0, keepdims=True)
            gvec_ref[3:4] += jnp.sum(grad, 0, keepdims=True)
            grad_out = mm(branch, w_ref[...])
            nat_ref[:, 0:GRID, :] = grad_out.reshape(lines, GRID, D)
            keep = lax.broadcasted_iota(jnp.int32, (lines, PITCH, D), 1) < WIN
            for b in range(SIDE):
                piece = nat_ref[:, WIN * b : WIN * b + PITCH, :]
                do_ref[b, pl.ds(i * lines, lines)] = jnp.where(keep, piece, 0.0).astype(BF)
            return carry

        lax.fori_loop(0, steps, three, 0, unroll=2)
        grad_wo = t_mm(n2_ref[...], onat_ref[...]).astype(BF)
        for sibling, ref in ((1, gas_ref), (0, gak_ref)):
            for t in range(4):
                @pl.when(c ^ (t % 2) == sibling)
                def _(t=t, ref=ref):
                    store_shards(
                        place_ref, ref.at[y ^ (t // 2)], grad_wo[:, t * width : (t + 1) * width]
                    )


def feed(place, o, x, g, rest, vectors, up_bias, rows, shards):
    tokens = rows * GRID
    blocks, chunks, depth = rest.shape[:3]
    line = pl.BlockSpec((None, 1, D), lambda s, p: (s, 0, 0))
    grid = (SIDE, rows, PITCH, D)
    out = jax.ShapeDtypeStruct((*shards, D // chunks), BF)
    shapes = [
        jax.ShapeDtypeStruct((tokens, D), BF),
        jax.ShapeDtypeStruct((tokens, D), F32),
        jax.ShapeDtypeStruct(grid, BF),
        jax.ShapeDtypeStruct((blocks, chunks, depth, 2 * D), BF),
        out, out,
        jax.ShapeDtypeStruct((8, D), F32),
        jax.ShapeDtypeStruct((chunks, 1, D), F32),
    ]
    specs = [whole(s.shape) for s in shapes]
    specs[3] = pl.BlockSpec((blocks, None, depth, 2 * D), lambda s, p: (0, s, 0, 0))
    specs[7] = line
    return pl.pallas_call(
        partial(feed_body, rows=rows),
        grid_spec=pltpu.PrefetchScalarGridSpec(
            num_scalar_prefetch=1,
            grid=(chunks,),
            in_specs=[
                whole(grid), whole((tokens, D)), whole((tokens, D)), whole((8, D)), line,
                pl.BlockSpec(memory_space=pl.ANY),
            ],
            out_specs=specs,
            scratch_shapes=[
                pltpu.VMEM((256 // GRID, GRID + PITCH, D), F32),
                pltpu.VMEM((tokens, D), BF),
                pltpu.VMEM((tokens, D), BF),
                pltpu.VMEM((D, tokens), BF),
                pltpu.VMEM((D, tokens), BF),
                pltpu.VMEM((tokens, D), F32),
                pltpu.VMEM((tokens, D), F32),
                pltpu.VMEM((tokens, D), F32),
                pltpu.VMEM((tokens, D), BF),
                pltpu.VMEM((tokens, D), BF),
                pltpu.VMEM((D, D), BF),
                pltpu.VMEM((2, blocks, depth, D), BF),
                pltpu.VMEM((2, blocks, depth, D), BF),
                pltpu.VMEM((blocks, chunks, depth, 256), BF),
                pltpu.SemaphoreType.DMA((3, 2)),
            ],
        ),
        out_shape=shapes,
        compiler_params=pltpu.CompilerParams(vmem_limit_bytes=63 << 20),
        cost_estimate=guess(50),
        name="feed",
    )(place, o, x, g, vectors, up_bias, rest)


def finish_body(own_ref, head_ref, tail_ref, x_ref, dh_ref, vec_ref, out_ref, sum_ref, nat_ref, *, heads, tails):
    step = pl.program_id(0)

    @pl.when(step == 0)
    def _():
        sum_ref[...] = jnp.zeros_like(sum_ref)

    has_head = step < heads
    has_tail = step >= pl.num_programs(0) - tails
    for i in range(own_ref.shape[1]):
        for b in range(SIDE):
            grad = own_ref[b, i] + jnp.where(has_head, head_ref[b, i].astype(F32), 0.0)
            grad = grad + jnp.where(has_tail, tail_ref[b, i].astype(F32), 0.0)
            nat_ref[i, WIN * b : WIN * b + PITCH, :] = grad
        grad = nat_ref[i, 0:GRID, :]
        hat, inverse = norm_parts(x_ref[i].astype(F32))
        out_ref[i] = (dh_ref[i] + norm_back(grad, hat, inverse, vec_ref[0:1])).astype(BF)
        sum_ref[0:1] += jnp.sum(grad * hat, 0, keepdims=True)
        sum_ref[1:2] += jnp.sum(grad, 0, keepdims=True)


def finish(own, head, tail, x, dh, vectors):
    rows, lines = own.shape[1], 4
    heads, tails = head.shape[1] // lines, tail.shape[1] // lines
    steps = rows // lines
    banded = lambda index: pl.BlockSpec((SIDE, lines, PITCH, D), lambda i: (0, index(i), 0, 0))
    plain = pl.BlockSpec((lines, GRID, D), lambda i: (i, 0, 0))
    return pl.pallas_call(
        partial(finish_body, heads=heads, tails=tails),
        grid=(steps,),
        in_specs=[
            banded(lambda i: i),
            banded(lambda i: jnp.minimum(i, heads - 1)),
            banded(lambda i: jnp.maximum(i - (steps - tails), 0)),
            plain, plain, whole(vectors.shape),
        ],
        out_specs=[plain, whole((8, D))],
        out_shape=[jax.ShapeDtypeStruct((rows, GRID, D), BF), jax.ShapeDtypeStruct((8, D), F32)],
        scratch_shapes=[pltpu.VMEM((lines, GRID + PITCH, D), F32)],
        compiler_params=pltpu.CompilerParams(vmem_limit_bytes=63 << 20),
        cost_estimate=guess(6),
        name="finish",
    )(own, head, tail, x, dh, vectors)


def fold_body(*refs, plan):
    terms = sum(count for count, *_ in plan)
    ins, outs = refs[:terms], refs[terms:]
    for (count, axis, index), out in zip(plan, outs):
        here, ins = ins[:count], ins[count:]
        lead = out.shape[:-2]
        for at in np.ndindex(*lead):
            spot = at if axis is None else at[:axis] + (index,) + at[axis:]
            total = here[0][spot].astype(F32)
            for ref in here[1:]:
                total = total + ref[spot].astype(F32)
            out[at] = total.astype(out.dtype)


def fold(*results):
    count = None
    args, in_specs, out_specs, shapes, plan = [], [], [], [], []
    for terms, z_axis, axis, index in results:
        shape = terms[0].shape
        count = shape[z_axis]
        block = tuple(None if i == z_axis else n for i, n in enumerate(shape))
        spec = pl.BlockSpec(block, lambda i, z_axis=z_axis, n=len(shape): tuple(i if k == z_axis else 0 for k in range(n)))
        args += terms
        in_specs += [spec] * len(terms)
        left = [n for i, n in enumerate(shape) if i != axis]
        z_left = z_axis if axis is None or axis > z_axis else z_axis - 1
        block = tuple(None if i == z_left else n for i, n in enumerate(left))
        out_specs.append(
            pl.BlockSpec(block, lambda i, z_left=z_left, n=len(left): tuple(i if k == z_left else 0 for k in range(n)))
        )
        shapes.append(jax.ShapeDtypeStruct(tuple(left), BF))
        inner = None if axis is None else (axis if axis < z_axis else axis - 1)
        plan.append((len(terms), inner, index))
    size = sum(2 * int(np.prod(a.shape)) for a in args)
    return pl.pallas_call(
        partial(fold_body, plan=plan),
        grid=(count,),
        in_specs=in_specs,
        out_specs=out_specs,
        out_shape=shapes,
        compiler_params=pltpu.CompilerParams(vmem_limit_bytes=63 << 20),
        cost_estimate=guess(1 + size / 2e6),
        name="fold",
    )(*args)


AXES = ("z", "x", "y", "c")
SWAP = [(0, 1), (1, 0)]


def swap(value, axis):
    return lax.ppermute(value, axis, SWAP)


def shift(value, count, by):
    return lax.ppermute(value, "z", [(i, (i + by) % count) for i in range(count)])


def spread_plane(shard, count):
    half = shard.shape[0] // 2
    lines = [shard] + [shift(shard, count, k) for k in range(1, count)]
    first = jnp.stack([line[:half] for line in lines])
    second = jnp.stack([line[half:] for line in lines])
    first_x, second_y = swap(first, "x"), swap(second, "y")
    return [
        first, swap(first, "y"), first_x, swap(first_x, "y"),
        second, second_y, swap(second, "x"), swap(second_y, "x"),
    ]


def after(value, *others):
    return lax.optimization_barrier((value, *others))


def along_z(pieces):
    count = pieces.shape[0]
    total = pieces[0].astype(F32)
    for k in range(1, count):
        total = total + shift(pieces[k], count, k).astype(F32)
    return total


def sum_all(value, count, fast):
    for axis in ("c", "y", "x"):
        value = value + swap(value, axis)
    if not fast:
        return lax.psum(value, "z")
    step = 1
    while step < count:
        value = value + lax.ppermute(value, "z", [(i, i ^ step) for i in range(count)])
        step *= 2
    return value


def body(
    features, first_gain, first_shift, qkv_weight, qv_bias, rel_height, rel_width, output_weight,
    output_bias, second_gain, second_shift, up_weight, up_bias, down_weight, down_bias, cotangent,
    *, count,
):
    depth, _, width = qkv_weight.shape
    hidden = up_weight.shape[1]
    tokens = features.shape[0]
    rows = tokens // GRID
    slots = 4
    fast = count <= 4 and depth % 32 == 0
    z, x, y, c = (lax.axis_index(a).astype(jnp.int32) for a in AXES)
    slot = 2 * y + c
    nought = jnp.zeros((), jnp.int32)
    place = jnp.stack([slot, z, x, y, c, y] if fast else [slot] + [nought] * 4 + [y])
    shards = (2, count, 2, depth)
    above, below = 2 * (slots - 1), WIN - 2

    grid_x = features.reshape(rows, GRID, D)
    pair = ("y", "c")
    up_pairs = [(s, s + 1) for s in range(slots - 1)]
    down_pairs = [(s + 1, s) for s in range(slots - 1)]
    from_above = lax.ppermute(grid_x[rows - above :], pair, up_pairs)
    from_below = lax.ppermute(grid_x[:below], pair, down_pairs)

    rest = jnp.concatenate([up_weight, down_weight, output_weight, jnp.zeros((depth, 256 - width), BF)], 1)
    rest_all = lax.all_gather(rest, AXES, axis=0).reshape(2 * count, slots, depth, 2 * hidden + 256)
    biases = jnp.concatenate([qv_bias.reshape(-1), up_bias])
    biases = jnp.where(jnp.arange(slots)[:, None] == slot, biases[None], jnp.zeros((), BF))
    biases = biases + swap(biases, "c")
    biases = (biases + swap(biases, "y")).astype(F32)
    qv_all = biases[:, : 2 * width].reshape(slots, 2, width).transpose(1, 0, 2).reshape(2, D)
    up_bias_all = biases[:, 2 * width :].reshape(slots, 1, hidden)

    vec_one = jnp.concatenate([first_gain[None], first_shift[None], jnp.zeros((6, D), BF)], 0).astype(F32)
    normed, turned, turned_own = windows(place, from_above, grid_x, from_below, vec_one)
    if fast:
        pieces = spread_plane(qkv_weight.reshape(depth, 3 * width), count)
        normed, pieces[3], pieces[7] = after(normed, pieces[3], pieces[7])
        pieces += [swap(piece, "c") for piece in pieces]
    else:
        full = lax.all_gather(qkv_weight, AXES, axis=0).reshape(2 * count, slots, depth, 3, width)
        pieces = [full.transpose(0, 2, 3, 1, 4).reshape(D, 3 * D)]
    q, k, v, weight = project(place, normed, pieces, qv_all, rows, depth)
    ahead, back = score_tables()
    rel_ahead, rel_back = offset_tables(rel_height, rel_width)
    attended, probs = attend(place, q, k, v, rel_ahead.T, jnp.asarray(ahead, BF), rows)

    vec_two = jnp.concatenate(
        [output_bias[None], second_gain[None], second_shift[None], down_bias[None], jnp.zeros((4, D), BF)], 0
    ).astype(F32)
    (
        output, grad_hidden, grad_out, grad_feed, out_send, out_keep, grad_vec, grad_up_bias,
    ) = feed(
        place, attended.reshape(SIDE, rows, PITCH, D), features, cotangent, rest_all, vec_two, up_bias_all,
        rows, shards,
    )
    grad_windows = grad_out.reshape(-1, D)
    table = jnp.asarray(back.transpose(0, 2, 1), BF)
    grad_feed = lax.psum_scatter(
        grad_feed.reshape(8 * count, depth, 2 * hidden), AXES, scatter_dimension=0
    ).astype(F32)
    grad_up, grad_down = grad_feed[:, :hidden], grad_feed[:, hidden:]
    if fast:
        out_got = swap(out_send, "c")
    *half0, drel0 = attend_back(place, q, k, v, probs, grad_windows, rel_back, table, rows, 0)
    first_send, first_keep, first_bias = project_grad(place, turned, turned_own, *half0, shards)
    if fast:
        first_got = swap(first_send, "c")
    *half1, drel1 = attend_back(place, q, k, v, probs, grad_windows, rel_back, table, rows, 1)
    if fast:
        first, out = [first_keep, first_got], [out_keep, out_got]
        first_away, first_here, out_away, out_here = fold(
            (first, 0, 1, 1), (first, 0, 1, 0), (out, 1, 2, 1), (out, 1, 2, 0)
        )
        place, first_away, out_away = after(place, first_away, out_away)
        first_got, out_got = swap(first_away, "x"), swap(out_away, "x")
    dqs, dks, dvs = zip(half0, half1)
    to_above, total, to_below = project_back(place, dqs, dks, dvs, weight, rows)
    place, to_above, to_below = after(place, to_above, to_below)
    from_below = lax.ppermute(to_above, pair, down_pairs)
    from_above = lax.ppermute(to_below, pair, up_pairs)
    last_send, last_keep, last_bias = project_grad(place, turned, turned_own, *half1, shards)
    if fast:
        last_got = swap(last_send, "c")
    grad_features, sums_one = finish(
        total, from_above, from_below, grid_x, grad_hidden.reshape(rows, GRID, D), vec_one
    )
    if fast:
        sums_one, last_got = after(sums_one, last_got)
        last = [last_keep, last_got]
        away, here = fold((last, 0, 1, 1), (last, 0, 1, 0))
        got = swap(away, "x")
        crossing, out_away, out_here = fold(
            ([first_here, first_got], 0, None, None), ([out_here, out_got], 1, 0, 1), ([out_here, out_got], 1, 0, 0)
        )
        crossing, out_away, sums_one = after(crossing, out_away, sums_one)
        crossing, out_got = swap(crossing, "y"), swap(out_away, "y")
        last, out = fold(([here, got, crossing], 0, None, None), ([out_here, out_got], 0, None, None))
        grad_qkv, grad_wo = along_z(last), along_z(out)
    else:
        pairs = [
            (out_send, out_keep),
            [
                jnp.where(y == 0, jnp.stack([last, first]), jnp.stack([first, last]))
                for first, last in ((first_send, last_send), (first_keep, last_keep))
            ],
        ]
        grad_wo, grad_qkv = [
            lax.psum_scatter(
                jnp.stack([keep, send], 3).transpose(1, 2, 0, 3, 4, 5).reshape(8 * count, depth, -1),
                AXES, scatter_dimension=0,
            ).astype(F32)
            for send, keep in pairs
        ]
    drel = (drel0 + drel1).T.reshape(4, 64, 128)
    drel = drel[1, :, :HD] + drel[2, :, HD:]
    grad_qv = jnp.where(y == 0, jnp.concatenate([last_bias, first_bias], 1), jnp.concatenate([first_bias, last_bias], 1))
    small = jnp.concatenate(
        [grad_vec[:4], grad_up_bias.reshape(slots, hidden), sums_one[:2], grad_qv], 0
    )
    small = sum_all(jnp.concatenate([small.reshape(-1), drel.reshape(-1)]).reshape(-1, 512), count, fast).reshape(-1)
    vec = small[: 12 * D].reshape(12, D)
    drel = small[12 * D :].reshape(64, HD)
    qv = lax.dynamic_index_in_dim(vec[10:12].reshape(2, slots, width), slot, 1, keepdims=False)
    bias = lax.dynamic_index_in_dim(vec[4:8], slot, 0, keepdims=False)
    return (
        output,
        grad_features.reshape(tokens, D),
        vec[8],
        vec[9],
        grad_qkv.reshape(depth, 3, width),
        qv,
        drel[0:OFFS],
        drel[32 : 32 + OFFS],
        grad_wo,
        vec[2],
        vec[0],
        vec[1],
        grad_up,
        bias,
        grad_down,
        vec[3],
    )


def solution(mesh):
    token = P(AXES, None)
    square = P(("z", "x"), ("y", "c"))
    cube = P(("z", "x"), None, ("y", "c"))
    lane = P(("y", "c"))
    count = mesh.shape["dp"] // 2
    assert mesh.shape["tensor"] == 4
    return jax.shard_map(
        partial(body, count=count),
        mesh=jax.sharding.Mesh(mesh.devices.reshape(count, 2, 2, 2), AXES),
        in_specs=(
            token, P(), P(), cube, P(None, ("y", "c")), P(), P(), square, P(), P(), P(), square,
            lane, square, P(), token,
        ),
        out_specs=(
            token, token, P(), P(), cube, P(None, ("y", "c")), P(), P(), square, P(), P(), P(), square,
            lane, square, P(),
        ),
        check_vma=False,
    )
```

```python
from functools import partial
import math

import jax
import jax.numpy as jnp
from jax import lax
from jax.experimental import pallas as pl
from jax.experimental.pallas import tpu as pltpu
from jax.sharding import PartitionSpec as P
import numpy as np

D = 768
HD = 64
GRID = 64
WIN = 14
SIDE = 5
PITCH = 16
KEYS = WIN * PITCH
EXT = 2 * WIN
PAIRS = D // (2 * HD)
OFFS = 2 * WIN - 1
EPSILON = 1e-06
FAR = -1e30
BF = jnp.bfloat16
F32 = jnp.float32
HIGH = lax.Precision.HIGHEST


def mm(left, right):
    return jnp.dot(left, right, preferred_element_type=F32)


def mm_t(left, right):
    return lax.dot_general(left, right, (((1,), (1,)), ((), ())), preferred_element_type=F32)


def t_mm(left, right):
    return lax.dot_general(left, right, (((0,), (0,)), ((), ())), preferred_element_type=F32)


def norm_parts(value):
    centered = value - jnp.mean(value, -1, keepdims=True)
    inverse = lax.rsqrt(jnp.mean(centered * centered, -1, keepdims=True) + EPSILON)
    return centered * inverse, inverse


def norm_back(upstream, hat, inverse, gain):
    scaled = upstream * gain
    return inverse * (
        scaled
        - jnp.mean(scaled, -1, keepdims=True)
        - hat * jnp.mean(scaled * hat, -1, keepdims=True)
    )


def score_tables():
    ahead = np.zeros((2, KEYS, 128), np.float32)
    back = np.zeros((2, KEYS, 128), np.float32)
    for head in range(2):
        base = 64 - 64 * head
        for c in range(WIN):
            for e in range(PITCH):
                k = c * PITCH + e
                if e >= WIN:
                    ahead[head, k, base] = FAR
                    continue
                ahead[head, k, base + 15 + c] = 1
                ahead[head, k, base + 1 + c] = 1
                ahead[head, k, base + 46 + e] = 1
                ahead[head, k, base + 32 + e] = 1
                back[head, k, base + WIN - 1 - c] = 1
                back[head, k, base + 32 + WIN - 1 - e] = 1
    return ahead, back


def offset_tables(rel_height, rel_width):
    def place(first, second, at_rows, at_cols):
        slab = jnp.zeros((64, HD), BF)
        slab = slab.at[at_rows : at_rows + OFFS].set(first)
        slab = slab.at[at_cols : at_cols + OFFS].set(second)
        low = jnp.concatenate([slab, jnp.zeros_like(slab)], 1)
        high = jnp.concatenate([jnp.zeros_like(slab), slab], 1)
        return jnp.concatenate([jnp.zeros_like(low), low, high, jnp.zeros_like(high)], 0)

    through = jnp.eye(HD, dtype=BF) * BF(HD ** (-0.5))
    nothing = jnp.zeros_like(through)
    through = jnp.concatenate(
        [jnp.concatenate([through, nothing], 1), jnp.zeros((128, 128), BF), jnp.concatenate([nothing, through], 1)], 0
    )
    return (
        place(rel_height[::-1], rel_width[::-1], 2, 33) + through,
        place(rel_height, rel_width, 0, 32),
    )


def whole(shape):
    return pl.BlockSpec(shape, lambda *_: (0,) * len(shape), pipeline_mode=pl.Buffered(1))


def windows_body(place_ref, above_ref, x_ref, below_ref, vec_ref, nw_ref, nat_ref, *, rows):
    band = pl.program_id(0)
    slot = place_ref[0]
    above, below = above_ref.shape[0], below_ref.shape[0]

    @pl.when(band == 0)
    def _():
        def normed(piece):
            hat, _ = norm_parts(piece.astype(F32))
            return hat * vec_ref[0:1] + vec_ref[1:2]

        def clear(i, carry):
            nat_ref[i, GRID : GRID + PITCH, :] = jnp.zeros((PITCH, D), F32)
            return carry

        def own(i, carry):
            nat_ref[2 * slot + i, 0:GRID, :] = normed(x_ref[i])
            return carry

        def before(i, carry):
            nat_ref[i, 0:GRID, :] = normed(above_ref[above - 2 * slot + i])
            return carry

        def after(i, carry):
            at = 2 * slot + rows + i
            inside = WIN * slot + at < GRID
            nat_ref[at, 0:GRID, :] = jnp.where(inside, normed(below_ref[i]), 0.0)
            return carry

        lax.fori_loop(0, EXT, clear, 0, unroll=4)
        lax.fori_loop(0, rows, own, 0, unroll=2)
        lax.fori_loop(0, 2 * slot, before, 0)
        lax.fori_loop(0, EXT - rows - 2 * slot, after, 0)

    keep = lax.broadcasted_iota(jnp.int32, (PITCH, D), 0) < WIN
    for b in range(SIDE):
        @pl.when(band == b)
        def _(b=b):
            def one(i, carry):
                piece = nat_ref[i, WIN * b : WIN * b + PITCH, :]
                start = pl.multiple_of(i * PITCH, PITCH)
                nw_ref[pl.ds(start, PITCH), :] = jnp.where(keep, piece, 0.0).astype(BF)
                return carry

            lax.fori_loop(0, EXT, one, 0, unroll=4)


def windows(place, above, x, below, vectors):
    rows = x.shape[0]
    return pl.pallas_call(
        partial(windows_body, rows=rows),
        grid_spec=pltpu.PrefetchScalarGridSpec(
            num_scalar_prefetch=1,
            grid=(SIDE,),
            in_specs=[whole(above.shape), whole(x.shape), whole(below.shape), whole((8, D))],
            out_specs=pl.BlockSpec((EXT * PITCH, D), lambda b, s: (b, 0)),
            scratch_shapes=[pltpu.VMEM((EXT, GRID + PITCH, D), F32)],
        ),
        out_shape=jax.ShapeDtypeStruct((SIDE * EXT * PITCH, D), BF),
        compiler_params=pltpu.CompilerParams(vmem_limit_bytes=63 << 20),
        cost_estimate=guess(8),
        name="windows",
    )(place, above, x, below, vectors)


def project_body(place_ref, nw_ref, *refs, rows, depth):
    *pieces, bias_ref, q_ref, k_ref, v_ref, w_ref, turned_ref, turned_own_ref, stage_ref = refs
    slot, z, x, y, c = (place_ref[i] for i in range(5))
    width = D // 4

    @pl.when(pl.program_id(0) == 0)
    def _():
        if len(pieces) == 1:
            w_ref[...] = pieces[0][...]
            return
        half = depth // 2
        for index, ref in enumerate(pieces):
            sibling, part, dx, dy = index // 8, index // 4 % 2, index // 2 % 2, index % 2
            count = ref.shape[0]
            from_slot = (y ^ dy) * 2 + (c ^ sibling)
            for dz in range(count):
                group = lax.rem(z - dz + count, count) * 2 + (x ^ dx)
                at = pl.multiple_of(group * depth + part * half, half)
                stage_ref[from_slot, pl.ds(at, half), :] = ref[dz]

        def join(i, carry):
            at = pl.ds(pl.multiple_of(i * 64, 64), 64)
            for kind in range(3):
                w_ref[at, kind * D : (kind + 1) * D] = jnp.concatenate(
                    [stage_ref[t, at, kind * width : (kind + 1) * width] for t in range(4)], 1
                )
            return carry

        lax.fori_loop(0, D // 64, join, 0)

    normed = nw_ref[...]
    own = nw_ref[pl.ds(pl.multiple_of(slot * 2 * PITCH, 2 * PITCH), rows * PITCH), :]
    q_ref[...] = (mm(own, w_ref[:, 0:D]) + bias_ref[0:1]).astype(BF)
    k_ref[...] = mm(normed, w_ref[:, D : 2 * D]).astype(BF)
    v_ref[...] = (mm(normed, w_ref[:, 2 * D :]) + bias_ref[1:2]).astype(BF)
    turned_ref[...] = normed.T
    turned_own_ref[...] = own.T


def guess(us):
    return pl.CostEstimate(flops=int(us * 1.1e9), bytes_accessed=int(us * 3e6), transcendentals=0)


def project(place, normed, pieces, bias, rows, depth):
    of_k = pl.BlockSpec((EXT * PITCH, D), lambda b, s: (b, 0))
    of_q = pl.BlockSpec((rows * PITCH, D), lambda b, s: (b, 0))
    keys = jax.ShapeDtypeStruct((SIDE * EXT * PITCH, D), BF)
    return pl.pallas_call(
        partial(project_body, rows=rows, depth=depth),
        grid_spec=pltpu.PrefetchScalarGridSpec(
            num_scalar_prefetch=1,
            grid=(SIDE,),
            in_specs=[of_k] + [whole(p.shape) for p in pieces] + [whole((2, D))],
            out_specs=[
                of_q, of_k, of_k, whole((D, 3 * D)),
                pl.BlockSpec((None, D, EXT * PITCH), lambda b, s: (b, 0, 0)),
                pl.BlockSpec((None, D, rows * PITCH), lambda b, s: (b, 0, 0)),
            ],
            scratch_shapes=[pltpu.VMEM((4, D, 3 * D // 4), BF)],
        ),
        out_shape=[
            jax.ShapeDtypeStruct((SIDE * rows * PITCH, D), BF), keys, keys,
            jax.ShapeDtypeStruct((D, 3 * D), BF),
            jax.ShapeDtypeStruct((SIDE, D, EXT * PITCH), BF),
            jax.ShapeDtypeStruct((SIDE, D, rows * PITCH), BF),
        ],
        compiler_params=pltpu.CompilerParams(vmem_limit_bytes=63 << 20),
        cost_estimate=guess(18),
        name="project",
    )(place, normed, *pieces, bias)


def store_shards(place_ref, refs, value, first=0):
    z, x = place_ref[1], place_ref[2]
    count, _, depth = refs.shape[:3]
    if depth % 32:
        refs[...] = value.reshape(refs.shape)
        return
    for zd in range(value.shape[0] // (2 * depth)):
        for xd in range(2):
            start = (zd * 2 + xd) * depth
            refs[lax.rem(first + zd - z + count, count), x ^ xd] = value[start : start + depth]


def project_grad_body(place_ref, turned_ref, own_ref, dq_ref, dk_ref, dv_ref, send_ref, keep_ref, bias_ref, *, parts):
    step = pl.program_id(0)
    c = place_ref[4]
    width = D // 4

    @pl.when(step == 0)
    def _():
        bias_ref[0:1] = jnp.sum(dq_ref[...].astype(F32), 0, keepdims=True)
        bias_ref[1:2] = jnp.sum(dv_ref[...].astype(F32), 0, keepdims=True)

    def over_bands(left, right):
        lines = left.shape[2]
        return sum(mm(left[b], right(slice(b * lines, (b + 1) * lines))) for b in range(SIDE)).astype(BF)

    both = over_bands(turned_ref, lambda at: jnp.concatenate([dk_ref[at], dv_ref[at]], 1))
    grads = [over_bands(own_ref, lambda at: dq_ref[at]), both[:, : D // 2], both[:, D // 2 :]]
    first = step * (keep_ref.shape[0] // parts)
    for core in range(2):
        value = jnp.concatenate([g[:, core * width : (core + 1) * width] for g in grads], 1)
        for sibling, ref in ((1, send_ref), (0, keep_ref)):
            @pl.when(c ^ core == sibling)
            def _(ref=ref, value=value):
                store_shards(place_ref, ref, value, first)


def project_grad(place, turned, own, dq, dk, dv, shards):
    count, depth = shards[1], shards[3]
    parts = 2 if depth % 32 == 0 else 1
    out = jax.ShapeDtypeStruct((count, 2, depth, 3 * D // 4), BF)
    return pl.pallas_call(
        partial(project_grad_body, parts=parts),
        grid_spec=pltpu.PrefetchScalarGridSpec(
            num_scalar_prefetch=1,
            grid=(parts,),
            in_specs=[
                pl.BlockSpec((SIDE, D // parts, turned.shape[2]), lambda i, s: (0, i, 0)),
                pl.BlockSpec((SIDE, D // parts, own.shape[2]), lambda i, s: (0, i, 0)),
                whole(dq.shape), whole(dk.shape), whole(dv.shape),
            ],
            out_specs=[whole(out.shape), whole(out.shape), whole((2, D // 2))],
        ),
        out_shape=[out, out, jax.ShapeDtypeStruct((2, D // 2), F32)],
        compiler_params=pltpu.CompilerParams(vmem_limit_bytes=63 << 20),
        cost_estimate=guess(6),
        name="project_grad",
    )(place, turned, own, dq, dk, dv)


def project_back_body(place_ref, *refs, rows):
    dqs, dks, dvs = refs[0:2], refs[2:4], refs[4:6]
    w_ref, above_ref, own_ref, below_ref, all_ref, dq_ref, dk_ref, dv_ref = refs[6:]
    slot, y = place_ref[0], place_ref[5]
    above, below = above_ref.shape[0], below_ref.shape[0]
    for halves, ref in ((dqs, dq_ref), (dks, dk_ref), (dvs, dv_ref)):
        for i in range(2):
            at = pl.multiple_of((y ^ (1 - i)) * (D // 2), D // 2)
            ref[:, pl.ds(at, D // 2)] = halves[i][...]
    grad = mm_t(dk_ref[...], w_ref[:, D : 2 * D]) + mm_t(dv_ref[...], w_ref[:, 2 * D :])
    direct = mm_t(dq_ref[...], w_ref[:, 0:D]).reshape(rows, PITCH, D)
    all_ref[0:above] = jnp.zeros((above, PITCH, D), F32)
    all_ref[above + rows :] = jnp.zeros((below, PITCH, D), F32)
    all_ref[pl.ds(above - 2 * slot, EXT)] = grad.reshape(EXT, PITCH, D)
    above_ref[...] = all_ref[0:above].astype(BF)
    own_ref[...] = all_ref[above : above + rows] + direct
    below_ref[...] = all_ref[above + rows :].astype(BF)


def project_back(place, dqs, dks, dvs, weight, rows):
    above, below = 8, WIN - 2
    of_k = pl.BlockSpec((EXT * PITCH, D // 2), lambda b, s: (b, 0))
    of_q = pl.BlockSpec((rows * PITCH, D // 2), lambda b, s: (b, 0))
    part = lambda n: pl.BlockSpec((None, n, PITCH, D), lambda b, s: (b, 0, 0, 0))
    return pl.pallas_call(
        partial(project_back_body, rows=rows),
        grid_spec=pltpu.PrefetchScalarGridSpec(
            num_scalar_prefetch=1,
            grid=(SIDE,),
            in_specs=[of_q, of_q, of_k, of_k, of_k, of_k, whole((D, 3 * D))],
            out_specs=[part(above), part(rows), part(below)],
            scratch_shapes=[
                pltpu.VMEM((above + rows + below, PITCH, D), F32),
                pltpu.VMEM((rows * PITCH, D), BF),
                pltpu.VMEM((EXT * PITCH, D), BF),
                pltpu.VMEM((EXT * PITCH, D), BF),
            ],
        ),
        out_shape=[
            jax.ShapeDtypeStruct((SIDE, above, PITCH, D), BF),
            jax.ShapeDtypeStruct((SIDE, rows, PITCH, D), F32),
            jax.ShapeDtypeStruct((SIDE, below, PITCH, D), BF),
        ],
        compiler_params=pltpu.CompilerParams(vmem_limit_bytes=63 << 20),
        cost_estimate=guess(10),
        name="project_back",
    )(place, *dqs, *dks, *dvs, weight)


def head_lanes(shape, head):
    lane = lax.broadcasted_iota(jnp.int32, shape, 1)
    return lane < HD if head == 0 else lane >= HD


def early_window(slot, rows):
    return (WIN - 2 * slot) * PITCH - rows * PITCH // 2


def lanes_of(pair):
    return slice(128 * pair, 128 * pair + 128)


def attend_body(place_ref, q_ref, k_ref, v_ref, rel_ref, tab_ref, o_ref, p_ref, *, rows):
    slot = place_ref[0]
    half = rows * PITCH // 2
    lane = lax.broadcasted_iota(jnp.int32, (PITCH, 128), 1)
    first = lax.broadcasted_iota(jnp.int32, (1, half), 1) < early_window(slot, rows)
    turns = [lax.rem(2 * slot + r, WIN) for r in range(rows)]
    heads = [(pair, head) for pair in range(q_ref.shape[1] // 128) for head in range(2)]
    raws = [mm(q_ref[:, lanes_of(pair)], rel_ref[...]) for pair in range(len(heads) // 2)]

    def extended(pair, head):
        base = 64 - 64 * head
        one = jnp.where(lane == base, 1.0, 0.0)
        on_row = (lane >= base + 15) & (lane < base + 29)
        on_col = (lane >= base + 46) & (lane < base + 60)
        mine = head_lanes((PITCH, 128), head)
        parts = []
        for r in range(rows):
            here = raws[pair][r * PITCH : (r + 1) * PITCH, lanes_of(head)]
            along_row = pltpu.roll(here, turns[r], 1)
            along_col = pltpu.roll(here, 0, 1, stride=1, stride_axis=0)
            kept = jnp.where(mine, here, one)
            both = jnp.where(on_row, along_row, jnp.where(on_col, along_col, kept))
            high = both.astype(BF).astype(F32)
            parts.append((high + pltpu.roll(both - high, 114, 1)).astype(BF))
        return jnp.concatenate(parts, 0)

    def scored(pair, head, left):
        mine = head_lanes((KEYS, 128), head)
        keys_a = jnp.where(mine, k_ref[0:KEYS, lanes_of(pair)], tab_ref[head])
        keys_b = jnp.where(mine, k_ref[KEYS:, lanes_of(pair)], tab_ref[head])
        scores = mm_t(keys_a, left)
        return scores[:, :half], jnp.where(first, scores[:, half:], mm_t(keys_b, left[half:]))

    def softmax(pair, head, pieces):
        for i, piece in enumerate(pieces):
            grown = jnp.exp(piece - jnp.max(piece, 0, keepdims=True))
            probs = (grown * (1.0 / jnp.sum(grown, 0, keepdims=True))).astype(BF)
            p_ref[pair, head, :, i * half : (i + 1) * half] = probs

    def weighed(pair, head):
        rows_of = slice(HD * head, HD * head + HD)
        out = mm(v_ref[0:KEYS, lanes_of(pair)].T[rows_of], p_ref[pair, head])
        late = mm(v_ref[KEYS:, lanes_of(pair)].T[rows_of], p_ref[pair, head, :, half:])
        return jnp.concatenate([out[:, :half], jnp.where(first, out[:, half:], late)], 1)

    lefts = [extended(*h) for h in heads]
    scores = [scored(*h, left) for h, left in zip(heads, lefts)]
    for h, pieces in zip(heads, scores):
        softmax(*h, pieces)
    outs = [weighed(*h) for h in heads]
    for pair in range(len(heads) // 2):
        o_ref[:, lanes_of(pair)] = jnp.concatenate(outs[2 * pair : 2 * pair + 2], 0).T.astype(BF)


def attend(slot, q, k, v, rel, table, rows):
    queries = rows * PITCH
    many = PAIRS // 2
    of_k = pl.BlockSpec((EXT * PITCH, 128 * many), lambda b, p, s: (b, p))
    of_q = pl.BlockSpec((queries, 128 * many), lambda b, p, s: (b, p))
    return pl.pallas_call(
        partial(attend_body, rows=rows),
        grid_spec=pltpu.PrefetchScalarGridSpec(
            num_scalar_prefetch=1,
            grid=(SIDE, PAIRS // many),
            in_specs=[of_q, of_k, of_k, whole((128, 256)), whole((2, KEYS, 128))],
            out_specs=[
                of_q,
                pl.BlockSpec((many, 2, KEYS, queries), lambda b, p, s: (b * (PAIRS // many) + p, 0, 0, 0)),
            ],
        ),
        out_shape=[
            jax.ShapeDtypeStruct((SIDE * queries, D), BF),
            jax.ShapeDtypeStruct((SIDE * PAIRS, 2, KEYS, queries), BF),
        ],
        compiler_params=pltpu.CompilerParams(vmem_limit_bytes=63 << 20),
        cost_estimate=guess(24),
        name="attend",
    )(slot, q, k, v, rel, table)


def attend_back_body(
    place_ref, q_ref, k_ref, v_ref, p_ref, do_ref, rel_ref, tab_ref, dq_ref, dk_ref, dv_ref, drel_ref, *, rows,
):
    slot = place_ref[0]
    count = rows * PITCH
    half = count // 2
    early = early_window(slot, rows)

    @pl.when(pl.program_id(0) == 0)
    def _():
        drel_ref[...] = jnp.zeros_like(drel_ref)

    lane = lax.broadcasted_iota(jnp.int32, (PITCH, 128), 1)
    first = lax.broadcasted_iota(jnp.int32, (1, half), 1) < early
    turns = [lax.rem(2 * slot + r, WIN) for r in range(rows)]
    heads = [(pair, head) for pair in range(q_ref.shape[1] // 128) for head in range(2)]

    def split(value, head):
        spot = lax.broadcasted_iota(jnp.int32, (half, 128), 0)
        mine = head_lanes((half, 128), head)
        value = value.astype(F32)
        top = jnp.where(mine, value[:half], 0.0)
        mid = jnp.where(mine & (spot < early), value[half:], 0.0)
        low = jnp.where(mine & (spot >= early), value[half:], 0.0)
        return jnp.concatenate([top, mid], 0).astype(BF), low.astype(BF), (mid + low).astype(BF)

    def upstream(pair, head):
        return split(do_ref[:, lanes_of(pair)], head)

    def probs_grad(pair, head, out_a, late):
        whole_out = jnp.concatenate([out_a[:half], late], 0)
        grad = mm_t(v_ref[0:KEYS, lanes_of(pair)], whole_out)
        more = mm_t(v_ref[KEYS:, lanes_of(pair)], late)
        return grad[:, :half], jnp.where(first, grad[:, half:], more)

    def scores_grad(pair, head, pieces):
        grads = []
        for i, piece in enumerate(pieces):
            exact = p_ref[pair, head, :, i * half : (i + 1) * half].astype(F32)
            inner = jnp.sum(exact * piece, 0, keepdims=True)
            grads.append((exact * (piece - inner)).astype(BF))
        return jnp.concatenate(grads, 1)

    def left_grad(pair, head, grad, turned):
        spot = lax.broadcasted_iota(jnp.int32, (128, KEYS), 0)
        mine = spot < HD if head == 0 else spot >= HD
        left = mm(jnp.where(mine, turned[0], tab_ref[head]), grad)
        late = mm(jnp.where(mine, turned[1], tab_ref[head]), grad[:, half:])
        return jnp.concatenate([left[:, :half], jnp.where(first, left[:, half:], late)], 1).T

    def raw_grad(head, left):
        base = 64 - 64 * head
        on_row = (lane >= base) & (lane < base + WIN)
        on_col = (lane >= base + 32) & (lane < base + 32 + WIN)
        parts = []
        for r in range(rows):
            here = left[r * PITCH : (r + 1) * PITCH]
            along_row = pltpu.roll(jnp.where(on_row, here, 0.0), turns[r], 1)
            along_col = pltpu.roll(jnp.where(on_col, here, 0.0), 0, 1, stride=1, stride_axis=0)
            parts.append((along_row + along_col).astype(BF))
        return jnp.concatenate(parts, 0)

    outs = [upstream(*h) for h in heads]
    pieces = [probs_grad(*h, out[0], out[2]) for h, out in zip(heads, outs)]
    grads = [scores_grad(*h, piece) for h, piece in zip(heads, pieces)]
    lefts = []
    for pair in range(len(heads) // 2):
        turned = [k_ref[w * KEYS : (w + 1) * KEYS, lanes_of(pair)].T for w in range(2)]
        lefts += [left_grad(pair, head, grads[2 * pair + head], turned) for head in range(2)]
    for pair in range(len(heads) // 2):
        scaled = q_ref[:, lanes_of(pair)].astype(F32) * HD ** (-0.5)
        owns = [split(scaled, head) for head in range(2)]
        for w in range(2):
            at = (slice(w * KEYS, (w + 1) * KEYS), lanes_of(pair))
            part = slice(0, count) if w == 0 else slice(half, count)
            dv_ref[at] = sum(mm(p_ref[pair, h, :, part], outs[2 * pair + h][w]) for h in range(2)).astype(BF)
            dk_ref[at] = sum(mm(grads[2 * pair + h][:, part], owns[h][w]) for h in range(2)).astype(BF)
    for pair in range(len(heads) // 2):
        mine = lefts[2 * pair : 2 * pair + 2]
        raw = jnp.concatenate([raw_grad(head, mine[head]) for head in range(2)], 1)
        direct = jnp.where(head_lanes((count, 128), 0), *mine) * HD ** (-0.5)
        dq_ref[:, lanes_of(pair)] = (direct + mm(raw, rel_ref[...])).astype(BF)
        drel_ref[...] += t_mm(q_ref[:, lanes_of(pair)], raw)


def attend_back(slot, q, k, v, probs, grad_out, rel, table, rows, group):
    queries = rows * PITCH
    many = PAIRS // 2
    half = lambda s: s[5] ^ (1 - group)
    of_q = pl.BlockSpec((queries, 128 * many), lambda b, s: (b, half(s)))
    of_k = pl.BlockSpec((EXT * PITCH, 128 * many), lambda b, s: (b, half(s)))
    to_q = pl.BlockSpec((queries, 128 * many), lambda b, s: (b, 0))
    to_k = pl.BlockSpec((EXT * PITCH, 128 * many), lambda b, s: (b, 0))
    return pl.pallas_call(
        partial(attend_back_body, rows=rows),
        grid_spec=pltpu.PrefetchScalarGridSpec(
            num_scalar_prefetch=1,
            grid=(SIDE,),
            in_specs=[
                of_q, of_k, of_k,
                pl.BlockSpec((many, 2, KEYS, queries), lambda b, s: (b * 2 + half(s), 0, 0, 0)),
                of_q, whole((256, 128)), whole((2, 128, KEYS)),
            ],
            out_specs=[to_q, to_k, to_k, whole((128, 256))],
        ),
        out_shape=[
            jax.ShapeDtypeStruct((q.shape[0], D // 2), BF),
            jax.ShapeDtypeStruct((k.shape[0], D // 2), BF),
            jax.ShapeDtypeStruct((k.shape[0], D // 2), BF),
            jax.ShapeDtypeStruct((128, 256), F32),
        ],
        compiler_params=pltpu.CompilerParams(vmem_limit_bytes=63 << 20),
        cost_estimate=guess(16),
        name="attend_back",
    )(slot, q, k, v, probs, grad_out, rel, table)


def feed_body(place_ref, o_ref, x_ref, g_ref, vec_ref, bias_ref, rest_ref, *refs, rows):
    (
        out_ref, dh_ref, do_ref, grad_ref, gas_ref, gak_ref, gvec_ref, gbias_ref,
        nat_ref, onat_ref, n2_ref, n2t_ref, gt_ref, h_ref, y_ref, dn_ref, a_ref, du_ref, w_ref,
        up_ref, down_ref, slots_ref, sems,
    ) = refs
    step = pl.program_id(0)
    steps = rows * GRID // 256
    lines = 256 // GRID
    width = D // 4
    y, c = place_ref[3], place_ref[4]
    buffer = lax.rem(step, 2)

    def fetch(chunk, where):
        for i, ref in enumerate((up_ref, down_ref)):
            source = rest_ref.at[:, chunk, :, pl.ds(i * D, D)]
            pltpu.make_async_copy(source, ref.at[where], sems.at[where, i]).start()

    @pl.when(step == 0)
    def _():
        pltpu.make_async_copy(rest_ref.at[:, :, :, pl.ds(2 * D, 256)], slots_ref, sems.at[2, 0]).start()
        fetch(step, buffer)

    @pl.when(step < pl.num_programs(0) - 1)
    def _():
        fetch(step + 1, 1 - buffer)

    @pl.when(step == 0)
    def _():
        pltpu.make_async_copy(slots_ref, slots_ref, sems.at[2, 0]).wait()

        for t in range(4):
            w_ref[:, t * width : (t + 1) * width] = slots_ref[:, t, :, 0:width].reshape(D, width)

        def one(i, carry):
            at = pl.ds(pl.multiple_of(i * 256, 256), 256)
            for b in range(SIDE):
                piece = o_ref[b, pl.ds(i * lines, lines)]
                nat_ref[:, WIN * b : WIN * b + PITCH, :] = piece.astype(F32)
            natural = nat_ref[:, 0:GRID, :].reshape(256, D).astype(BF)
            onat_ref[at, :] = natural
            hidden = x_ref[at, :].astype(F32) + mm_t(natural, w_ref[...]) + vec_ref[0:1]
            h_ref[at, :] = hidden
            hat, _ = norm_parts(hidden)
            normed = (hat * vec_ref[1:2] + vec_ref[2:3]).astype(BF)
            n2_ref[at, :] = normed
            n2t_ref[:, at] = normed.T
            gt_ref[:, at] = g_ref[at, :].T
            y_ref[at, :] = jnp.zeros((256, D), F32)
            dn_ref[at, :] = jnp.zeros((256, D), F32)
            return carry

        lax.fori_loop(0, steps, one, 0, unroll=2)

    pltpu.make_async_copy(up_ref.at[buffer], up_ref.at[buffer], sems.at[buffer, 0]).wait()
    pltpu.make_async_copy(down_ref.at[buffer], down_ref.at[buffer], sems.at[buffer, 1]).wait()
    up, down = up_ref[buffer].reshape(D, D), down_ref[buffer].reshape(D, D)
    total = jnp.zeros((1, D), F32)

    def inward(i):
        at = slice(i * 512, i * 512 + 512)
        upper = mm(n2_ref[at, :], up) + bias_ref[...].reshape(1, D)
        cdf = 0.5 * (1.0 + lax.erf(upper * (1.0 / math.sqrt(2.0))))
        a_ref[at, :] = (upper * cdf).astype(BF)
        slope = cdf + upper * jnp.exp(-0.5 * upper * upper) * (1.0 / math.sqrt(2.0 * math.pi))
        delta = (mm(g_ref[at, :], down) * slope).astype(BF)
        du_ref[at, :] = delta
        return jnp.sum(delta.astype(F32), 0, keepdims=True)

    def outward(i):
        at = slice(i * 512, i * 512 + 512)
        y_ref[at, :] += mm_t(a_ref[at, :], down)
        dn_ref[at, :] += mm_t(du_ref[at, :], up)

    for i in range(rows * GRID // 512):
        total = total + inward(i)
        if i:
            outward(i - 1)
    outward(rows * GRID // 512 - 1)
    gbias_ref[...] = total.reshape(gbias_ref.shape)
    grad_up = mm(n2t_ref[...], du_ref[...]).astype(BF)
    grad_down = mm(gt_ref[...], a_ref[...]).astype(BF)
    shape = (grad_ref.shape[0], grad_ref.shape[1], D)
    grad_ref[:, :, 0:D] = grad_up.reshape(shape)
    grad_ref[:, :, D:] = grad_down.reshape(shape)

    @pl.when(step == pl.num_programs(0) - 1)
    def _():
        nat_ref[...] = jnp.zeros_like(nat_ref)
        gvec_ref[...] = jnp.zeros_like(gvec_ref)

        def three(i, carry):
            at = pl.ds(pl.multiple_of(i * 256, 256), 256)
            hidden = h_ref[at, :]
            grad = g_ref[at, :].astype(F32)
            hat, inverse = norm_parts(hidden)
            grad_normed = dn_ref[at, :]
            out_ref[at, :] = (hidden + y_ref[at, :] + vec_ref[3:4]).astype(BF)
            grad_hidden = grad + norm_back(grad_normed, hat, inverse, vec_ref[1:2])
            dh_ref[at, :] = grad_hidden
            branch = grad_hidden.astype(BF)
            n2_ref[at, :] = branch
            gvec_ref[0:1] += jnp.sum(grad_normed * hat, 0, keepdims=True)
            gvec_ref[1:2] += jnp.sum(grad_normed, 0, keepdims=True)
            gvec_ref[2:3] += jnp.sum(branch.astype(F32), 0, keepdims=True)
            gvec_ref[3:4] += jnp.sum(grad, 0, keepdims=True)
            grad_out = mm(branch, w_ref[...])
            nat_ref[:, 0:GRID, :] = grad_out.reshape(lines, GRID, D)
            keep = lax.broadcasted_iota(jnp.int32, (lines, PITCH, D), 1) < WIN
            for b in range(SIDE):
                piece = nat_ref[:, WIN * b : WIN * b + PITCH, :]
                do_ref[b, pl.ds(i * lines, lines)] = jnp.where(keep, piece, 0.0).astype(BF)
            return carry

        lax.fori_loop(0, steps, three, 0, unroll=2)
        grad_wo = t_mm(n2_ref[...], onat_ref[...]).astype(BF)
        for sibling, ref in ((1, gas_ref), (0, gak_ref)):
            for t in range(4):
                @pl.when(c ^ (t % 2) == sibling)
                def _(t=t, ref=ref):
                    store_shards(
                        place_ref, ref.at[y ^ (t // 2)], grad_wo[:, t * width : (t + 1) * width]
                    )


def feed(place, o, x, g, rest, vectors, up_bias, rows, shards):
    tokens = rows * GRID
    blocks, chunks, depth = rest.shape[:3]
    line = pl.BlockSpec((None, 1, D), lambda s, p: (s, 0, 0))
    grid = (SIDE, rows, PITCH, D)
    out = jax.ShapeDtypeStruct((*shards, D // chunks), BF)
    shapes = [
        jax.ShapeDtypeStruct((tokens, D), BF),
        jax.ShapeDtypeStruct((tokens, D), F32),
        jax.ShapeDtypeStruct(grid, BF),
        jax.ShapeDtypeStruct((blocks, chunks, depth, 2 * D), BF),
        out, out,
        jax.ShapeDtypeStruct((8, D), F32),
        jax.ShapeDtypeStruct((chunks, 1, D), F32),
    ]
    specs = [whole(s.shape) for s in shapes]
    specs[3] = pl.BlockSpec((blocks, None, depth, 2 * D), lambda s, p: (0, s, 0, 0))
    specs[7] = line
    return pl.pallas_call(
        partial(feed_body, rows=rows),
        grid_spec=pltpu.PrefetchScalarGridSpec(
            num_scalar_prefetch=1,
            grid=(chunks,),
            in_specs=[
                whole(grid), whole((tokens, D)), whole((tokens, D)), whole((8, D)), line,
                pl.BlockSpec(memory_space=pl.ANY),
            ],
            out_specs=specs,
            scratch_shapes=[
                pltpu.VMEM((256 // GRID, GRID + PITCH, D), F32),
                pltpu.VMEM((tokens, D), BF),
                pltpu.VMEM((tokens, D), BF),
                pltpu.VMEM((D, tokens), BF),
                pltpu.VMEM((D, tokens), BF),
                pltpu.VMEM((tokens, D), F32),
                pltpu.VMEM((tokens, D), F32),
                pltpu.VMEM((tokens, D), F32),
                pltpu.VMEM((tokens, D), BF),
                pltpu.VMEM((tokens, D), BF),
                pltpu.VMEM((D, D), BF),
                pltpu.VMEM((2, blocks, depth, D), BF),
                pltpu.VMEM((2, blocks, depth, D), BF),
                pltpu.VMEM((blocks, chunks, depth, 256), BF),
                pltpu.SemaphoreType.DMA((3, 2)),
            ],
        ),
        out_shape=shapes,
        compiler_params=pltpu.CompilerParams(vmem_limit_bytes=63 << 20),
        cost_estimate=guess(50),
        name="feed",
    )(place, o, x, g, vectors, up_bias, rest)


def finish_body(own_ref, head_ref, tail_ref, x_ref, dh_ref, vec_ref, out_ref, sum_ref, nat_ref, *, heads, tails):
    step = pl.program_id(0)

    @pl.when(step == 0)
    def _():
        sum_ref[...] = jnp.zeros_like(sum_ref)

    has_head = step < heads
    has_tail = step >= pl.num_programs(0) - tails
    for i in range(own_ref.shape[1]):
        for b in range(SIDE):
            grad = own_ref[b, i] + jnp.where(has_head, head_ref[b, i].astype(F32), 0.0)
            grad = grad + jnp.where(has_tail, tail_ref[b, i].astype(F32), 0.0)
            nat_ref[i, WIN * b : WIN * b + PITCH, :] = grad
        grad = nat_ref[i, 0:GRID, :]
        hat, inverse = norm_parts(x_ref[i].astype(F32))
        out_ref[i] = (dh_ref[i] + norm_back(grad, hat, inverse, vec_ref[0:1])).astype(BF)
        sum_ref[0:1] += jnp.sum(grad * hat, 0, keepdims=True)
        sum_ref[1:2] += jnp.sum(grad, 0, keepdims=True)


def finish(own, head, tail, x, dh, vectors):
    rows, lines = own.shape[1], 4
    heads, tails = head.shape[1] // lines, tail.shape[1] // lines
    steps = rows // lines
    banded = lambda index: pl.BlockSpec((SIDE, lines, PITCH, D), lambda i: (0, index(i), 0, 0))
    plain = pl.BlockSpec((lines, GRID, D), lambda i: (i, 0, 0))
    return pl.pallas_call(
        partial(finish_body, heads=heads, tails=tails),
        grid=(steps,),
        in_specs=[
            banded(lambda i: i),
            banded(lambda i: jnp.minimum(i, heads - 1)),
            banded(lambda i: jnp.maximum(i - (steps - tails), 0)),
            plain, plain, whole(vectors.shape),
        ],
        out_specs=[plain, whole((8, D))],
        out_shape=[jax.ShapeDtypeStruct((rows, GRID, D), BF), jax.ShapeDtypeStruct((8, D), F32)],
        scratch_shapes=[pltpu.VMEM((lines, GRID + PITCH, D), F32)],
        compiler_params=pltpu.CompilerParams(vmem_limit_bytes=63 << 20),
        cost_estimate=guess(6),
        name="finish",
    )(own, head, tail, x, dh, vectors)


def fold_body(*refs, plan):
    terms = sum(count for count, *_ in plan)
    ins, outs = refs[:terms], refs[terms:]
    for (count, axis, index), out in zip(plan, outs):
        here, ins = ins[:count], ins[count:]
        lead = out.shape[:-2]
        for at in np.ndindex(*lead):
            spot = at if axis is None else at[:axis] + (index,) + at[axis:]
            total = here[0][spot].astype(F32)
            for ref in here[1:]:
                total = total + ref[spot].astype(F32)
            out[at] = total.astype(out.dtype)


def fold(*results):
    count = None
    args, in_specs, out_specs, shapes, plan = [], [], [], [], []
    for terms, z_axis, axis, index in results:
        shape = terms[0].shape
        count = shape[z_axis]
        block = tuple(None if i == z_axis else n for i, n in enumerate(shape))
        spec = pl.BlockSpec(block, lambda i, z_axis=z_axis, n=len(shape): tuple(i if k == z_axis else 0 for k in range(n)))
        args += terms
        in_specs += [spec] * len(terms)
        left = [n for i, n in enumerate(shape) if i != axis]
        z_left = z_axis if axis is None or axis > z_axis else z_axis - 1
        block = tuple(None if i == z_left else n for i, n in enumerate(left))
        out_specs.append(
            pl.BlockSpec(block, lambda i, z_left=z_left, n=len(left): tuple(i if k == z_left else 0 for k in range(n)))
        )
        shapes.append(jax.ShapeDtypeStruct(tuple(left), BF))
        inner = None if axis is None else (axis if axis < z_axis else axis - 1)
        plan.append((len(terms), inner, index))
    size = sum(2 * int(np.prod(a.shape)) for a in args)
    return pl.pallas_call(
        partial(fold_body, plan=plan),
        grid=(count,),
        in_specs=in_specs,
        out_specs=out_specs,
        out_shape=shapes,
        compiler_params=pltpu.CompilerParams(vmem_limit_bytes=63 << 20),
        cost_estimate=guess(1 + size / 2e6),
        name="fold",
    )(*args)


AXES = ("z", "x", "y", "c")
SWAP = [(0, 1), (1, 0)]


def swap(value, axis):
    return lax.ppermute(value, axis, SWAP)


def shift(value, count, by):
    return lax.ppermute(value, "z", [(i, (i + by) % count) for i in range(count)])


def spread_plane(shard, count):
    half = shard.shape[0] // 2
    lines = [shard] + [shift(shard, count, k) for k in range(1, count)]
    first = jnp.stack([line[:half] for line in lines])
    second = jnp.stack([line[half:] for line in lines])
    first_x, second_y = swap(first, "x"), swap(second, "y")
    return [
        first, swap(first, "y"), first_x, swap(first_x, "y"),
        second, second_y, swap(second, "x"), swap(second_y, "x"),
    ]


def after(value, *others):
    return lax.optimization_barrier((value, *others))


def along_z(pieces):
    count = pieces.shape[0]
    total = pieces[0].astype(F32)
    for k in range(1, count):
        total = total + shift(pieces[k], count, k).astype(F32)
    return total


def sum_all(value, count, fast):
    for axis in ("c", "y", "x"):
        value = value + swap(value, axis)
    if not fast:
        return lax.psum(value, "z")
    step = 1
    while step < count:
        value = value + lax.ppermute(value, "z", [(i, i ^ step) for i in range(count)])
        step *= 2
    return value


def body(
    features, first_gain, first_shift, qkv_weight, qv_bias, rel_height, rel_width, output_weight,
    output_bias, second_gain, second_shift, up_weight, up_bias, down_weight, down_bias, cotangent,
    *, count,
):
    depth, _, width = qkv_weight.shape
    hidden = up_weight.shape[1]
    tokens = features.shape[0]
    rows = tokens // GRID
    slots = 4
    fast = count <= 4 and depth % 32 == 0
    z, x, y, c = (lax.axis_index(a).astype(jnp.int32) for a in AXES)
    slot = 2 * y + c
    nought = jnp.zeros((), jnp.int32)
    place = jnp.stack([slot, z, x, y, c, y] if fast else [slot] + [nought] * 4 + [y])
    shards = (2, count, 2, depth)
    above, below = 2 * (slots - 1), WIN - 2

    grid_x = features.reshape(rows, GRID, D)
    pair = ("y", "c")
    up_pairs = [(s, s + 1) for s in range(slots - 1)]
    down_pairs = [(s + 1, s) for s in range(slots - 1)]
    from_above = lax.ppermute(grid_x[rows - above :], pair, up_pairs)
    from_below = lax.ppermute(grid_x[:below], pair, down_pairs)

    rest = jnp.concatenate([up_weight, down_weight, output_weight, jnp.zeros((depth, 256 - width), BF)], 1)
    rest_all = lax.all_gather(rest, AXES, axis=0).reshape(2 * count, slots, depth, 2 * hidden + 256)
    biases = jnp.concatenate([qv_bias.reshape(-1), up_bias])
    biases = jnp.where(jnp.arange(slots)[:, None] == slot, biases[None], jnp.zeros((), BF))
    biases = biases + swap(biases, "c")
    biases = (biases + swap(biases, "y")).astype(F32)
    qv_all = biases[:, : 2 * width].reshape(slots, 2, width).transpose(1, 0, 2).reshape(2, D)
    up_bias_all = biases[:, 2 * width :].reshape(slots, 1, hidden)

    vec_one = jnp.concatenate([first_gain[None], first_shift[None], jnp.zeros((6, D), BF)], 0).astype(F32)
    normed = windows(place, from_above, grid_x, from_below, vec_one)
    if fast:
        pieces = spread_plane(qkv_weight.reshape(depth, 3 * width), count)
        normed, pieces[3], pieces[7] = after(normed, pieces[3], pieces[7])
        pieces += [swap(piece, "c") for piece in pieces]
    else:
        full = lax.all_gather(qkv_weight, AXES, axis=0).reshape(2 * count, slots, depth, 3, width)
        pieces = [full.transpose(0, 2, 3, 1, 4).reshape(D, 3 * D)]
    q, k, v, weight, turned, turned_own = project(place, normed, pieces, qv_all, rows, depth)
    ahead, back = score_tables()
    rel_ahead, rel_back = offset_tables(rel_height, rel_width)
    attended, probs = attend(place, q, k, v, rel_ahead.T, jnp.asarray(ahead, BF), rows)

    vec_two = jnp.concatenate(
        [output_bias[None], second_gain[None], second_shift[None], down_bias[None], jnp.zeros((4, D), BF)], 0
    ).astype(F32)
    (
        output, grad_hidden, grad_out, grad_feed, out_send, out_keep, grad_vec, grad_up_bias,
    ) = feed(
        place, attended.reshape(SIDE, rows, PITCH, D), features, cotangent, rest_all, vec_two, up_bias_all,
        rows, shards,
    )
    grad_windows = grad_out.reshape(-1, D)
    table = jnp.asarray(back.transpose(0, 2, 1), BF)
    grad_feed = lax.psum_scatter(
        grad_feed.reshape(8 * count, depth, 2 * hidden), AXES, scatter_dimension=0
    ).astype(F32)
    grad_up, grad_down = grad_feed[:, :hidden], grad_feed[:, hidden:]
    if fast:
        out_got = swap(out_send, "c")
    *half0, drel0 = attend_back(place, q, k, v, probs, grad_windows, rel_back, table, rows, 0)
    first_send, first_keep, first_bias = project_grad(place, turned, turned_own, *half0, shards)
    if fast:
        first_got = swap(first_send, "c")
    *half1, drel1 = attend_back(place, q, k, v, probs, grad_windows, rel_back, table, rows, 1)
    if fast:
        first, out = [first_keep, first_got], [out_keep, out_got]
        first_away, first_here, out_away, out_here = fold(
            (first, 0, 1, 1), (first, 0, 1, 0), (out, 1, 2, 1), (out, 1, 2, 0)
        )
        place, first_away, out_away = after(place, first_away, out_away)
        first_got, out_got = swap(first_away, "x"), swap(out_away, "x")
    dqs, dks, dvs = zip(half0, half1)
    to_above, total, to_below = project_back(place, dqs, dks, dvs, weight, rows)
    place, to_above, to_below = after(place, to_above, to_below)
    from_below = lax.ppermute(to_above, pair, down_pairs)
    from_above = lax.ppermute(to_below, pair, up_pairs)
    last_send, last_keep, last_bias = project_grad(place, turned, turned_own, *half1, shards)
    if fast:
        last_got = swap(last_send, "c")
    grad_features, sums_one = finish(
        total, from_above, from_below, grid_x, grad_hidden.reshape(rows, GRID, D), vec_one
    )
    if fast:
        sums_one, last_got = after(sums_one, last_got)
        last = [last_keep, last_got]
        away, here = fold((last, 0, 1, 1), (last, 0, 1, 0))
        got = swap(away, "x")
        crossing, out_away, out_here = fold(
            ([first_here, first_got], 0, None, None), ([out_here, out_got], 1, 0, 1), ([out_here, out_got], 1, 0, 0)
        )
        crossing, out_away, sums_one = after(crossing, out_away, sums_one)
        crossing, out_got = swap(crossing, "y"), swap(out_away, "y")
        last, out = fold(([here, got, crossing], 0, None, None), ([out_here, out_got], 0, None, None))
        grad_qkv, grad_wo = along_z(last), along_z(out)
    else:
        pairs = [
            (out_send, out_keep),
            [
                jnp.where(y == 0, jnp.stack([last, first]), jnp.stack([first, last]))
                for first, last in ((first_send, last_send), (first_keep, last_keep))
            ],
        ]
        grad_wo, grad_qkv = [
            lax.psum_scatter(
                jnp.stack([keep, send], 3).transpose(1, 2, 0, 3, 4, 5).reshape(8 * count, depth, -1),
                AXES, scatter_dimension=0,
            ).astype(F32)
            for send, keep in pairs
        ]
    drel = (drel0 + drel1).T.reshape(4, 64, 128)
    drel = drel[1, :, :HD] + drel[2, :, HD:]
    grad_qv = jnp.where(y == 0, jnp.concatenate([last_bias, first_bias], 1), jnp.concatenate([first_bias, last_bias], 1))
    small = jnp.concatenate(
        [grad_vec[:4], grad_up_bias.reshape(slots, hidden), sums_one[:2], grad_qv], 0
    )
    small = sum_all(jnp.concatenate([small.reshape(-1), drel.reshape(-1)]).reshape(-1, 512), count, fast).reshape(-1)
    vec = small[: 12 * D].reshape(12, D)
    drel = small[12 * D :].reshape(64, HD)
    qv = lax.dynamic_index_in_dim(vec[10:12].reshape(2, slots, width), slot, 1, keepdims=False)
    bias = lax.dynamic_index_in_dim(vec[4:8], slot, 0, keepdims=False)
    return (
        output,
        grad_features.reshape(tokens, D),
        vec[8],
        vec[9],
        grad_qkv.reshape(depth, 3, width),
        qv,
        drel[0:OFFS],
        drel[32 : 32 + OFFS],
        grad_wo,
        vec[2],
        vec[0],
        vec[1],
        grad_up,
        bias,
        grad_down,
        vec[3],
    )


def solution(mesh):
    token = P(AXES, None)
    square = P(("z", "x"), ("y", "c"))
    cube = P(("z", "x"), None, ("y", "c"))
    lane = P(("y", "c"))
    count = mesh.shape["dp"] // 2
    assert mesh.shape["tensor"] == 4
    return jax.shard_map(
        partial(body, count=count),
        mesh=jax.sharding.Mesh(mesh.devices.reshape(count, 2, 2, 2), AXES),
        in_specs=(
            token, P(), P(), cube, P(None, ("y", "c")), P(), P(), square, P(), P(), P(), square,
            lane, square, P(), token,
        ),
        out_specs=(
            token, token, P(), P(), cube, P(None, ("y", "c")), P(), P(), square, P(), P(), P(), square,
            lane, square, P(),
        ),
        check_vma=False,
    )
```

```python
from functools import partial
import math

import jax
import jax.numpy as jnp
from jax import lax
from jax.experimental import pallas as pl
from jax.experimental.pallas import tpu as pltpu
from jax.sharding import PartitionSpec as P
import numpy as np

D = 768
HD = 64
GRID = 64
WIN = 14
SIDE = 5
PITCH = 16
KEYS = WIN * PITCH
EXT = 2 * WIN
PAIRS = D // (2 * HD)
OFFS = 2 * WIN - 1
EPSILON = 1e-06
FAR = -1e30
BF = jnp.bfloat16
F32 = jnp.float32
HIGH = lax.Precision.HIGHEST


def mm(left, right):
    return jnp.dot(left, right, preferred_element_type=F32)


def mm_t(left, right):
    return lax.dot_general(left, right, (((1,), (1,)), ((), ())), preferred_element_type=F32)


def t_mm(left, right):
    return lax.dot_general(left, right, (((0,), (0,)), ((), ())), preferred_element_type=F32)


def norm_parts(value):
    centered = value - jnp.mean(value, -1, keepdims=True)
    inverse = lax.rsqrt(jnp.mean(centered * centered, -1, keepdims=True) + EPSILON)
    return centered * inverse, inverse


def norm_back(upstream, hat, inverse, gain):
    scaled = upstream * gain
    return inverse * (
        scaled
        - jnp.mean(scaled, -1, keepdims=True)
        - hat * jnp.mean(scaled * hat, -1, keepdims=True)
    )


def score_tables():
    ahead = np.zeros((2, KEYS, 128), np.float32)
    back = np.zeros((2, KEYS, 128), np.float32)
    for head in range(2):
        base = 64 - 64 * head
        for c in range(WIN):
            for e in range(PITCH):
                k = c * PITCH + e
                if e >= WIN:
                    ahead[head, k, base] = FAR
                    continue
                ahead[head, k, base + 15 + c] = 1
                ahead[head, k, base + 1 + c] = 1
                ahead[head, k, base + 46 + e] = 1
                ahead[head, k, base + 32 + e] = 1
                back[head, k, base + WIN - 1 - c] = 1
                back[head, k, base + 32 + WIN - 1 - e] = 1
    return ahead, back


def offset_tables(rel_height, rel_width):
    def place(first, second, at_rows, at_cols):
        slab = jnp.zeros((64, HD), BF)
        slab = slab.at[at_rows : at_rows + OFFS].set(first)
        slab = slab.at[at_cols : at_cols + OFFS].set(second)
        low = jnp.concatenate([slab, jnp.zeros_like(slab)], 1)
        high = jnp.concatenate([jnp.zeros_like(slab), slab], 1)
        return jnp.concatenate([jnp.zeros_like(low), low, high, jnp.zeros_like(high)], 0)

    through = jnp.eye(HD, dtype=BF) * BF(HD ** (-0.5))
    nothing = jnp.zeros_like(through)
    through = jnp.concatenate(
        [jnp.concatenate([through, nothing], 1), jnp.zeros((128, 128), BF), jnp.concatenate([nothing, through], 1)], 0
    )
    return (
        place(rel_height[::-1], rel_width[::-1], 2, 33) + through,
        place(rel_height, rel_width, 0, 32),
    )


def whole(shape):
    return pl.BlockSpec(shape, lambda *_: (0,) * len(shape), pipeline_mode=pl.Buffered(1))


def windows_body(place_ref, above_ref, x_ref, below_ref, vec_ref, nw_ref, nat_ref, *, rows):
    band = pl.program_id(0)
    slot = place_ref[0]
    above, below = above_ref.shape[0], below_ref.shape[0]

    @pl.when(band == 0)
    def _():
        def normed(piece):
            hat, _ = norm_parts(piece.astype(F32))
            return hat * vec_ref[0:1] + vec_ref[1:2]

        def clear(i, carry):
            nat_ref[i, GRID : GRID + PITCH, :] = jnp.zeros((PITCH, D), F32)
            return carry

        def own(i, carry):
            nat_ref[2 * slot + i, 0:GRID, :] = normed(x_ref[i])
            return carry

        def before(i, carry):
            nat_ref[i, 0:GRID, :] = normed(above_ref[above - 2 * slot + i])
            return carry

        def after(i, carry):
            at = 2 * slot + rows + i
            inside = WIN * slot + at < GRID
            nat_ref[at, 0:GRID, :] = jnp.where(inside, normed(below_ref[i]), 0.0)
            return carry

        lax.fori_loop(0, EXT, clear, 0, unroll=4)
        lax.fori_loop(0, rows, own, 0, unroll=2)
        lax.fori_loop(0, 2 * slot, before, 0)
        lax.fori_loop(0, EXT - rows - 2 * slot, after, 0)

    keep = lax.broadcasted_iota(jnp.int32, (PITCH, D), 0) < WIN
    for b in range(SIDE):
        @pl.when(band == b)
        def _(b=b):
            def one(i, carry):
                piece = nat_ref[i, WIN * b : WIN * b + PITCH, :]
                start = pl.multiple_of(i * PITCH, PITCH)
                nw_ref[pl.ds(start, PITCH), :] = jnp.where(keep, piece, 0.0).astype(BF)
                return carry

            lax.fori_loop(0, EXT, one, 0, unroll=4)


def windows(place, above, x, below, vectors):
    rows = x.shape[0]
    return pl.pallas_call(
        partial(windows_body, rows=rows),
        grid_spec=pltpu.PrefetchScalarGridSpec(
            num_scalar_prefetch=1,
            grid=(SIDE,),
            in_specs=[whole(above.shape), whole(x.shape), whole(below.shape), whole((8, D))],
            out_specs=pl.BlockSpec((EXT * PITCH, D), lambda b, s: (b, 0)),
            scratch_shapes=[pltpu.VMEM((EXT, GRID + PITCH, D), F32)],
        ),
        out_shape=jax.ShapeDtypeStruct((SIDE * EXT * PITCH, D), BF),
        compiler_params=pltpu.CompilerParams(vmem_limit_bytes=63 << 20),
        cost_estimate=guess(8),
        name="windows",
    )(place, above, x, below, vectors)


def project_body(place_ref, nw_ref, *refs, rows, depth):
    *pieces, bias_ref, q_ref, k_ref, v_ref, w_ref, turned_ref, turned_own_ref, stage_ref = refs
    slot, z, x, y, c = (place_ref[i] for i in range(5))
    width = D // 4

    @pl.when(pl.program_id(0) == 0)
    def _():
        if len(pieces) == 1:
            w_ref[...] = pieces[0][...]
            return
        half = depth // 2
        for index, ref in enumerate(pieces):
            sibling, part, dx, dy = index // 8, index // 4 % 2, index // 2 % 2, index % 2
            count = ref.shape[0]
            from_slot = (y ^ dy) * 2 + (c ^ sibling)
            for dz in range(count):
                group = lax.rem(z - dz + count, count) * 2 + (x ^ dx)
                at = pl.multiple_of(group * depth + part * half, half)
                stage_ref[from_slot, pl.ds(at, half), :] = ref[dz]

        def join(i, carry):
            at = pl.ds(pl.multiple_of(i * 64, 64), 64)
            for kind in range(3):
                w_ref[at, kind * D : (kind + 1) * D] = jnp.concatenate(
                    [stage_ref[t, at, kind * width : (kind + 1) * width] for t in range(4)], 1
                )
            return carry

        lax.fori_loop(0, D // 64, join, 0)

    normed = nw_ref[...]
    own = nw_ref[pl.ds(pl.multiple_of(slot * 2 * PITCH, 2 * PITCH), rows * PITCH), :]
    q_ref[...] = (mm(own, w_ref[:, 0:D]) + bias_ref[0:1]).astype(BF)
    k_ref[...] = mm(normed, w_ref[:, D : 2 * D]).astype(BF)
    v_ref[...] = (mm(normed, w_ref[:, 2 * D :]) + bias_ref[1:2]).astype(BF)
    turned_ref[...] = normed.T
    turned_own_ref[...] = own.T


def guess(us):
    return pl.CostEstimate(flops=int(us * 1.1e9), bytes_accessed=int(us * 3e6), transcendentals=0)


def project(place, normed, pieces, bias, rows, depth):
    of_k = pl.BlockSpec((EXT * PITCH, D), lambda b, s: (b, 0))
    of_q = pl.BlockSpec((rows * PITCH, D), lambda b, s: (b, 0))
    keys = jax.ShapeDtypeStruct((SIDE * EXT * PITCH, D), BF)
    return pl.pallas_call(
        partial(project_body, rows=rows, depth=depth),
        grid_spec=pltpu.PrefetchScalarGridSpec(
            num_scalar_prefetch=1,
            grid=(SIDE,),
            in_specs=[of_k] + [whole(p.shape) for p in pieces] + [whole((2, D))],
            out_specs=[
                of_q, of_k, of_k, whole((D, 3 * D)),
                pl.BlockSpec((None, D, EXT * PITCH), lambda b, s: (b, 0, 0)),
                pl.BlockSpec((None, D, rows * PITCH), lambda b, s: (b, 0, 0)),
            ],
            scratch_shapes=[pltpu.VMEM((4, D, 3 * D // 4), BF)],
        ),
        out_shape=[
            jax.ShapeDtypeStruct((SIDE * rows * PITCH, D), BF), keys, keys,
            jax.ShapeDtypeStruct((D, 3 * D), BF),
            jax.ShapeDtypeStruct((SIDE, D, EXT * PITCH), BF),
            jax.ShapeDtypeStruct((SIDE, D, rows * PITCH), BF),
        ],
        compiler_params=pltpu.CompilerParams(vmem_limit_bytes=63 << 20),
        cost_estimate=guess(18),
        name="project",
    )(place, normed, *pieces, bias)


def store_shards(place_ref, refs, value, first=0):
    z, x = place_ref[1], place_ref[2]
    count, _, depth = refs.shape[:3]
    if depth % 32:
        refs[...] = value.reshape(refs.shape)
        return
    for zd in range(value.shape[0] // (2 * depth)):
        for xd in range(2):
            start = (zd * 2 + xd) * depth
            refs[lax.rem(first + zd - z + count, count), x ^ xd] = value[start : start + depth]


def project_grad_body(place_ref, turned_ref, own_ref, dq_ref, dk_ref, dv_ref, send_ref, keep_ref, bias_ref, *, parts):
    step = pl.program_id(0)
    c = place_ref[4]
    width = D // 4

    @pl.when(step == 0)
    def _():
        bias_ref[0:1] = jnp.sum(dq_ref[...].astype(F32), 0, keepdims=True)
        bias_ref[1:2] = jnp.sum(dv_ref[...].astype(F32), 0, keepdims=True)

    def over_bands(left, right):
        lines = left.shape[2]
        return sum(mm(left[b], right(slice(b * lines, (b + 1) * lines))) for b in range(SIDE)).astype(BF)

    both = over_bands(turned_ref, lambda at: jnp.concatenate([dk_ref[at], dv_ref[at]], 1))
    grads = [over_bands(own_ref, lambda at: dq_ref[at]), both[:, : D // 2], both[:, D // 2 :]]
    first = step * (keep_ref.shape[0] // parts)
    for core in range(2):
        value = jnp.concatenate([g[:, core * width : (core + 1) * width] for g in grads], 1)
        for sibling, ref in ((1, send_ref), (0, keep_ref)):
            @pl.when(c ^ core == sibling)
            def _(ref=ref, value=value):
                store_shards(place_ref, ref, value, first)


def project_grad(place, turned, own, dq, dk, dv, shards):
    count, depth = shards[1], shards[3]
    parts = 2 if depth % 32 == 0 else 1
    out = jax.ShapeDtypeStruct((count, 2, depth, 3 * D // 4), BF)
    return pl.pallas_call(
        partial(project_grad_body, parts=parts),
        grid_spec=pltpu.PrefetchScalarGridSpec(
            num_scalar_prefetch=1,
            grid=(parts,),
            in_specs=[
                pl.BlockSpec((SIDE, D // parts, turned.shape[2]), lambda i, s: (0, i, 0)),
                pl.BlockSpec((SIDE, D // parts, own.shape[2]), lambda i, s: (0, i, 0)),
                whole(dq.shape), whole(dk.shape), whole(dv.shape),
            ],
            out_specs=[whole(out.shape), whole(out.shape), whole((2, D // 2))],
        ),
        out_shape=[out, out, jax.ShapeDtypeStruct((2, D // 2), F32)],
        compiler_params=pltpu.CompilerParams(vmem_limit_bytes=63 << 20),
        cost_estimate=guess(6),
        name="project_grad",
    )(place, turned, own, dq, dk, dv)


def project_back_body(place_ref, *refs, rows):
    dqs, dks, dvs = refs[0:2], refs[2:4], refs[4:6]
    w_ref, above_ref, own_ref, below_ref, all_ref, dq_ref, dk_ref, dv_ref = refs[6:]
    slot, y = place_ref[0], place_ref[5]
    above, below = above_ref.shape[0], below_ref.shape[0]
    for halves, ref in ((dqs, dq_ref), (dks, dk_ref), (dvs, dv_ref)):
        for i in range(2):
            at = pl.multiple_of((y ^ (1 - i)) * (D // 2), D // 2)
            ref[:, pl.ds(at, D // 2)] = halves[i][...]
    grad = mm_t(dk_ref[...], w_ref[:, D : 2 * D]) + mm_t(dv_ref[...], w_ref[:, 2 * D :])
    direct = mm_t(dq_ref[...], w_ref[:, 0:D]).reshape(rows, PITCH, D)
    all_ref[0:above] = jnp.zeros((above, PITCH, D), F32)
    all_ref[above + rows :] = jnp.zeros((below, PITCH, D), F32)
    all_ref[pl.ds(above - 2 * slot, EXT)] = grad.reshape(EXT, PITCH, D)
    above_ref[...] = all_ref[0:above].astype(BF)
    own_ref[...] = all_ref[above : above + rows] + direct
    below_ref[...] = all_ref[above + rows :].astype(BF)


def project_back(place, dqs, dks, dvs, weight, rows):
    above, below = 8, WIN - 2
    of_k = pl.BlockSpec((EXT * PITCH, D // 2), lambda b, s: (b, 0))
    of_q = pl.BlockSpec((rows * PITCH, D // 2), lambda b, s: (b, 0))
    part = lambda n: pl.BlockSpec((None, n, PITCH, D), lambda b, s: (b, 0, 0, 0))
    return pl.pallas_call(
        partial(project_back_body, rows=rows),
        grid_spec=pltpu.PrefetchScalarGridSpec(
            num_scalar_prefetch=1,
            grid=(SIDE,),
            in_specs=[of_q, of_q, of_k, of_k, of_k, of_k, whole((D, 3 * D))],
            out_specs=[part(above), part(rows), part(below)],
            scratch_shapes=[
                pltpu.VMEM((above + rows + below, PITCH, D), F32),
                pltpu.VMEM((rows * PITCH, D), BF),
                pltpu.VMEM((EXT * PITCH, D), BF),
                pltpu.VMEM((EXT * PITCH, D), BF),
            ],
        ),
        out_shape=[
            jax.ShapeDtypeStruct((SIDE, above, PITCH, D), BF),
            jax.ShapeDtypeStruct((SIDE, rows, PITCH, D), F32),
            jax.ShapeDtypeStruct((SIDE, below, PITCH, D), BF),
        ],
        compiler_params=pltpu.CompilerParams(vmem_limit_bytes=63 << 20),
        cost_estimate=guess(10),
        name="project_back",
    )(place, *dqs, *dks, *dvs, weight)


def head_lanes(shape, head):
    lane = lax.broadcasted_iota(jnp.int32, shape, 1)
    return lane < HD if head == 0 else lane >= HD


def early_window(slot, rows):
    return (WIN - 2 * slot) * PITCH - rows * PITCH // 2


def lanes_of(pair):
    return slice(128 * pair, 128 * pair + 128)


def attend_body(place_ref, q_ref, k_ref, v_ref, rel_ref, tab_ref, o_ref, p_ref, *, rows):
    slot = place_ref[0]
    half = rows * PITCH // 2
    lane = lax.broadcasted_iota(jnp.int32, (PITCH, 128), 1)
    first = lax.broadcasted_iota(jnp.int32, (1, half), 1) < early_window(slot, rows)
    turns = [lax.rem(2 * slot + r, WIN) for r in range(rows)]
    heads = [(pair, head) for pair in range(q_ref.shape[1] // 128) for head in range(2)]
    raws = [mm(q_ref[:, lanes_of(pair)], rel_ref[...]) for pair in range(len(heads) // 2)]

    def extended(pair, head):
        base = 64 - 64 * head
        one = jnp.where(lane == base, 1.0, 0.0)
        on_row = (lane >= base + 15) & (lane < base + 29)
        on_col = (lane >= base + 46) & (lane < base + 60)
        mine = head_lanes((PITCH, 128), head)
        parts = []
        for r in range(rows):
            here = raws[pair][r * PITCH : (r + 1) * PITCH, lanes_of(head)]
            along_row = pltpu.roll(here, turns[r], 1)
            along_col = pltpu.roll(here, 0, 1, stride=1, stride_axis=0)
            kept = jnp.where(mine, here, one)
            both = jnp.where(on_row, along_row, jnp.where(on_col, along_col, kept))
            high = both.astype(BF).astype(F32)
            parts.append((high + pltpu.roll(both - high, 114, 1)).astype(BF))
        return jnp.concatenate(parts, 0)

    def scored(pair, head, left):
        mine = head_lanes((KEYS, 128), head)
        keys_a = jnp.where(mine, k_ref[0:KEYS, lanes_of(pair)], tab_ref[head])
        keys_b = jnp.where(mine, k_ref[KEYS:, lanes_of(pair)], tab_ref[head])
        scores = mm_t(keys_a, left)
        return scores[:, :half], jnp.where(first, scores[:, half:], mm_t(keys_b, left[half:]))

    def softmax(pair, head, pieces):
        for i, piece in enumerate(pieces):
            grown = jnp.exp(piece - jnp.max(piece, 0, keepdims=True))
            probs = (grown * (1.0 / jnp.sum(grown, 0, keepdims=True))).astype(BF)
            p_ref[pair, head, :, i * half : (i + 1) * half] = probs

    def weighed(pair, head):
        rows_of = slice(HD * head, HD * head + HD)
        out = mm(v_ref[0:KEYS, lanes_of(pair)].T[rows_of], p_ref[pair, head])
        late = mm(v_ref[KEYS:, lanes_of(pair)].T[rows_of], p_ref[pair, head, :, half:])
        return jnp.concatenate([out[:, :half], jnp.where(first, out[:, half:], late)], 1)

    lefts = [extended(*h) for h in heads]
    scores = [scored(*h, left) for h, left in zip(heads, lefts)]
    for h, pieces in zip(heads, scores):
        softmax(*h, pieces)
    outs = [weighed(*h) for h in heads]
    for pair in range(len(heads) // 2):
        o_ref[:, lanes_of(pair)] = jnp.concatenate(outs[2 * pair : 2 * pair + 2], 0).T.astype(BF)


def attend(slot, q, k, v, rel, table, rows):
    queries = rows * PITCH
    many = PAIRS // 2
    of_k = pl.BlockSpec((EXT * PITCH, 128 * many), lambda b, p, s: (b, p))
    of_q = pl.BlockSpec((queries, 128 * many), lambda b, p, s: (b, p))
    return pl.pallas_call(
        partial(attend_body, rows=rows),
        grid_spec=pltpu.PrefetchScalarGridSpec(
            num_scalar_prefetch=1,
            grid=(SIDE, PAIRS // many),
            in_specs=[of_q, of_k, of_k, whole((128, 256)), whole((2, KEYS, 128))],
            out_specs=[
                of_q,
                pl.BlockSpec((many, 2, KEYS, queries), lambda b, p, s: (b * (PAIRS // many) + p, 0, 0, 0)),
            ],
        ),
        out_shape=[
            jax.ShapeDtypeStruct((SIDE * queries, D), BF),
            jax.ShapeDtypeStruct((SIDE * PAIRS, 2, KEYS, queries), BF),
        ],
        compiler_params=pltpu.CompilerParams(vmem_limit_bytes=63 << 20),
        cost_estimate=guess(24),
        name="attend",
    )(slot, q, k, v, rel, table)


def attend_back_body(
    place_ref, q_ref, k_ref, v_ref, p_ref, do_ref, rel_ref, tab_ref, dq_ref, dk_ref, dv_ref, drel_ref, *, rows,
):
    slot = place_ref[0]
    count = rows * PITCH
    half = count // 2
    early = early_window(slot, rows)

    @pl.when(pl.program_id(0) == 0)
    def _():
        drel_ref[...] = jnp.zeros_like(drel_ref)

    lane = lax.broadcasted_iota(jnp.int32, (PITCH, 128), 1)
    first = lax.broadcasted_iota(jnp.int32, (1, half), 1) < early
    turns = [lax.rem(2 * slot + r, WIN) for r in range(rows)]
    heads = [(pair, head) for pair in range(q_ref.shape[1] // 128) for head in range(2)]

    def split(value, head):
        spot = lax.broadcasted_iota(jnp.int32, (half, 128), 0)
        mine = head_lanes((half, 128), head)
        value = value.astype(F32)
        top = jnp.where(mine, value[:half], 0.0)
        mid = jnp.where(mine & (spot < early), value[half:], 0.0)
        low = jnp.where(mine & (spot >= early), value[half:], 0.0)
        return jnp.concatenate([top, mid], 0).astype(BF), low.astype(BF), (mid + low).astype(BF)

    def upstream(pair, head):
        return split(do_ref[:, lanes_of(pair)], head)

    def probs_grad(pair, head, out_a, late):
        whole_out = jnp.concatenate([out_a[:half], late], 0)
        grad = mm_t(v_ref[0:KEYS, lanes_of(pair)], whole_out)
        more = mm_t(v_ref[KEYS:, lanes_of(pair)], late)
        return grad[:, :half], jnp.where(first, grad[:, half:], more)

    def scores_grad(pair, head, pieces):
        grads = []
        for i, piece in enumerate(pieces):
            exact = p_ref[pair, head, :, i * half : (i + 1) * half].astype(F32)
            inner = jnp.sum(exact * piece, 0, keepdims=True)
            grads.append((exact * (piece - inner)).astype(BF))
        return jnp.concatenate(grads, 1)

    def left_grad(pair, head, grad, turned):
        spot = lax.broadcasted_iota(jnp.int32, (128, KEYS), 0)
        mine = spot < HD if head == 0 else spot >= HD
        left = mm(jnp.where(mine, turned[0], tab_ref[head]), grad)
        late = mm(jnp.where(mine, turned[1], tab_ref[head]), grad[:, half:])
        return jnp.concatenate([left[:, :half], jnp.where(first, left[:, half:], late)], 1).T

    def raw_grad(head, left):
        base = 64 - 64 * head
        on_row = (lane >= base) & (lane < base + WIN)
        on_col = (lane >= base + 32) & (lane < base + 32 + WIN)
        parts = []
        for r in range(rows):
            here = left[r * PITCH : (r + 1) * PITCH]
            along_row = pltpu.roll(jnp.where(on_row, here, 0.0), turns[r], 1)
            along_col = pltpu.roll(jnp.where(on_col, here, 0.0), 0, 1, stride=1, stride_axis=0)
            parts.append((along_row + along_col).astype(BF))
        return jnp.concatenate(parts, 0)

    outs = [upstream(*h) for h in heads]
    pieces = [probs_grad(*h, out[0], out[2]) for h, out in zip(heads, outs)]
    grads = [scores_grad(*h, piece) for h, piece in zip(heads, pieces)]
    lefts = []
    for pair in range(len(heads) // 2):
        turned = [k_ref[w * KEYS : (w + 1) * KEYS, lanes_of(pair)].T for w in range(2)]
        lefts += [left_grad(pair, head, grads[2 * pair + head], turned) for head in range(2)]
    for pair in range(len(heads) // 2):
        scaled = q_ref[:, lanes_of(pair)].astype(F32) * HD ** (-0.5)
        owns = [split(scaled, head) for head in range(2)]
        for w in range(2):
            at = (slice(w * KEYS, (w + 1) * KEYS), lanes_of(pair))
            part = slice(0, count) if w == 0 else slice(half, count)
            dv_ref[at] = sum(mm(p_ref[pair, h, :, part], outs[2 * pair + h][w]) for h in range(2)).astype(BF)
            dk_ref[at] = sum(mm(grads[2 * pair + h][:, part], owns[h][w]) for h in range(2)).astype(BF)
    for pair in range(len(heads) // 2):
        mine = lefts[2 * pair : 2 * pair + 2]
        raw = jnp.concatenate([raw_grad(head, mine[head]) for head in range(2)], 1)
        direct = jnp.where(head_lanes((count, 128), 0), *mine) * HD ** (-0.5)
        dq_ref[:, lanes_of(pair)] = (direct + mm(raw, rel_ref[...])).astype(BF)
        drel_ref[...] += t_mm(q_ref[:, lanes_of(pair)], raw)


def attend_back(slot, q, k, v, probs, grad_out, rel, table, rows, group):
    queries = rows * PITCH
    many = PAIRS // 2
    half = lambda s: s[5] ^ (1 - group)
    of_q = pl.BlockSpec((queries, 128 * many), lambda b, s: (b, half(s)))
    of_k = pl.BlockSpec((EXT * PITCH, 128 * many), lambda b, s: (b, half(s)))
    to_q = pl.BlockSpec((queries, 128 * many), lambda b, s: (b, 0))
    to_k = pl.BlockSpec((EXT * PITCH, 128 * many), lambda b, s: (b, 0))
    return pl.pallas_call(
        partial(attend_back_body, rows=rows),
        grid_spec=pltpu.PrefetchScalarGridSpec(
            num_scalar_prefetch=1,
            grid=(SIDE,),
            in_specs=[
                of_q, of_k, of_k,
                pl.BlockSpec((many, 2, KEYS, queries), lambda b, s: (b * 2 + half(s), 0, 0, 0)),
                of_q, whole((256, 128)), whole((2, 128, KEYS)),
            ],
            out_specs=[to_q, to_k, to_k, whole((128, 256))],
        ),
        out_shape=[
            jax.ShapeDtypeStruct((q.shape[0], D // 2), BF),
            jax.ShapeDtypeStruct((k.shape[0], D // 2), BF),
            jax.ShapeDtypeStruct((k.shape[0], D // 2), BF),
            jax.ShapeDtypeStruct((128, 256), F32),
        ],
        compiler_params=pltpu.CompilerParams(vmem_limit_bytes=63 << 20),
        cost_estimate=guess(16),
        name="attend_back",
    )(slot, q, k, v, probs, grad_out, rel, table)


def feed_body(place_ref, o_ref, x_ref, g_ref, vec_ref, bias_ref, rest_ref, *refs, rows):
    (
        out_ref, dh_ref, do_ref, grad_ref, gas_ref, gak_ref, gvec_ref, gbias_ref,
        nat_ref, onat_ref, n2_ref, n2t_ref, gt_ref, h_ref, y_ref, dn_ref, a_ref, du_ref, w_ref,
        up_ref, down_ref, slots_ref, sems,
    ) = refs
    step = pl.program_id(0)
    steps = rows * GRID // 256
    lines = 256 // GRID
    width = D // 4
    y, c = place_ref[3], place_ref[4]
    buffer = lax.rem(step, 2)

    def fetch(chunk, where):
        for i, ref in enumerate((up_ref, down_ref)):
            source = rest_ref.at[:, chunk, :, pl.ds(i * D, D)]
            pltpu.make_async_copy(source, ref.at[where], sems.at[where, i]).start()

    @pl.when(step == 0)
    def _():
        pltpu.make_async_copy(rest_ref.at[:, :, :, pl.ds(2 * D, 256)], slots_ref, sems.at[2, 0]).start()
        fetch(step, buffer)

    @pl.when(step < pl.num_programs(0) - 1)
    def _():
        fetch(step + 1, 1 - buffer)

    @pl.when(step == 0)
    def _():
        pltpu.make_async_copy(slots_ref, slots_ref, sems.at[2, 0]).wait()

        for t in range(4):
            w_ref[:, t * width : (t + 1) * width] = slots_ref[:, t, :, 0:width].reshape(D, width)

        def one(i, carry):
            at = pl.ds(pl.multiple_of(i * 256, 256), 256)
            for b in range(SIDE):
                piece = o_ref[b, pl.ds(i * lines, lines)]
                nat_ref[:, WIN * b : WIN * b + PITCH, :] = piece.astype(F32)
            natural = nat_ref[:, 0:GRID, :].reshape(256, D).astype(BF)
            onat_ref[at, :] = natural
            hidden = x_ref[at, :].astype(F32) + mm_t(natural, w_ref[...]) + vec_ref[0:1]
            h_ref[at, :] = hidden
            hat, _ = norm_parts(hidden)
            normed = (hat * vec_ref[1:2] + vec_ref[2:3]).astype(BF)
            n2_ref[at, :] = normed
            n2t_ref[:, at] = normed.T
            gt_ref[:, at] = g_ref[at, :].T
            y_ref[at, :] = jnp.zeros((256, D), F32)
            dn_ref[at, :] = jnp.zeros((256, D), F32)
            return carry

        lax.fori_loop(0, steps, one, 0, unroll=2)

    pltpu.make_async_copy(up_ref.at[buffer], up_ref.at[buffer], sems.at[buffer, 0]).wait()
    pltpu.make_async_copy(down_ref.at[buffer], down_ref.at[buffer], sems.at[buffer, 1]).wait()
    up, down = up_ref[buffer].reshape(D, D), down_ref[buffer].reshape(D, D)
    total = jnp.zeros((1, D), F32)

    def inward(i):
        at = slice(i * 512, i * 512 + 512)
        upper = mm(n2_ref[at, :], up) + bias_ref[...].reshape(1, D)
        cdf = 0.5 * (1.0 + lax.erf(upper * (1.0 / math.sqrt(2.0))))
        a_ref[at, :] = (upper * cdf).astype(BF)
        slope = cdf + upper * jnp.exp(-0.5 * upper * upper) * (1.0 / math.sqrt(2.0 * math.pi))
        delta = (mm(g_ref[at, :], down) * slope).astype(BF)
        du_ref[at, :] = delta
        return jnp.sum(delta.astype(F32), 0, keepdims=True)

    def outward(i):
        at = slice(i * 512, i * 512 + 512)
        y_ref[at, :] += mm_t(a_ref[at, :], down)
        dn_ref[at, :] += mm_t(du_ref[at, :], up)

    for i in range(rows * GRID // 512):
        total = total + inward(i)
        if i:
            outward(i - 1)
    outward(rows * GRID // 512 - 1)
    gbias_ref[...] = total.reshape(gbias_ref.shape)
    grad_up = mm(n2t_ref[...], du_ref[...]).astype(BF)
    grad_down = mm(gt_ref[...], a_ref[...]).astype(BF)
    shape = (grad_ref.shape[0], grad_ref.shape[1], D)
    grad_ref[:, :, 0:D] = grad_up.reshape(shape)
    grad_ref[:, :, D:] = grad_down.reshape(shape)

    @pl.when(step == pl.num_programs(0) - 1)
    def _():
        nat_ref[...] = jnp.zeros_like(nat_ref)
        gvec_ref[...] = jnp.zeros_like(gvec_ref)

        def three(i, carry):
            at = pl.ds(pl.multiple_of(i * 256, 256), 256)
            hidden = h_ref[at, :]
            grad = g_ref[at, :].astype(F32)
            hat, inverse = norm_parts(hidden)
            grad_normed = dn_ref[at, :]
            out_ref[at, :] = (hidden + y_ref[at, :] + vec_ref[3:4]).astype(BF)
            grad_hidden = grad + norm_back(grad_normed, hat, inverse, vec_ref[1:2])
            dh_ref[at, :] = grad_hidden
            branch = grad_hidden.astype(BF)
            n2_ref[at, :] = branch
            gvec_ref[0:1] += jnp.sum(grad_normed * hat, 0, keepdims=True)
            gvec_ref[1:2] += jnp.sum(grad_normed, 0, keepdims=True)
            gvec_ref[2:3] += jnp.sum(branch.astype(F32), 0, keepdims=True)
            gvec_ref[3:4] += jnp.sum(grad, 0, keepdims=True)
            grad_out = mm(branch, w_ref[...])
            nat_ref[:, 0:GRID, :] = grad_out.reshape(lines, GRID, D)
            keep = lax.broadcasted_iota(jnp.int32, (lines, PITCH, D), 1) < WIN
            for b in range(SIDE):
                piece = nat_ref[:, WIN * b : WIN * b + PITCH, :]
                do_ref[b, pl.ds(i * lines, lines)] = jnp.where(keep, piece, 0.0).astype(BF)
            return carry

        lax.fori_loop(0, steps, three, 0, unroll=2)
        grad_wo = t_mm(n2_ref[...], onat_ref[...]).astype(BF)
        for sibling, ref in ((1, gas_ref), (0, gak_ref)):
            for t in range(4):
                @pl.when(c ^ (t % 2) == sibling)
                def _(t=t, ref=ref):
                    store_shards(
                        place_ref, ref.at[y ^ (t // 2)], grad_wo[:, t * width : (t + 1) * width]
                    )


def feed(place, o, x, g, rest, vectors, up_bias, rows, shards):
    tokens = rows * GRID
    blocks, chunks, depth = rest.shape[:3]
    line = pl.BlockSpec((None, 1, D), lambda s, p: (s, 0, 0))
    grid = (SIDE, rows, PITCH, D)
    out = jax.ShapeDtypeStruct((*shards, D // chunks), BF)
    shapes = [
        jax.ShapeDtypeStruct((tokens, D), BF),
        jax.ShapeDtypeStruct((tokens, D), F32),
        jax.ShapeDtypeStruct(grid, BF),
        jax.ShapeDtypeStruct((blocks, chunks, depth, 2 * D), BF),
        out, out,
        jax.ShapeDtypeStruct((8, D), F32),
        jax.ShapeDtypeStruct((chunks, 1, D), F32),
    ]
    specs = [whole(s.shape) for s in shapes]
    specs[3] = pl.BlockSpec((blocks, None, depth, 2 * D), lambda s, p: (0, s, 0, 0))
    specs[7] = line
    return pl.pallas_call(
        partial(feed_body, rows=rows),
        grid_spec=pltpu.PrefetchScalarGridSpec(
            num_scalar_prefetch=1,
            grid=(chunks,),
            in_specs=[
                whole(grid), whole((tokens, D)), whole((tokens, D)), whole((8, D)), line,
                pl.BlockSpec(memory_space=pl.ANY),
            ],
            out_specs=specs,
            scratch_shapes=[
                pltpu.VMEM((256 // GRID, GRID + PITCH, D), F32),
                pltpu.VMEM((tokens, D), BF),
                pltpu.VMEM((tokens, D), BF),
                pltpu.VMEM((D, tokens), BF),
                pltpu.VMEM((D, tokens), BF),
                pltpu.VMEM((tokens, D), F32),
                pltpu.VMEM((tokens, D), F32),
                pltpu.VMEM((tokens, D), F32),
                pltpu.VMEM((tokens, D), BF),
                pltpu.VMEM((tokens, D), BF),
                pltpu.VMEM((D, D), BF),
                pltpu.VMEM((2, blocks, depth, D), BF),
                pltpu.VMEM((2, blocks, depth, D), BF),
                pltpu.VMEM((blocks, chunks, depth, 256), BF),
                pltpu.SemaphoreType.DMA((3, 2)),
            ],
        ),
        out_shape=shapes,
        compiler_params=pltpu.CompilerParams(vmem_limit_bytes=63 << 20),
        cost_estimate=guess(50),
        name="feed",
    )(place, o, x, g, vectors, up_bias, rest)


def finish_body(own_ref, head_ref, tail_ref, x_ref, dh_ref, vec_ref, out_ref, sum_ref, nat_ref, *, heads, tails):
    step = pl.program_id(0)

    @pl.when(step == 0)
    def _():
        sum_ref[...] = jnp.zeros_like(sum_ref)

    has_head = step < heads
    has_tail = step >= pl.num_programs(0) - tails
    for i in range(own_ref.shape[1]):
        for b in range(SIDE):
            grad = own_ref[b, i] + jnp.where(has_head, head_ref[b, i].astype(F32), 0.0)
            grad = grad + jnp.where(has_tail, tail_ref[b, i].astype(F32), 0.0)
            nat_ref[i, WIN * b : WIN * b + PITCH, :] = grad
        grad = nat_ref[i, 0:GRID, :]
        hat, inverse = norm_parts(x_ref[i].astype(F32))
        out_ref[i] = (dh_ref[i] + norm_back(grad, hat, inverse, vec_ref[0:1])).astype(BF)
        sum_ref[0:1] += jnp.sum(grad * hat, 0, keepdims=True)
        sum_ref[1:2] += jnp.sum(grad, 0, keepdims=True)


def finish(own, head, tail, x, dh, vectors):
    rows, lines = own.shape[1], 4
    heads, tails = head.shape[1] // lines, tail.shape[1] // lines
    steps = rows // lines
    banded = lambda index: pl.BlockSpec((SIDE, lines, PITCH, D), lambda i: (0, index(i), 0, 0))
    plain = pl.BlockSpec((lines, GRID, D), lambda i: (i, 0, 0))
    return pl.pallas_call(
        partial(finish_body, heads=heads, tails=tails),
        grid=(steps,),
        in_specs=[
            banded(lambda i: i),
            banded(lambda i: jnp.minimum(i, heads - 1)),
            banded(lambda i: jnp.maximum(i - (steps - tails), 0)),
            plain, plain, whole(vectors.shape),
        ],
        out_specs=[plain, whole((8, D))],
        out_shape=[jax.ShapeDtypeStruct((rows, GRID, D), BF), jax.ShapeDtypeStruct((8, D), F32)],
        scratch_shapes=[pltpu.VMEM((lines, GRID + PITCH, D), F32)],
        compiler_params=pltpu.CompilerParams(vmem_limit_bytes=63 << 20),
        cost_estimate=guess(6),
        name="finish",
    )(own, head, tail, x, dh, vectors)


def fold_body(*refs, plan):
    terms = sum(count for count, *_ in plan)
    ins, outs = refs[:terms], refs[terms:]
    for (count, axis, index), out in zip(plan, outs):
        here, ins = ins[:count], ins[count:]
        lead = out.shape[:-2]
        for at in np.ndindex(*lead):
            spot = at if axis is None else at[:axis] + (index,) + at[axis:]
            total = here[0][spot].astype(F32)
            for ref in here[1:]:
                total = total + ref[spot].astype(F32)
            out[at] = total.astype(out.dtype)


def fold(*results):
    count = None
    args, in_specs, out_specs, shapes, plan = [], [], [], [], []
    for terms, z_axis, axis, index in results:
        shape = terms[0].shape
        count = shape[z_axis]
        block = tuple(None if i == z_axis else n for i, n in enumerate(shape))
        spec = pl.BlockSpec(block, lambda i, z_axis=z_axis, n=len(shape): tuple(i if k == z_axis else 0 for k in range(n)))
        args += terms
        in_specs += [spec] * len(terms)
        left = [n for i, n in enumerate(shape) if i != axis]
        z_left = z_axis if axis is None or axis > z_axis else z_axis - 1
        block = tuple(None if i == z_left else n for i, n in enumerate(left))
        out_specs.append(
            pl.BlockSpec(block, lambda i, z_left=z_left, n=len(left): tuple(i if k == z_left else 0 for k in range(n)))
        )
        shapes.append(jax.ShapeDtypeStruct(tuple(left), BF))
        inner = None if axis is None else (axis if axis < z_axis else axis - 1)
        plan.append((len(terms), inner, index))
    size = sum(2 * int(np.prod(a.shape)) for a in args)
    return pl.pallas_call(
        partial(fold_body, plan=plan),
        grid=(count,),
        in_specs=in_specs,
        out_specs=out_specs,
        out_shape=shapes,
        compiler_params=pltpu.CompilerParams(vmem_limit_bytes=63 << 20),
        cost_estimate=guess(1 + size / 2e6),
        name="fold",
    )(*args)


AXES = ("z", "x", "y", "c")
SWAP = [(0, 1), (1, 0)]


def swap(value, axis):
    return lax.ppermute(value, axis, SWAP)


def shift(value, count, by):
    return lax.ppermute(value, "z", [(i, (i + by) % count) for i in range(count)])


def spread_plane(shard, count):
    half = shard.shape[0] // 2
    lines = [shard] + [shift(shard, count, k) for k in range(1, count)]
    first = jnp.stack([line[:half] for line in lines])
    second = jnp.stack([line[half:] for line in lines])
    first_x, second_y = swap(first, "x"), swap(second, "y")
    return [
        first, swap(first, "y"), first_x, swap(first_x, "y"),
        second, second_y, swap(second, "x"), swap(second_y, "x"),
    ]


def after(value, *others):
    return lax.optimization_barrier((value, *others))


def along_z(pieces):
    count = pieces.shape[0]
    total = pieces[0].astype(F32)
    for k in range(1, count):
        total = total + shift(pieces[k], count, k).astype(F32)
    return total


def sum_all(value, count, fast):
    for axis in ("c", "y", "x"):
        value = value + swap(value, axis)
    if not fast:
        return lax.psum(value, "z")
    step = 1
    while step < count:
        value = value + lax.ppermute(value, "z", [(i, i ^ step) for i in range(count)])
        step *= 2
    return value


def body(
    features, first_gain, first_shift, qkv_weight, qv_bias, rel_height, rel_width, output_weight,
    output_bias, second_gain, second_shift, up_weight, up_bias, down_weight, down_bias, cotangent,
    *, count,
):
    depth, _, width = qkv_weight.shape
    hidden = up_weight.shape[1]
    tokens = features.shape[0]
    rows = tokens // GRID
    slots = 4
    fast = count <= 4 and depth % 32 == 0
    z, x, y, c = (lax.axis_index(a).astype(jnp.int32) for a in AXES)
    slot = 2 * y + c
    nought = jnp.zeros((), jnp.int32)
    place = jnp.stack([slot, z, x, y, c, y] if fast else [slot] + [nought] * 4 + [y])
    shards = (2, count, 2, depth)
    above, below = 2 * (slots - 1), WIN - 2

    grid_x = features.reshape(rows, GRID, D)
    pair = ("y", "c")
    up_pairs = [(s, s + 1) for s in range(slots - 1)]
    down_pairs = [(s + 1, s) for s in range(slots - 1)]
    from_above = lax.ppermute(grid_x[rows - above :], pair, up_pairs)
    from_below = lax.ppermute(grid_x[:below], pair, down_pairs)

    qkv_rows, up_weight = after(qkv_weight.reshape(depth, 3 * width), up_weight)
    rest = jnp.concatenate([up_weight, down_weight, output_weight, jnp.zeros((depth, 256 - width), BF)], 1)
    rest_all = lax.all_gather(rest, AXES, axis=0).reshape(2 * count, slots, depth, 2 * hidden + 256)
    biases = jnp.concatenate([qv_bias.reshape(-1), up_bias])
    biases = jnp.where(jnp.arange(slots)[:, None] == slot, biases[None], jnp.zeros((), BF))
    biases = biases + swap(biases, "c")
    biases = (biases + swap(biases, "y")).astype(F32)
    qv_all = biases[:, : 2 * width].reshape(slots, 2, width).transpose(1, 0, 2).reshape(2, D)
    up_bias_all = biases[:, 2 * width :].reshape(slots, 1, hidden)

    vec_one = jnp.concatenate([first_gain[None], first_shift[None], jnp.zeros((6, D), BF)], 0).astype(F32)
    normed = windows(place, from_above, grid_x, from_below, vec_one)
    if fast:
        pieces = spread_plane(qkv_rows, count)
        normed, pieces[3], pieces[7] = after(normed, pieces[3], pieces[7])
        pieces += [swap(piece, "c") for piece in pieces]
    else:
        full = lax.all_gather(qkv_weight, AXES, axis=0).reshape(2 * count, slots, depth, 3, width)
        pieces = [full.transpose(0, 2, 3, 1, 4).reshape(D, 3 * D)]
    q, k, v, weight, turned, turned_own = project(place, normed, pieces, qv_all, rows, depth)
    ahead, back = score_tables()
    rel_ahead, rel_back = offset_tables(rel_height, rel_width)
    attended, probs = attend(place, q, k, v, rel_ahead.T, jnp.asarray(ahead, BF), rows)

    vec_two = jnp.concatenate(
        [output_bias[None], second_gain[None], second_shift[None], down_bias[None], jnp.zeros((4, D), BF)], 0
    ).astype(F32)
    (
        output, grad_hidden, grad_out, grad_feed, out_send, out_keep, grad_vec, grad_up_bias,
    ) = feed(
        place, attended.reshape(SIDE, rows, PITCH, D), features, cotangent, rest_all, vec_two, up_bias_all,
        rows, shards,
    )
    grad_windows = grad_out.reshape(-1, D)
    table = jnp.asarray(back.transpose(0, 2, 1), BF)
    grad_feed = lax.psum_scatter(
        grad_feed.reshape(8 * count, depth, 2 * hidden), AXES, scatter_dimension=0
    ).astype(F32)
    grad_up, grad_down = grad_feed[:, :hidden], grad_feed[:, hidden:]
    if fast:
        out_got = swap(out_send, "c")
    *half0, drel0 = attend_back(place, q, k, v, probs, grad_windows, rel_back, table, rows, 0)
    first_send, first_keep, first_bias = project_grad(place, turned, turned_own, *half0, shards)
    if fast:
        first_got = swap(first_send, "c")
    *half1, drel1 = attend_back(place, q, k, v, probs, grad_windows, rel_back, table, rows, 1)
    if fast:
        first, out = [first_keep, first_got], [out_keep, out_got]
        first_away, first_here, out_away, out_here = fold(
            (first, 0, 1, 1), (first, 0, 1, 0), (out, 1, 2, 1), (out, 1, 2, 0)
        )
        place, first_away, out_away = after(place, first_away, out_away)
        first_got, out_got = swap(first_away, "x"), swap(out_away, "x")
    dqs, dks, dvs = zip(half0, half1)
    to_above, total, to_below = project_back(place, dqs, dks, dvs, weight, rows)
    place, to_above, to_below = after(place, to_above, to_below)
    from_below = lax.ppermute(to_above, pair, down_pairs)
    from_above = lax.ppermute(to_below, pair, up_pairs)
    last_send, last_keep, last_bias = project_grad(place, turned, turned_own, *half1, shards)
    if fast:
        last_got = swap(last_send, "c")
    grad_features, sums_one = finish(
        total, from_above, from_below, grid_x, grad_hidden.reshape(rows, GRID, D), vec_one
    )
    if fast:
        sums_one, last_got = after(sums_one, last_got)
        last = [last_keep, last_got]
        away, here = fold((last, 0, 1, 1), (last, 0, 1, 0))
        got = swap(away, "x")
        crossing, out_away, out_here = fold(
            ([first_here, first_got], 0, None, None), ([out_here, out_got], 1, 0, 1), ([out_here, out_got], 1, 0, 0)
        )
        crossing, out_away, sums_one = after(crossing, out_away, sums_one)
        crossing, out_got = swap(crossing, "y"), swap(out_away, "y")
        last, out = fold(([here, got, crossing], 0, None, None), ([out_here, out_got], 0, None, None))
        grad_qkv, grad_wo = along_z(last), along_z(out)
    else:
        pairs = [
            (out_send, out_keep),
            [
                jnp.where(y == 0, jnp.stack([last, first]), jnp.stack([first, last]))
                for first, last in ((first_send, last_send), (first_keep, last_keep))
            ],
        ]
        grad_wo, grad_qkv = [
            lax.psum_scatter(
                jnp.stack([keep, send], 3).transpose(1, 2, 0, 3, 4, 5).reshape(8 * count, depth, -1),
                AXES, scatter_dimension=0,
            ).astype(F32)
            for send, keep in pairs
        ]
    drel = (drel0 + drel1).T.reshape(4, 64, 128)
    drel = drel[1, :, :HD] + drel[2, :, HD:]
    grad_qv = jnp.where(y == 0, jnp.concatenate([last_bias, first_bias], 1), jnp.concatenate([first_bias, last_bias], 1))
    small = jnp.concatenate(
        [grad_vec[:4], grad_up_bias.reshape(slots, hidden), sums_one[:2], grad_qv], 0
    )
    small = sum_all(jnp.concatenate([small.reshape(-1), drel.reshape(-1)]).reshape(-1, 512), count, fast).reshape(-1)
    vec = small[: 12 * D].reshape(12, D)
    drel = small[12 * D :].reshape(64, HD)
    qv = lax.dynamic_index_in_dim(vec[10:12].reshape(2, slots, width), slot, 1, keepdims=False)
    bias = lax.dynamic_index_in_dim(vec[4:8], slot, 0, keepdims=False)
    return (
        output,
        grad_features.reshape(tokens, D),
        vec[8],
        vec[9],
        grad_qkv.reshape(depth, 3, width),
        qv,
        drel[0:OFFS],
        drel[32 : 32 + OFFS],
        grad_wo,
        vec[2],
        vec[0],
        vec[1],
        grad_up,
        bias,
        grad_down,
        vec[3],
    )


def solution(mesh):
    token = P(AXES, None)
    square = P(("z", "x"), ("y", "c"))
    cube = P(("z", "x"), None, ("y", "c"))
    lane = P(("y", "c"))
    count = mesh.shape["dp"] // 2
    assert mesh.shape["tensor"] == 4
    return jax.shard_map(
        partial(body, count=count),
        mesh=jax.sharding.Mesh(mesh.devices.reshape(count, 2, 2, 2), AXES),
        in_specs=(
            token, P(), P(), cube, P(None, ("y", "c")), P(), P(), square, P(), P(), P(), square,
            lane, square, P(), token,
        ),
        out_specs=(
            token, token, P(), P(), cube, P(None, ("y", "c")), P(), P(), square, P(), P(), P(), square,
            lane, square, P(),
        ),
        check_vma=False,
    )
```
